128 devices in a mesh: mem: 2 (over x_lo), row: 32 (over z, y, x_hi), col: 2 (over core).
Axes of the slice: x: 4 (x_hi: 2, x_lo: 2; x = x_hi * 2 + x_lo), y: 4, z: 4, core: 2. Of those that a mesh axis runs over, the one named last changes fastest.
Arguments:
- control: float32 [16, 2, 1024, 2048], P('mem', None, 'row', 'col'), may hold values from -6 to 6
- members: bfloat16 [16, 2, 1024, 2048], P('mem', None, 'row', 'col'), may hold values from -6 to 6
- obs_corner: int32 [128, 8192], P(('mem', 'row', 'col')), may hold values from 0 to 31742, as said below
- obs_count: int32 [128, 64], P(('mem', 'row', 'col')), may hold values from 0 to 128, as said below
- offset_y: float32 [128, 8192], P(('mem', 'row', 'col')), may hold values from 0 to 1
- offset_x: float32 [128, 8192], P(('mem', 'row', 'col')), may hold values from 0 to 1
- offset_z: float32 [128, 8192], P(('mem', 'row', 'col')), may hold values from 0 to 1
- innovation: float32 [128, 8192], P(('mem', 'row', 'col')), may hold values from -6 to 6
- precision: float32 [128, 8192], P(('mem', 'row', 'col')), may hold values from 1 to 16
Outputs:
- gradient: float32 [16, 2, 1024, 2048], P('mem', None, 'row', 'col')
- departures: float32 [128, 8192], P(('mem', 'row', 'col'))
The draws below stay inside these ranges and needn't reach their ends.
Inputs may be any that keep to these rules, and one draw needn't show every extreme that they name: obs_corner is r * 1024 + c with r at most 30 and c at most 1022, so that every stencil lies inside its owner tile. `obs_count`: in every draw some owner tile receives 128 observations from every source.
All inputs are finite; a program needn't handle non-finite values.
Results may differ from the reference program's by a relative error of at most 0.0003.
Values sent between devices are 32-bit elements; how exact they have to be, the bound alone decides.
A program may use at most 64 MiB of HBM per device.

```python
import math
import jax
import jax.numpy as jnp
from jax import lax

LEV = 2
TY = 32
TX = 1024
CAP = 128
NPASS = 2
MEMBERS = 16
NY = 1024
NX = 2048
TILES = 64
SRCS = 128
SLOTS = 8192
N_COL = 2


def draw_obs_corner(key, part):
    first = jax.random.fold_in(key, 11)
    second = jax.random.fold_in(key, 12)
    row_in = jax.random.randint(first, (SRCS, SLOTS), 0, TY - 1)
    col_in = jax.random.randint(second, (SRCS, SLOTS), 0, TX - 1)
    corner = (row_in * TX + col_in).astype(jnp.int32)
    return corner.at[0, 0].set((TY - 2) * TX + TX - 2).astype(jnp.int32)


def draw_obs_count(key, part):
    first = jax.random.fold_in(key, 21)
    second = jax.random.fold_in(key, 22)
    third = jax.random.fold_in(key, 23)
    density = jax.random.randint(first, (TILES,), 2, 6)
    raw_count = jax.random.randint(second, (SRCS, TILES), 0, CAP // 4 + 1)
    counts = jnp.minimum(raw_count * density[None, :], CAP)
    full_tile = jax.random.randint(third, (), 0, TILES)
    counts = jnp.where(jnp.arange(TILES)[None, :] == full_tile, CAP, counts)
    return counts.astype(jnp.int32)


def levels(key, dims, cuts, least, high):
    factor_of = 1.0
    for dim, shards_of in cuts:
        heights = jax.random.uniform(jax.random.fold_in(jax.random.fold_in(key, 6), dim), (shards_of,), jnp.float32, least / len(cuts), high / len(cuts))
        factor_of = factor_of * jnp.repeat(jnp.exp(heights), dims[dim] // shards_of).reshape((-1,) + (1,) * (len(dims) - 1 - dim))
    return factor_of


def normal_values(key, extent, width, limit, cuts=(), dtype=jnp.bfloat16):
    result = width * jax.random.normal(key, extent, jnp.float32)
    if cuts:
        result = result * levels(key, extent, cuts, -0.22, 0.18)
    return jnp.clip(result, -limit, limit).astype(dtype)


def setup_inputs(seed: int = 0) -> dict:
    arg_keys = jax.random.split(jax.random.key(seed), 10)
    return {
        "control": normal_values(arg_keys[0], (MEMBERS, LEV, NY, NX), 1.0, 6.0, ((0, 2), (2, 32), (3, 2)), jnp.float32),
        "members": normal_values(arg_keys[1], (MEMBERS, LEV, NY, NX), 1.0, 6.0, ((0, 2), (2, 32), (3, 2))),
        "obs_corner": draw_obs_corner(jax.random.fold_in(arg_keys[9], 71), 0),
        "obs_count": draw_obs_count(jax.random.fold_in(arg_keys[9], 71), 0),
        "offset_y": jnp.clip(1.0 * jax.random.uniform(arg_keys[4], (SRCS, SLOTS), jnp.float32) ** levels(arg_keys[4], (SRCS, SLOTS), ((0, 128),), -0.2, 0.2), 0.0, 1.0),
        "offset_x": jnp.clip(1.0 * jax.random.uniform(arg_keys[5], (SRCS, SLOTS), jnp.float32) ** levels(arg_keys[5], (SRCS, SLOTS), ((0, 128),), -0.2, 0.2), 0.0, 1.0),
        "offset_z": jnp.clip(1.0 * jax.random.uniform(arg_keys[6], (SRCS, SLOTS), jnp.float32) ** levels(arg_keys[6], (SRCS, SLOTS), ((0, 128),), -0.2, 0.2), 0.0, 1.0),
        "innovation": normal_values(arg_keys[7], (SRCS, SLOTS), 1.0, 6.0, ((0, 128),), jnp.float32),
        "precision": jnp.clip(jnp.exp(math.log(16.0) - 2.7725887 * jax.random.uniform(arg_keys[8], (SRCS, SLOTS), jnp.float32) ** levels(arg_keys[8], (SRCS, SLOTS), ((0, 128),), -0.2, 0.2)), 1.0, 16.0),
    }


def rates(length):
    decay = jnp.exp(-1.0 / length)
    weight = ((1.0 - decay * decay) ** 3 / (1.0 + decay * decay)) ** 0.25
    return decay, weight


def sweep(field, decay, weight, reverse):
    moved = jnp.moveaxis(field, 3, 0)

    def advance(state, column):
        state = decay[None, :, None] * state + weight[None, :, None] * column
        return state, state

    start = jnp.zeros(moved.shape[1:], jnp.float32)
    ignored, swept = lax.scan(advance, start, moved, reverse=reverse)
    return jnp.moveaxis(swept, 0, 3)


def stencil(corner, frac_y, frac_x, frac_z, rows, cols):
    index_list = []
    weight_list = []
    for level in range(2):
        for down in range(2):
            for right in range(2):
                index_list.append(corner + level * rows * cols + down * cols + right)
                weight_z = frac_z if level == 1 else 1.0 - frac_z
                weight_y = frac_y if down == 1 else 1.0 - frac_y
                weight_x = frac_x if right == 1 else 1.0 - frac_x
                weight_list.append(weight_z * weight_y * weight_x)
    return jnp.stack(index_list), jnp.stack(weight_list)


def reference(control, members, obs_corner, obs_count, offset_y, offset_x, offset_z, innovation, precision):
    decay_x, weight_x = rates(jnp.array([TX / 16.0, TX / 64.0], jnp.float32))
    decay_y, weight_y = rates(jnp.array([NY / 2.0, TY / 2.0], jnp.float32))
    scale = float(MEMBERS) ** -0.5
    field = control
    for turn in range(NPASS):
        field = sweep(field, decay_x, weight_x, False)
    field = jnp.swapaxes(field, 2, 3)
    for turn in range(NPASS):
        field = sweep(field, decay_y, weight_y, False)
    field = jnp.swapaxes(field, 2, 3)
    increment = jnp.sum(members.astype(jnp.float32) * field, axis=0) * scale
    slots = jnp.arange(SLOTS)
    tile_of = slots // CAP
    anchor = ((tile_of // N_COL) * TY * NX + (tile_of % N_COL) * TX)[None, :]
    row_in = obs_corner // TX
    col_in = obs_corner - row_in * TX
    global_corner = (anchor + row_in * NX + col_in).astype(jnp.int32)
    indices, weights = stencil(global_corner, offset_y, offset_x, offset_z, NY, NX)
    images = jnp.sum(weights * jnp.take(increment.reshape(-1), indices), axis=0)
    live = (slots % CAP)[None, :] < jnp.take(obs_count, tile_of, axis=1)
    departures = jnp.where(live, precision * (images - innovation), 0.0)
    forcing = jnp.zeros((LEV * NY * NX,), jnp.float32).at[indices.reshape(-1)].add((weights * departures[None]).reshape(-1))
    forcing = forcing.reshape(LEV, NY, NX)
    work = members.astype(jnp.float32) * forcing[None] * scale
    work = jnp.swapaxes(work, 2, 3)
    for turn in range(NPASS):
        work = sweep(work, decay_y, weight_y, True)
    work = jnp.swapaxes(work, 2, 3)
    for turn in range(NPASS):
        work = sweep(work, decay_x, weight_x, True)
    return control + work, departures
```

```python
import functools

import jax
import jax.numpy as jnp
import numpy as np
from jax import lax
from jax.experimental import pallas as pl
from jax.experimental.pallas import tpu as pltpu
from jax.sharding import PartitionSpec as P

CAP = 128
LANES = 128
BLOCK = 256
F32 = jnp.float32
BF16 = jnp.bfloat16
MESH = pl.DeviceIdType.MESH
VMEM = pl.BlockSpec(memory_space=pltpu.VMEM)


def filter_rates(length):
    one = np.float32(1.0)
    decay = np.exp(-one / np.float32(length), dtype=np.float32)
    square = np.float32(decay * decay)
    weight = np.power(np.power(one - square, np.float32(3.0)) / (one + square), np.float32(0.25))
    return float(decay), float(weight)


def halves(array):
    high = array.astype(jnp.bfloat16)
    low = (array - high.astype(np.float32)).astype(jnp.bfloat16)
    return high, low


class Geometry:
    def __init__(self, members, levels, ty, tx, rows):
        self.m, self.levels, self.ty, self.tx, self.rows = members, levels, ty, tx, rows
        self.lines = members * ty
        self.blocks = tx // LANES
        self.wide = tx // BLOCK
        self.chunks = levels * self.blocks
        self.half = rows // 2
        self.per = self.chunks // self.half
        self.x_rates = [filter_rates(tx / 16.0), filter_rates(tx / 64.0)]
        self.y_rates = [filter_rates(rows * ty / 2.0), filter_rates(ty / 2.0)]

    def row_matrix(self, reverse):
        m, ty = self.m, self.ty
        result = []
        for a, b in self.y_rates:
            place = np.arange(ty)
            gap = place[:, None] - place[None, :]
            local = np.where(gap >= 0, b * b * (gap + 1.0) * a ** np.maximum(gap, 0), 0.0)
            edge = np.stack([b * a ** (ty - 1.0 - place), b * b * (ty - place) * a ** (ty - 1.0 - place)])
            if reverse:
                local, edge = local.T, edge[:, ::-1]
            main = np.kron(np.eye(m), local)
            ends = np.concatenate([np.kron(np.eye(m), edge[s : s + 1]) for s in range(2)])
            result.append(np.concatenate([main, ends]))
        return halves(np.stack(result).astype(np.float32))

    def col_tables(self, reverse):
        tx = self.tx
        result = []
        for a, b in self.x_rates:
            place = np.arange(tx)
            ends = [b * a ** (tx - 1.0 - place), b * b * (tx - place) * a ** (tx - 1.0 - place)]
            enter = [b * (place + 1.0) * a ** (place + 1.0), a ** (place + 1.0)]
            table = np.stack(ends + enter)
            result.append(table[:, ::-1] if reverse else table)
        return np.stack(result).astype(np.float32)

    def row_tables(self, reverse):
        result = []
        for a, b in self.y_rates:
            place = np.arange(self.ty)
            table = np.stack([b * (place + 1.0) * a ** (place + 1.0), a ** (place + 1.0)])
            table = table[:, ::-1] if reverse else table
            result.append(np.broadcast_to(table[:, :, None], (2, self.ty, LANES)))
        return np.stack(result).astype(np.float32)

    def row_step(self):
        return [(a**self.ty, b * self.ty * a**self.ty) for a, b in self.y_rates]


def split(value):
    high = value.astype(BF16)
    return high, (value - high.astype(F32)).astype(BF16)


def dot(a, b):
    return jnp.dot(a, b, preferred_element_type=F32)


def dot3(ah, al, bh, bl):
    return dot(ah, bh) + dot(al, bh) + dot(ah, bl)


def make_strips(geo, reverse, high, low):
    step = LANES
    tx = geo.tx

    for level, (a, b) in enumerate(geo.x_rates):
        rate = float(np.log(a))
        scale = b * b

        def part(index, carry):
            first = pl.multiple_of(index * step, step)
            down = lax.broadcasted_iota(jnp.int32, (step, BLOCK), 0) + first
            across = lax.broadcasted_iota(jnp.int32, (step, BLOCK), 1)
            gap = down - across if reverse else across + (tx - BLOCK) - down
            gap_f = gap.astype(F32)
            value = scale * (gap_f + 1.0) * jnp.exp(jnp.maximum(gap_f, 0.0) * rate)
            value = jnp.where(gap >= 0, value, 0.0)
            h, w = split(value)
            high[level, pl.ds(first, step), :] = h
            low[level, pl.ds(first, step), :] = w
            return carry

        lax.fori_loop(0, tx // step, part, 0)


def along_x(geo, reverse, h_ref, l_ref, level, wide, high, low):
    tx = geo.tx
    if reverse:
        cut, strip = pl.ds(BLOCK * wide, tx - BLOCK * wide), pl.ds(0, tx - BLOCK * wide)
    else:
        size = BLOCK * (wide + 1)
        cut, strip = pl.ds(0, size), pl.ds(tx - size, size)
    return dot3(
        h_ref[level, :, cut], l_ref[level, :, cut], high[level, strip, :], low[level, strip, :]
    )


def filter_kernel(geo, reverse, *refs):
    if reverse:
        control, members, forcing, payload, ph, plo, cols, rowt, out, a2a_out = refs[:10]
        refs = refs[10:]
    else:
        control, members, payload, ph, plo, cols, rowt, out, a2a_out = refs[:9]
        refs = refs[9:]
    (dh, dl, bst, bh, bl, ebsend, ebrecv, esend, erecv, bsend, brecv, csend, crecv, field, sh, sl, arrived,
     obs_s, obs_r, eb_s, eb_r, e_s, e_r, b_s, b_r, c_s, c_r) = refs
    m, levels, ty, tx, rows = geo.m, geo.levels, geo.ty, geo.tx, geo.rows
    lines, blocks, half = geo.lines, geo.blocks, geo.half
    my_row, my_col = lax.axis_index("row"), lax.axis_index("col")
    tiles = rows * 2
    me = my_row * 2 + my_col
    other_col = 1 - my_col

    barrier = pltpu.get_barrier_semaphore()

    def greet(k, carry):
        t = lax.rem(me + k, tiles)
        pl.semaphore_signal(barrier, inc=1, device_id={"row": t // 2, "col": lax.rem(t, 2)}, device_id_type=MESH)
        return carry

    lax.fori_loop(1, tiles, greet, 0)

    make_strips(geo, reverse, sh, sl)
    for level in range(levels):
        for i in range(m):
            cut = slice(i * ty, (i + 1) * ty)
            if reverse:
                value = members[i, level].astype(F32) * forcing[level]
            else:
                value = control[i, level]
            h, w = split(value)
            dh[level, cut, :] = h
            dl[level, cut, :] = w
    for level in range(levels):
        edge = dot3(ph[level, lines:, :], plo[level, lines:, :], dh[level], dl[level])
        bst[level] = edge
        h, w = split(edge)
        bh[level] = h
        bl[level] = w
        for s in range(2):
            total = jnp.sum(edge * cols[level, s : s + 1, :], axis=1, keepdims=True)
            ebsend[level, s] = jnp.broadcast_to(total, (2 * m, LANES))

    pl.semaphore_wait(barrier, tiles - 1)

    def obs_copy(k, to, slot):
        return pltpu.make_async_remote_copy(
            src_ref=payload.at[to], dst_ref=arrived.at[slot], send_sem=obs_s.at[k - 1], recv_sem=obs_r.at[k - 1],
            device_id={"row": to // 2, "col": lax.rem(to, 2)}, device_id_type=MESH,
        )

    eb_copy = pltpu.make_async_remote_copy(
        src_ref=ebsend, dst_ref=ebrecv, send_sem=eb_s, recv_sem=eb_r, device_id={"col": other_col}, device_id_type=MESH
    )
    eb_copy.start()
    eb_copy.wait()

    enters = jnp.where(my_col == (0 if reverse else 1), 1.0, 0.0).astype(F32)
    for level in range(levels):
        e1 = ebrecv[level, 0] * enters
        e2 = ebrecv[level, 1] * enters
        for wide in range(geo.wide):
            value = along_x(geo, reverse, bh, bl, level, wide, sh, sl)
            for k in range(BLOCK // LANES):
                at = wide * BLOCK + k * LANES
                piece = value[:, k * LANES : (k + 1) * LANES]
                piece = piece + e1 * cols[level, 2:3, at : at + LANES] + e2 * cols[level, 3:4, at : at + LANES]
                chunk = level * blocks + at // LANES
                bsend[chunk, 0] = piece[:m]
                bsend[chunk, 1] = piece[m:]

    scans = lax.rem(my_row, 2) == my_col
    spot = my_row // 2

    def row_of(i):
        return 2 * i + my_col

    def b_copy(p, i, source):
        return pltpu.make_async_remote_copy(
            src_ref=bsend.at[p * half + i], dst_ref=brecv.at[p, source], send_sem=b_s.at[p * half + i],
            recv_sem=b_r.at[p * rows + source], device_id={"row": row_of(i)}, device_id_type=MESH,
        )

    def c_copy(p, i, target):
        return pltpu.make_async_remote_copy(
            src_ref=csend.at[p, target], dst_ref=crecv.at[p * half + i], send_sem=c_s.at[p * rows + target],
            recv_sem=c_r.at[p * half + i], device_id={"row": target}, device_id_type=MESH,
        )

    def each(count, action):
        def one(i, carry):
            action(i)
            return carry

        lax.fori_loop(0, count, one, 0)

    for p in range(geo.per):
        def begin(i, p=p):
            pl.when(row_of(i) != my_row)(lambda: b_copy(p, i, my_row).start())

        each(half, begin)

        @pl.when(scans)
        def _(p=p):
            brecv[p, my_row] = bsend[p * half + spot]

    def obs_begin(k, carry):
        obs_copy(k, lax.rem(me + k, tiles), me).start()
        return carry

    lax.fori_loop(1, tiles, obs_begin, 0)
    arrived[me] = payload[me]

    for level in range(levels):
        sums = [jnp.zeros((lines, LANES), F32) for s in range(2)]
        for wide in range(geo.wide):
            cut = slice(wide * BLOCK, (wide + 1) * BLOCK)
            value = dot3(ph[level, :lines, :], plo[level, :lines, :], dh[level, :, cut], dl[level, :, cut])
            field[level, :, cut] = value
            for k in range(BLOCK // LANES):
                at = wide * BLOCK + k * LANES
                piece = value[:, k * LANES : (k + 1) * LANES]
                sums = [sums[s] + piece * cols[level, s : s + 1, at : at + LANES] for s in range(2)]
        for s in range(2):
            total = jnp.sum(sums[s], axis=1, keepdims=True)
            esend[level, s] = jnp.broadcast_to(total, (lines, LANES))
        for i in range(m):
            cut = slice(i * ty, (i + 1) * ty)
            h, w = split(field[level, cut, :])
            dh[level, cut, :] = h
            dl[level, cut, :] = w
    e_copy = pltpu.make_async_remote_copy(
        src_ref=esend, dst_ref=erecv, send_sem=e_s, recv_sem=e_r, device_id={"col": other_col}, device_id_type=MESH
    )
    e_copy.start()
    for level in range(levels):
        for wide in range(geo.wide):
            field[level, :, wide * BLOCK : (wide + 1) * BLOCK] = along_x(geo, reverse, dh, dl, level, wide, sh, sl)
    steps = geo.row_step()

    @pl.when(scans)
    def _():
        for p in range(geo.per):
            def arrive(r, p=p):
                pl.when(r != my_row)(lambda: b_copy(p, spot, r).wait_recv())

            each(rows, arrive)
            first_level = p * half + spot < blocks
            keep = jnp.where(first_level, steps[0][0], steps[1][0]).astype(F32)
            mix = jnp.where(first_level, steps[0][1], steps[1][1]).astype(F32)

            def advance(lap, state, p=p, keep=keep, mix=mix):
                s1, s2 = state
                r = rows - 1 - lap if reverse else lap
                csend[p, r, 0] = s1
                csend[p, r, 1] = s2
                return keep * s1 + brecv[p, r, 0], keep * s2 + mix * s1 + brecv[p, r, 1]

            zero = jnp.zeros((m, LANES), F32)
            lax.fori_loop(0, rows, advance, (zero, zero))

            def give(r, p=p):
                pl.when(r != my_row)(lambda: c_copy(p, spot, r).start())

            each(rows, give)
            crecv[p * half + spot] = csend[p, my_row]

    e_copy.wait()
    for p in range(geo.per):
        def taken(i, p=p):
            @pl.when(row_of(i) != my_row)
            def _():
                b_copy(p, i, my_row).wait_send()
                c_copy(p, i, my_row).wait_recv()

        each(half, taken)

    for level in range(levels):
        def finish(k, carry, level=level):
            at = pl.ds(pl.multiple_of(k * LANES, LANES), LANES)
            q = cols[level, 2:3, at] * enters
            w = cols[level, 3:4, at] * enters
            total = jnp.zeros((ty, LANES), F32)
            for i in range(m):
                cut = slice(i * ty, (i + 1) * ty)
                value = field[level, cut, at] + erecv[level, 0, cut] * q + erecv[level, 1, cut] * w
                chunk = level * blocks + k
                value = value + rowt[level, 0] * crecv[chunk, 0, i : i + 1, :]
                value = value + rowt[level, 1] * crecv[chunk, 1, i : i + 1, :]
                if reverse:
                    out[i, level, :, at] = control[i, level, :, at] + value
                else:
                    total = total + members[i, level, :, at].astype(F32) * value
            if not reverse:
                out[level, :, at] = total * scale_of(geo)
            return carry

        lax.fori_loop(0, blocks, finish, 0)

    def obs_end(k, carry):
        copy = obs_copy(k, lax.rem(me + k, tiles), lax.rem(me - k + tiles, tiles))
        copy.wait_send()
        copy.wait_recv()
        return carry

    lax.fori_loop(1, tiles, obs_end, 0)
    if reverse:
        a2a_out[...] = arrived[:, 0, :]
    else:
        a2a_out[...] = arrived[...]

    @pl.when(scans)
    def _():
        for p in range(geo.per):
            def given(r, p=p):
                pl.when(r != my_row)(lambda: c_copy(p, spot, r).wait_send())

            each(rows, given)


def scale_of(geo):
    return float(geo.m * 2) ** -0.5


def run_filter(geo, reverse, control, members, forcing, payload):
    m, levels, ty, tx, rows = geo.m, geo.levels, geo.ty, geo.tx, geo.rows
    tiles = rows * 2
    ph, plo = geo.row_matrix(reverse)
    operands = [control, members] + ([forcing] if reverse else []) + [payload]
    operands += [jnp.asarray(ph), jnp.asarray(plo), jnp.asarray(geo.col_tables(reverse)), jnp.asarray(geo.row_tables(reverse))]
    if reverse:
        outs = (jax.ShapeDtypeStruct((m, levels, ty, tx), F32), jax.ShapeDtypeStruct((tiles, CAP), F32))
    else:
        outs = (jax.ShapeDtypeStruct((levels, ty, tx), F32), jax.ShapeDtypeStruct((tiles, 8, CAP), F32))
    dma = pltpu.SemaphoreType.DMA
    scratch = [
        pltpu.VMEM((levels, geo.lines, tx), BF16),
        pltpu.VMEM((levels, geo.lines, tx), BF16),
        pltpu.VMEM((levels, 2 * m, tx), F32),
        pltpu.VMEM((levels, 2 * m, tx), BF16),
        pltpu.VMEM((levels, 2 * m, tx), BF16),
        pltpu.VMEM((levels, 2, 2 * m, LANES), F32),
        pltpu.VMEM((levels, 2, 2 * m, LANES), F32),
        pltpu.VMEM((levels, 2, geo.lines, LANES), F32),
        pltpu.VMEM((levels, 2, geo.lines, LANES), F32),
        pltpu.VMEM((geo.chunks, 2, m, LANES), F32),
        pltpu.VMEM((geo.per, rows, 2, m, LANES), F32),
        pltpu.VMEM((geo.per, rows, 2, m, LANES), F32),
        pltpu.VMEM((geo.chunks, 2, m, LANES), F32),
        pltpu.VMEM((levels, geo.lines, tx), F32),
        pltpu.VMEM((levels, tx, BLOCK), BF16),
        pltpu.VMEM((levels, tx, BLOCK), BF16),
        pltpu.VMEM((tiles, 8, CAP), F32),
        dma((tiles - 1,)),
        dma((tiles - 1,)),
        dma,
        dma,
        dma,
        dma,
        dma((geo.chunks,)),
        dma((geo.per * rows,)),
        dma((geo.per * rows,)),
        dma((geo.chunks,)),
    ]
    return pl.pallas_call(
        functools.partial(filter_kernel, geo, reverse),
        out_shape=outs,
        in_specs=[VMEM] * len(operands),
        out_specs=(VMEM, VMEM),
        scratch_shapes=scratch,
        compiler_params=pltpu.CompilerParams(
            collective_id=2 if reverse else 0, has_side_effects=True, vmem_limit_bytes=60 * 1024 * 1024
        ),
        name="filter_back" if reverse else "filter_forward",
    )(*operands)


def stencil_rows(obs, levels, ty):
    y0, fy, fz = obs[0:1], obs[2:3], obs[4:5]
    place = lax.broadcasted_iota(jnp.int32, (ty, CAP), 0).astype(F32)
    weight = jnp.where(place == y0, 1.0 - fy, jnp.where(place == y0 + 1.0, fy, 0.0))
    return jnp.concatenate([weight * (1.0 - fz), weight * fz], axis=0)


def obs_kernel(geo, own, obs, forcing, back, recv, select, parts, spread, total, got, f_s, f_r, t_s, t_r):
    levels, ty, tx = geo.levels, geo.ty, geo.tx
    cells = levels * ty
    sources = obs.shape[0]
    my_mem = lax.axis_index("mem")
    partner = {"mem": 1 - my_mem}
    barrier = pltpu.get_barrier_semaphore()
    pl.semaphore_signal(barrier, inc=1, device_id=partner, device_id_type=MESH)
    pl.semaphore_wait(barrier, 1)
    copy = pltpu.make_async_remote_copy(
        src_ref=own, dst_ref=recv, send_sem=f_s, recv_sem=f_r, device_id=partner, device_id_type=MESH
    )
    copy.start()

    def choose(s, carry):
        x0 = obs[s, 1:2, :]
        at = pl.ds(pl.multiple_of(s * CAP, CAP), CAP)
        for first in range(0, tx, LANES):
            place = (lax.broadcasted_iota(jnp.int32, (LANES, CAP), 0) + first).astype(F32)
            select[first : first + LANES, at] = jnp.where(place == x0, 1.0, 0.0).astype(BF16)
        return carry

    lax.fori_loop(0, sources, choose, 0)
    copy.wait()

    value = (own[...] + recv[...]).reshape(cells, tx)
    moved = pltpu.roll(value, tx - 1, 1)
    h, w = split(value)
    parts[0:cells] = h
    parts[cells : 2 * cells] = w
    h, w = split(moved)
    parts[2 * cells : 3 * cells] = h
    parts[3 * cells :] = w

    pair = BLOCK // CAP

    def interpolate(t, carry):
        at = pl.ds(pl.multiple_of(t * BLOCK, BLOCK), BLOCK)
        values = dot(parts[...], select[:, at])
        for i in range(pair):
            s = t * pair + i
            data = obs[s]
            cut = slice(i * CAP, (i + 1) * CAP)
            fx = data[3:4]
            left = values[0:cells, cut] + values[cells : 2 * cells, cut]
            right = values[2 * cells : 3 * cells, cut] + values[3 * cells :, cut]
            weight = stencil_rows(data, levels, ty)
            mixed = left * (1.0 - fx) + right * fx
            image = jnp.sum(weight * mixed, axis=0, keepdims=True)
            departure = data[6:7] * (image - data[5:6])
            back[s] = jnp.broadcast_to(departure, (8, CAP))
            weight = weight * departure
            here = pl.ds(pl.multiple_of(s * CAP, CAP), CAP)
            h, w = split(weight * (1.0 - fx))
            spread[0:cells, here] = h
            spread[cells : 2 * cells, here] = w
            h, w = split(weight * fx)
            spread[2 * cells : 3 * cells, here] = h
            spread[3 * cells :, here] = w
        return carry

    lax.fori_loop(0, sources // pair, interpolate, 0)

    lane = lax.broadcasted_iota(jnp.int32, (cells, LANES), 1)
    last = jnp.zeros((cells, LANES), F32)
    for first in range(0, tx, BLOCK):
        piece = lax.dot_general(
            select[first : first + BLOCK, :], spread[...], (((1,), (1,)), ((), ())), preferred_element_type=F32
        )
        piece = piece.T
        for k in range(BLOCK // LANES):
            cut = slice(k * LANES, (k + 1) * LANES)
            here = piece[0:cells, cut] + piece[cells : 2 * cells, cut]
            ahead = pltpu.roll(piece[2 * cells : 3 * cells, cut] + piece[3 * cells :, cut], 1, 1)
            here = here + jnp.where(lane == 0, last, ahead)
            last = ahead
            total[:, :, first + k * LANES : first + (k + 1) * LANES] = here.reshape(levels, ty, LANES)
    copy = pltpu.make_async_remote_copy(
        src_ref=total, dst_ref=got, send_sem=t_s, recv_sem=t_r, device_id=partner, device_id_type=MESH
    )
    copy.start()
    copy.wait()
    forcing[...] = (total[...] + got[...]) * scale_of(geo)


def run_obs(geo, own, obs):
    levels, ty, tx = geo.levels, geo.ty, geo.tx
    sources = obs.shape[0]
    slots = sources * CAP
    cells = levels * ty
    dma = pltpu.SemaphoreType.DMA
    return pl.pallas_call(
        functools.partial(obs_kernel, geo),
        out_shape=(jax.ShapeDtypeStruct((levels, ty, tx), F32), jax.ShapeDtypeStruct((sources, 8, CAP), F32)),
        in_specs=[VMEM, VMEM],
        out_specs=(VMEM, VMEM),
        scratch_shapes=[
            pltpu.VMEM((levels, ty, tx), F32),
            pltpu.VMEM((tx, slots), BF16),
            pltpu.VMEM((4 * cells, tx), BF16),
            pltpu.VMEM((4 * cells, slots), BF16),
            pltpu.VMEM((levels, ty, tx), F32),
            pltpu.VMEM((levels, ty, tx), F32),
            dma,
            dma,
            dma,
            dma,
        ],
        compiler_params=pltpu.CompilerParams(
            collective_id=1, has_side_effects=True, vmem_limit_bytes=60 * 1024 * 1024
        ),
        name="observations",
    )(own, obs)


def body(control, members, obs_corner, obs_count, offset_y, offset_x, offset_z, innovation, precision):
    m, levels, ty, tx = control.shape
    rows = lax.axis_size("row")
    tiles = rows * lax.axis_size("col")
    geo = Geometry(m, levels, ty, tx, rows)

    def by_tile(array):
        return array.reshape(tiles, CAP)

    corner = by_tile(obs_corner)
    row_in = corner // tx
    live = jnp.arange(CAP)[None, :] < obs_count.reshape(tiles, 1)
    fields = [
        row_in.astype(F32),
        (corner - row_in * tx).astype(F32),
        by_tile(offset_y),
        by_tile(offset_x),
        by_tile(offset_z),
        by_tile(innovation),
        jnp.where(live, by_tile(precision), 0.0),
        jnp.zeros((tiles, CAP), F32),
    ]
    payload = jnp.stack(fields, axis=1)
    own, obs = run_filter(geo, False, control, members, None, payload)
    forcing, back = run_obs(geo, own, obs)
    gradient, departures = run_filter(geo, True, control, members, forcing, back)
    return gradient, departures.reshape(1, tiles * CAP)


def solution(mesh):
    return jax.shard_map(
        body,
        mesh=mesh,
        in_specs=(
            P("mem", None, "row", "col"),
            P("mem", None, "row", "col"),
            P(("mem", "row", "col"), None),
            P(("mem", "row", "col"), None),
            P(("mem", "row", "col"), None),
            P(("mem", "row", "col"), None),
            P(("mem", "row", "col"), None),
            P(("mem", "row", "col"), None),
            P(("mem", "row", "col"), None),
        ),
        out_specs=(P("mem", None, "row", "col"), P(("mem", "row", "col"), None)),
        check_vma=False,
    )
```

```python
import functools

import jax
import jax.numpy as jnp
import numpy as np
from jax import lax
from jax.experimental import pallas as pl
from jax.experimental.pallas import tpu as pltpu
from jax.sharding import PartitionSpec as P

CAP = 128
LANES = 128
BLOCK = 256
F32 = jnp.float32
BF16 = jnp.bfloat16
MESH = pl.DeviceIdType.MESH
VMEM = pl.BlockSpec(memory_space=pltpu.VMEM)


def filter_rates(length):
    one = np.float32(1.0)
    decay = np.exp(-one / np.float32(length), dtype=np.float32)
    square = np.float32(decay * decay)
    weight = np.power(np.power(one - square, np.float32(3.0)) / (one + square), np.float32(0.25))
    return float(decay), float(weight)


def halves(array):
    high = array.astype(jnp.bfloat16)
    low = (array - high.astype(np.float32)).astype(jnp.bfloat16)
    return high, low


class Geometry:
    def __init__(self, members, levels, ty, tx, rows):
        self.m, self.levels, self.ty, self.tx, self.rows = members, levels, ty, tx, rows
        self.lines = members * ty
        self.blocks = tx // LANES
        self.wide = tx // BLOCK
        self.chunks = levels * self.blocks
        self.half = rows // 2
        self.per = self.chunks // self.half
        self.x_rates = [filter_rates(tx / 16.0), filter_rates(tx / 64.0)]
        self.y_rates = [filter_rates(rows * ty / 2.0), filter_rates(ty / 2.0)]

    def row_matrix(self, reverse):
        m, ty = self.m, self.ty
        result = []
        for a, b in self.y_rates:
            place = np.arange(ty)
            gap = place[:, None] - place[None, :]
            local = np.where(gap >= 0, b * b * (gap + 1.0) * a ** np.maximum(gap, 0), 0.0)
            edge = np.stack([b * a ** (ty - 1.0 - place), b * b * (ty - place) * a ** (ty - 1.0 - place)])
            if reverse:
                local, edge = local.T, edge[:, ::-1]
            main = np.kron(np.eye(m), local)
            ends = np.concatenate([np.kron(np.eye(m), edge[s : s + 1]) for s in range(2)])
            result.append(np.concatenate([main, ends]))
        return halves(np.stack(result).astype(np.float32))

    def col_tables(self, reverse):
        tx = self.tx
        result = []
        for a, b in self.x_rates:
            place = np.arange(tx)
            ends = [b * a ** (tx - 1.0 - place), b * b * (tx - place) * a ** (tx - 1.0 - place)]
            enter = [b * (place + 1.0) * a ** (place + 1.0), a ** (place + 1.0)]
            table = np.stack(ends + enter)
            result.append(table[:, ::-1] if reverse else table)
        return np.stack(result).astype(np.float32)

    def row_tables(self, reverse):
        result = []
        for a, b in self.y_rates:
            place = np.arange(self.ty)
            table = np.stack([b * (place + 1.0) * a ** (place + 1.0), a ** (place + 1.0)])
            table = table[:, ::-1] if reverse else table
            result.append(np.broadcast_to(table[:, :, None], (2, self.ty, LANES)))
        return np.stack(result).astype(np.float32)

    def row_step(self):
        return [(a**self.ty, b * self.ty * a**self.ty) for a, b in self.y_rates]


def split(value):
    high = value.astype(BF16)
    return high, (value - high.astype(F32)).astype(BF16)


def dot(a, b):
    return jnp.dot(a, b, preferred_element_type=F32)


def dot3(ah, al, bh, bl):
    return dot(ah, bh) + dot(al, bh) + dot(ah, bl)


def each(low, high, action, unroll=1):
    def one(i, carry):
        action(i)
        return carry

    lax.fori_loop(low, high, one, 0, unroll=unroll)


def lanes(start, size=LANES):
    return pl.ds(pl.multiple_of(start, LANES), size)


def remote(src, dst, send, recv, device):
    return pltpu.make_async_remote_copy(
        src_ref=src, dst_ref=dst, send_sem=send, recv_sem=recv, device_id=device, device_id_type=MESH
    )


def scale_of(geo):
    return float(geo.m * 2) ** -0.5


def make_strips(geo, reverse, high, low):
    step = LANES
    tx = geo.tx
    for level, (a, b) in enumerate(geo.x_rates):
        rate = float(np.log(a))

        def part(index, level=level, rate=rate, scale=b * b):
            first = pl.multiple_of(index * step, step)
            down = lax.broadcasted_iota(jnp.int32, (step, BLOCK), 0) + first
            across = lax.broadcasted_iota(jnp.int32, (step, BLOCK), 1)
            gap = down - across if reverse else across + (tx - BLOCK) - down
            gap_f = gap.astype(F32)
            value = scale * (gap_f + 1.0) * jnp.exp(jnp.maximum(gap_f, 0.0) * rate)
            value = jnp.where(gap >= 0, value, 0.0)
            h, w = split(value)
            high[level, pl.ds(first, step), :] = h
            low[level, pl.ds(first, step), :] = w

        each(0, tx // step, part)


class Filter:
    def __init__(self, geo, reverse, consts, comm, work, place):
        self.geo, self.reverse = geo, reverse
        self.ph, self.plo, self.cols, self.rowt = consts
        (self.esend, self.erecv, self.bsend, self.brecv, self.csend, self.crecv, self.dsend, self.sh, self.sl,
         self.e_s, self.e_r, self.b_s, self.b_r, self.c_s, self.c_r, self.d_s, self.d_r) = comm
        self.dh, self.dl, self.bcat, self.bout, self.field = work
        self.row, self.col = place
        self.other = 1 - self.col
        self.enters = jnp.where(self.col == (0 if reverse else 1), 1.0, 0.0).astype(F32)
        self.scans = lax.rem(self.row, 2) == self.col
        self.spot = self.row // 2
        self.end_scan = 1 - self.col
        self.ends = geo.chunks

    def edge(self, wide, totals):
        geo = self.geo
        cut = slice(wide * BLOCK, (wide + 1) * BLOCK)
        for level in range(geo.levels):
            value = dot3(
                self.ph[level, geo.lines :, :], self.plo[level, geo.lines :, :], self.dh[level, :, cut], self.dl[level, :, cut]
            )
            h, w = split(value)
            base = wide * 4 * geo.m
            self.bcat[level, base : base + 2 * geo.m, :] = h
            self.bcat[level, base + 2 * geo.m : base + 4 * geo.m, :] = w
            for s in range(2):
                for k in range(BLOCK // LANES):
                    at = wide * BLOCK + k * LANES
                    totals[level][s] += value[:, k * LANES : (k + 1) * LANES] * self.cols[level, s : s + 1, at : at + LANES]

    def edge_start(self):
        geo = self.geo
        return [[jnp.zeros((2 * geo.m, LANES), F32) for s in range(2)] for level in range(geo.levels)]

    def edge_along_x(self, totals):
        geo = self.geo
        m, size = geo.m, 4 * geo.m
        lane = lax.broadcasted_iota(jnp.int32, (2 * m, LANES), 1)
        ends = jnp.zeros((2 * m, LANES), F32)
        for level in range(geo.levels):
            for s in range(2):
                total = jnp.sum(totals[level][s], axis=1, keepdims=True)
                ends = jnp.where(lane == 2 * level + s, total, ends)
        self.bsend[self.ends, 0] = ends[:m]
        self.bsend[self.ends, 1] = ends[m:]
        for level in range(geo.levels):
            sums = [None] * geo.wide
            for gap in range(geo.wide):
                count = geo.wide - gap
                if self.reverse:
                    rows = slice(gap * size, geo.wide * size)
                    strip = slice(gap * BLOCK, (gap + 1) * BLOCK)
                else:
                    rows = slice(0, count * size)
                    strip = slice((count - 1) * BLOCK, count * BLOCK)
                left = self.bcat[level, rows, :]
                value = dot(left, self.sh[level, strip, :]) + dot(left, self.sl[level, strip, :])
                for i in range(count):
                    to = i if self.reverse else i + gap
                    term = value[i * size : i * size + 2 * m] + value[i * size + 2 * m : (i + 1) * size]
                    sums[to] = term if sums[to] is None else sums[to] + term
            for wide in range(geo.wide):
                for k in range(BLOCK // LANES):
                    piece = sums[wide][:, k * LANES : (k + 1) * LANES]
                    chunk = level * geo.blocks + wide * (BLOCK // LANES) + k
                    self.bsend[chunk, 0] = piece[:m]
                    self.bsend[chunk, 1] = piece[m:]

    def row_of(self, i):
        return 2 * i + self.col

    def b_copy(self, p, i, source):
        half, rows = self.geo.half, self.geo.rows
        return remote(
            self.bsend.at[p * half + i], self.brecv.at[p, source], self.b_s.at[p * half + i],
            self.b_r.at[p * rows + source], {"row": self.row_of(i)},
        )

    def c_copy(self, p, i, target):
        half, rows = self.geo.half, self.geo.rows
        return remote(
            self.csend.at[p, target], self.crecv.at[p * half + i], self.c_s.at[p * rows + target],
            self.c_r.at[p * half + i], {"row": target},
        )

    def end_copy(self, source):
        slot, rows = self.geo.per, self.geo.rows
        return remote(
            self.bsend.at[self.ends], self.brecv.at[0, source], self.d_s.at[0], self.b_r.at[source], {"row": self.end_scan}
        )

    def give_copy(self, target):
        return remote(
            self.csend.at[0, target], self.crecv.at[self.ends], self.c_s.at[target], self.d_r.at[0],
            {"row": target, "col": self.other},
        )

    def gather_start(self):
        geo = self.geo
        pl.when(self.row != self.end_scan)(lambda: self.end_copy(self.row).start())
        for p in range(geo.per):
            def begin(i, p=p):
                pl.when(self.row_of(i) != self.row)(lambda: self.b_copy(p, i, self.row).start())

            each(0, geo.half, begin, 4 if geo.half % 4 == 0 else 1)

        @pl.when(self.row == self.end_scan)
        def _():
            self.brecv[0, self.row] = self.bsend[self.ends]

        @pl.when(self.scans)
        def _():
            for p in range(geo.per):
                self.brecv[p, self.row] = self.bsend[p * geo.half + self.spot]

    def run_scan(self, p, keep, mix):
        geo = self.geo

        def advance(lap, state):
            s1, s2 = state
            r = geo.rows - 1 - lap if self.reverse else lap
            self.csend[p, r, 0] = s1
            self.csend[p, r, 1] = s2
            return keep * s1 + self.brecv[p, r, 0], keep * s2 + mix * s1 + self.brecv[p, r, 1]

        zero = jnp.zeros((geo.m, LANES), F32)
        lax.fori_loop(0, geo.rows, advance, (zero, zero), unroll=4 if geo.rows % 4 == 0 else 1)

    def scan(self):
        geo = self.geo
        steps = geo.row_step()

        @pl.when(self.row == self.end_scan)
        def _():
            each(0, geo.rows, lambda r: pl.when(r != self.row)(lambda: self.end_copy(r).wait_recv()))
            lane = lax.broadcasted_iota(jnp.int32, (geo.m, LANES), 1)
            keep = jnp.where(lane < 2, steps[0][0], steps[1][0]).astype(F32)
            mix = jnp.where(lane < 2, steps[0][1], steps[1][1]).astype(F32)
            self.run_scan(0, keep, mix)
            each(0, geo.rows, lambda r: self.give_copy(r).start())

        @pl.when(self.scans)
        def _():
            for p in range(geo.per):
                each(0, geo.rows, lambda r, p=p: pl.when(r != self.row)(lambda: self.b_copy(p, self.spot, r).wait_recv()))
                first = p * geo.half + self.spot < geo.blocks
                keep = jnp.where(first, steps[0][0], steps[1][0]).astype(F32)
                mix = jnp.where(first, steps[0][1], steps[1][1]).astype(F32)
                self.run_scan(p, keep, mix)
                each(0, geo.rows, lambda r, p=p: pl.when(r != self.row)(lambda: self.c_copy(p, self.spot, r).start()))
                self.crecv[p * geo.half + self.spot] = self.csend[p, self.row]

    def main_rows(self):
        geo = self.geo
        for level in range(geo.levels):
            sums = [jnp.zeros((geo.lines, LANES), F32) for s in range(2)]
            for wide in range(geo.wide):
                cut = slice(wide * BLOCK, (wide + 1) * BLOCK)
                value = dot3(
                    self.ph[level, : geo.lines, :], self.plo[level, : geo.lines, :], self.dh[level, :, cut], self.dl[level, :, cut]
                )
                h, w = split(value)
                self.dh[level, :, cut] = h
                self.dl[level, :, cut] = w
                for k in range(BLOCK // LANES):
                    at = wide * BLOCK + k * LANES
                    piece = value[:, k * LANES : (k + 1) * LANES]
                    sums = [sums[s] + piece * self.cols[level, s : s + 1, at : at + LANES] for s in range(2)]
            for s in range(2):
                total = jnp.sum(sums[s], axis=1, keepdims=True)
                self.esend[level, s] = jnp.broadcast_to(total, (geo.lines, LANES))

    def e_copy(self):
        return remote(self.esend, self.erecv, self.e_s, self.e_r, {"col": self.other})

    def main_cols(self):
        geo = self.geo
        tx = geo.tx
        for level in range(geo.levels):
            for wide in range(geo.wide):
                if self.reverse:
                    cut, strip = slice(BLOCK * wide, tx), slice(0, tx - BLOCK * wide)
                else:
                    cut, strip = slice(0, BLOCK * (wide + 1)), slice(tx - BLOCK * (wide + 1), tx)
                self.field[level, :, wide * BLOCK : (wide + 1) * BLOCK] = dot3(
                    self.dh[level, :, cut], self.dl[level, :, cut], self.sh[level, strip, :], self.sl[level, strip, :]
                )

    def inner(self, level, i, at):
        cut = slice(i * self.geo.ty, (i + 1) * self.geo.ty)
        q = self.cols[level, 2:3, at] * self.enters
        w = self.cols[level, 3:4, at] * self.enters
        return self.field[level, cut, at] + self.erecv[level, 0, cut] * q + self.erecv[level, 1, cut] * w

    def take(self):
        geo = self.geo
        for p in range(geo.per):
            def taken(i, p=p):
                @pl.when(self.row_of(i) != self.row)
                def _():
                    self.b_copy(p, i, self.row).wait_send()
                    self.c_copy(p, i, self.row).wait_recv()

            each(0, geo.half, taken)
        self.give_copy(self.row).wait_recv()
        ends = [self.crecv[self.ends, s] * self.enters for s in range(2)]
        return [
            [[jnp.broadcast_to(ends[s][:, 2 * level + e : 2 * level + e + 1], (geo.m, LANES)) for e in range(2)] for s in range(2)]
            for level in range(geo.levels)
        ]

    def entering(self, ends, level, k):
        at = slice(k * LANES, (k + 1) * LANES)
        q, w = self.cols[level, 2:3, at], self.cols[level, 3:4, at]
        return [
            self.crecv[level * self.geo.blocks + k, s] + ends[level][s][0] * q + ends[level][s][1] * w for s in range(2)
        ]

    def sent(self):
        geo = self.geo
        pl.when(self.row != self.end_scan)(lambda: self.end_copy(self.row).wait_send())

        @pl.when(self.row == self.end_scan)
        def _():
            each(0, geo.rows, lambda r: self.give_copy(r).wait_send())

        @pl.when(self.scans)
        def _():
            for p in range(geo.per):
                each(0, geo.rows, lambda r, p=p: pl.when(r != self.row)(lambda: self.c_copy(p, self.spot, r).wait_send()))


def stencil_rows(data, ty):
    y0, fy, fz = data[0:1], data[2:3], data[4:5]
    place = lax.broadcasted_iota(jnp.int32, (ty, CAP), 0).astype(F32)
    weight = jnp.where(place == y0, 1.0 - fy, jnp.where(place == y0 + 1.0, fy, 0.0))
    return jnp.concatenate([weight * (1.0 - fz), weight * fz], axis=0)


def kernel(geo, *refs):
    (control_h, members_h, corner, count, off_y, off_x, off_z, innov, prec, ph0, pl0, cols0, rowt0, ph1, pl1, cols1, rowt1,
     out, out_dep) = refs[:19]
    refs = refs[19:]
    control, members, in_sem = refs[:3]
    work, comms = refs[3:8], (refs[8:25], refs[25:42])
    (payload, arrived, back, returned, obs_s, obs_r, dep_s, dep_r, own, got, total, got2, own_s, own_r, tot_s, tot_r,
     select, parts, mixed, latest, spread) = refs[42:]
    m, levels, ty, tx, rows = geo.m, geo.levels, geo.ty, geo.tx, geo.rows
    cells = levels * ty
    wides, per_wide = geo.wide, BLOCK // LANES
    row, col, mem = lax.axis_index("row"), lax.axis_index("col"), lax.axis_index("mem")
    tiles = rows * 2
    me = row * 2 + col
    partner = {"mem": 1 - mem}
    dh, dl, bcat, bout, field = work
    unroll = 7 if (tiles - 1) % 7 == 0 else 1

    loads = [
        pltpu.make_async_copy(control_h, control, in_sem.at[0]),
        pltpu.make_async_copy(members_h, members, in_sem.at[1]),
    ]
    for load in loads:
        load.start()

    def where_is(t):
        return {"row": t // 2, "col": lax.rem(t, 2)}

    barrier = pltpu.get_barrier_semaphore()

    def greet(k):
        t = lax.rem(me + k, tiles)
        pl.semaphore_signal(barrier, inc=1, device_id=where_is(t), device_id_type=MESH)

    each(1, tiles, greet, unroll)
    pl.semaphore_signal(barrier, inc=1, device_id=partner, device_id_type=MESH)

    place = (row, col)
    ahead = Filter(geo, False, (ph0, pl0, cols0, rowt0), comms[0], work, place)
    behind = Filter(geo, True, (ph1, pl1, cols1, rowt1), comms[1], work, place)

    make_strips(geo, False, ahead.sh, ahead.sl)
    for load in loads:
        load.wait()
    for level in range(levels):
        for i in range(m):
            cut = slice(i * ty, (i + 1) * ty)
            h, w = split(control[i, level])
            dh[level, cut, :] = h
            dl[level, cut, :] = w
    totals = ahead.edge_start()
    for wide in range(wides):
        ahead.edge(wide, totals)
    ahead.edge_along_x(totals)

    corners = corner[...]
    row_in = lax.shift_right_logical(corners, int(tx).bit_length() - 1)
    payload[:, 0, :] = row_in.astype(F32)
    payload[:, 1, :] = (corners - row_in * tx).astype(F32)
    payload[:, 2, :] = off_y[...]
    payload[:, 3, :] = off_x[...]
    payload[:, 4, :] = off_z[...]
    payload[:, 5, :] = innov[...]
    down = lax.broadcasted_iota(jnp.int32, (tiles, tiles), 0)
    across = lax.broadcasted_iota(jnp.int32, (tiles, tiles), 1)
    used = jnp.sum(jnp.where(down == across, count[...].astype(F32), 0.0), axis=1, keepdims=True)
    slot = lax.broadcasted_iota(jnp.int32, (tiles, CAP), 1).astype(F32)
    payload[:, 6, :] = jnp.where(slot < used, prec[...], 0.0)
    payload[:, 7, :] = jnp.zeros((tiles, CAP), F32)

    pl.semaphore_wait(barrier, tiles)
    ahead.gather_start()

    def obs_copy(k, to, slot):
        return remote(payload.at[to], arrived.at[slot], obs_s.at[k - 1], obs_r.at[k - 1], where_is(to))

    def dep_copy(k, to, slot):
        return remote(back.at[to], returned.at[slot], dep_s.at[k - 1], dep_r.at[k - 1], where_is(to))

    each(1, tiles, lambda k: obs_copy(k, lax.rem(me + k, tiles), me).start(), unroll)
    arrived[me] = payload[me]

    ahead.main_rows()
    ahead.e_copy().start()
    ahead.main_cols()
    ahead.scan()

    make_strips(geo, True, behind.sh, behind.sl)
    ahead.e_copy().wait()
    for wide in range(wides):
        for k in range(per_wide):
            at = slice(wide * BLOCK + k * LANES, wide * BLOCK + (k + 1) * LANES)
            for level in range(levels):
                value = members[0, level, :, at].astype(F32) * ahead.inner(level, 0, at)
                for i in range(1, m):
                    value = value + members[i, level, :, at].astype(F32) * ahead.inner(level, i, at)
                own[wide, level * ty : (level + 1) * ty, k * LANES : (k + 1) * LANES] = value

    def obs_end(k):
        copy = obs_copy(k, lax.rem(me + k, tiles), lax.rem(me - k + tiles, tiles))
        copy.wait_send()
        copy.wait_recv()

    each(1, tiles, obs_end)

    iota = lax.broadcasted_iota(jnp.int32, (LANES, CAP), 0).astype(F32)

    def choose(s):
        x0 = arrived[s, 1:2, :]
        for first in range(0, tx, LANES):
            select[first : first + LANES, lanes(s * CAP)] = jnp.where(iota == x0 - float(first), 1.0, 0.0).astype(BF16)

    each(0, tiles, choose)

    ends = ahead.take()

    def own_copy(wide):
        return remote(own.at[wide], got.at[wide], own_s.at[wide], own_r.at[wide], partner)

    for wide in reversed(range(wides)):
        for k in range(per_wide):
            block = wide * per_wide + k
            at = slice(block * LANES, (block + 1) * LANES)
            here = slice(k * LANES, (k + 1) * LANES)
            for level in range(levels):
                s1, s2 = ahead.entering(ends, level, block)
                value = own[wide, level * ty : (level + 1) * ty, here]
                for i in range(m):
                    value = value + members[i, level, :, at].astype(F32) * (
                        rowt0[level, 0] * s1[i : i + 1, :] + rowt0[level, 1] * s2[i : i + 1, :]
                    )
                own[wide, level * ty : (level + 1) * ty, here] = value * scale_of(geo)
        own_copy(wide).start()

    lane = lax.broadcasted_iota(jnp.int32, (cells, BLOCK), 1)
    first_of_right = jnp.zeros((cells, 1), F32)
    for wide in reversed(range(wides)):
        own_copy(wide).wait_recv()
        value = own[wide] + got[wide]
        moved = jnp.where(lane == BLOCK - 1, first_of_right, pltpu.roll(value, BLOCK - 1, 1))
        first_of_right = value[:, 0:1]
        h, w = split(value)
        parts[0:cells] = h
        parts[cells : 2 * cells] = w
        h, w = split(moved)
        parts[2 * cells : 3 * cells] = h
        parts[3 * cells :] = w
        rows_of = slice(wide * BLOCK, (wide + 1) * BLOCK)
        if wide > 0:
            def gather(t, wide=wide, rows_of=rows_of):
                at = lanes(t * 2 * BLOCK, 2 * BLOCK)
                value = dot(parts[...], select[rows_of, at])
                if wide < wides - 1:
                    value = value + mixed[:, at]
                mixed[:, at] = value

            each(0, tiles * CAP // (2 * BLOCK), gather)

    pair = BLOCK // CAP
    groups = tiles // pair
    rows_of = slice(0, BLOCK)
    latest[0] = dot(parts[...], select[rows_of, 0:BLOCK])

    def interpolate(t):
        ahead_t = jnp.minimum(t + 1, groups - 1)
        latest[lax.rem(t + 1, 2)] = dot(parts[...], select[rows_of, lanes(ahead_t * BLOCK, BLOCK)])
        now = lax.rem(t, 2)
        for i in range(pair):
            s = t * pair + i
            data = arrived[s]
            cut = slice(i * CAP, (i + 1) * CAP)
            here = lanes(s * CAP)
            fx = data[3:4]

            def part(j):
                mine = slice(j * cells, (j + 1) * cells)
                return latest[now, mine, cut] + mixed[mine, here]

            left = part(0) + part(1)
            right = part(2) + part(3)
            weight = stencil_rows(data, ty)
            image = jnp.sum(weight * (left + fx * (right - left)), axis=0, keepdims=True)
            departure = data[6:7] * (image - data[5:6])
            back[s] = jnp.broadcast_to(departure, (8, CAP))
            weight = weight * (departure * scale_of(geo))
            far = weight * fx
            h, w = split(weight - far)
            spread[0:cells, here] = h
            spread[cells : 2 * cells, here] = w
            h, w = split(far)
            spread[2 * cells : 3 * cells, here] = h
            spread[3 * cells :, here] = w

    each(0, groups, interpolate)

    def tot_copy(wide):
        return remote(total.at[wide], got2.at[wide], tot_s.at[wide], tot_r.at[wide], partner)

    lane = lax.broadcasted_iota(jnp.int32, (cells, LANES), 1)
    last = jnp.zeros((cells, LANES), F32)
    for wide in range(wides):
        piece = lax.dot_general(
            select[wide * BLOCK : (wide + 1) * BLOCK, :], spread[...], (((1,), (1,)), ((), ())), preferred_element_type=F32
        )
        piece = piece.T
        for k in range(per_wide):
            cut = slice(k * LANES, (k + 1) * LANES)
            here = piece[0:cells, cut] + piece[cells : 2 * cells, cut]
            moved = pltpu.roll(piece[2 * cells : 3 * cells, cut] + piece[3 * cells :, cut], 1, 1)
            total[wide, :, cut] = here + jnp.where(lane == 0, last, moved)
            last = moved
        tot_copy(wide).start()

    totals = behind.edge_start()
    for wide in range(wides):
        tot_copy(wide).wait_recv()
        at = slice(wide * BLOCK, (wide + 1) * BLOCK)
        for level in range(levels):
            part = slice(level * ty, (level + 1) * ty)
            forcing = total[wide, part, :] + got2[wide, part, :]
            for i in range(m):
                h, w = split(members[i, level, :, at].astype(F32) * forcing)
                dh[level, i * ty : (i + 1) * ty, at] = h
                dl[level, i * ty : (i + 1) * ty, at] = w
        behind.edge(wide, totals)
    behind.edge_along_x(totals)
    behind.gather_start()
    each(1, tiles, lambda k: dep_copy(k, lax.rem(me + k, tiles), me).start(), unroll)
    returned[me] = back[me]
    behind.main_rows()
    behind.e_copy().start()
    behind.main_cols()
    behind.scan()
    behind.e_copy().wait()
    for level in range(levels):
        def finish(k, level=level):
            at = lanes(k * LANES)
            for i in range(m):
                out[i, level, :, at] = control[i, level, :, at] + behind.inner(level, i, at)

        each(0, geo.blocks, finish)

    def dep_end(k):
        copy = dep_copy(k, lax.rem(me + k, tiles), lax.rem(me - k + tiles, tiles))
        copy.wait_send()
        copy.wait_recv()

    each(1, tiles, dep_end)
    for t in range(tiles):
        out_dep[0:1, t * CAP : (t + 1) * CAP] = returned[t, 0:1, :]
    ahead.sent()
    for wide in range(wides):
        own_copy(wide).wait_send()
        tot_copy(wide).wait_send()
    ends = behind.take()
    for k in range(geo.blocks):
        at = slice(k * LANES, (k + 1) * LANES)
        for level in range(levels):
            s1, s2 = behind.entering(ends, level, k)
            for i in range(m):
                out[i, level, :, at] += rowt1[level, 0] * s1[i : i + 1, :] + rowt1[level, 1] * s2[i : i + 1, :]
    behind.sent()


def body(control, members, obs_corner, obs_count, offset_y, offset_x, offset_z, innovation, precision):
    m, levels, ty, tx = control.shape
    rows = lax.axis_size("row")
    tiles = rows * lax.axis_size("col")
    geo = Geometry(m, levels, ty, tx, rows)
    cells = levels * ty

    def by_tile(array):
        return array.reshape(tiles, CAP)

    operands = [control, members, by_tile(obs_corner), obs_count]
    operands += [by_tile(a) for a in (offset_y, offset_x, offset_z, innovation, precision)]
    for reverse in (False, True):
        ph, plo = geo.row_matrix(reverse)
        operands += [ph, plo, geo.col_tables(reverse), geo.row_tables(reverse)]
    operands = [jnp.asarray(a) for a in operands]
    dma = pltpu.SemaphoreType.DMA
    chunks, per, lines = geo.chunks, geo.per, geo.lines
    comm = [
        pltpu.VMEM((levels, 2, lines, LANES), F32),
        pltpu.VMEM((levels, 2, lines, LANES), F32),
        pltpu.VMEM((chunks + 1, 2, m, LANES), F32),
        pltpu.VMEM((per, rows, 2, m, LANES), F32),
        pltpu.VMEM((per, rows, 2, m, LANES), F32),
        pltpu.VMEM((chunks + 1, 2, m, LANES), F32),
        pltpu.VMEM((8, LANES), F32),
        pltpu.VMEM((levels, tx, BLOCK), BF16),
        pltpu.VMEM((levels, tx, BLOCK), BF16),
        dma,
        dma,
        dma((chunks,)),
        dma((per * rows,)),
        dma((per * rows,)),
        dma((chunks,)),
        dma((1,)),
        dma((1,)),
    ]
    scratch = [
        pltpu.VMEM(control.shape, F32),
        pltpu.VMEM(members.shape, BF16),
        dma((2,)),
        pltpu.VMEM((levels, lines, tx), BF16),
        pltpu.VMEM((levels, lines, tx), BF16),
        pltpu.VMEM((levels, geo.wide * 4 * m, BLOCK), BF16),
        pltpu.VMEM((8, LANES), F32),
        pltpu.VMEM((levels, lines, tx), F32),
    ]
    scratch += comm + comm
    wide_shape = (geo.wide, cells, BLOCK)
    scratch += [
        pltpu.VMEM((tiles, 8, CAP), F32),
        pltpu.VMEM((tiles, 8, CAP), F32),
        pltpu.VMEM((tiles, 8, CAP), F32),
        pltpu.VMEM((tiles, 8, CAP), F32),
        dma((tiles - 1,)),
        dma((tiles - 1,)),
        dma((tiles - 1,)),
        dma((tiles - 1,)),
        pltpu.VMEM(wide_shape, F32),
        pltpu.VMEM(wide_shape, F32),
        pltpu.VMEM(wide_shape, F32),
        pltpu.VMEM(wide_shape, F32),
        dma((geo.wide,)),
        dma((geo.wide,)),
        dma((geo.wide,)),
        dma((geo.wide,)),
        pltpu.VMEM((tx, tiles * CAP), BF16),
        pltpu.VMEM((4 * cells, BLOCK), BF16),
        pltpu.VMEM((4 * cells, tiles * CAP), F32),
        pltpu.VMEM((2, 4 * cells, BLOCK), F32),
        pltpu.VMEM((4 * cells, tiles * CAP), BF16),
    ]
    hbm = pl.BlockSpec(memory_space=pl.ANY)
    return pl.pallas_call(
        functools.partial(kernel, geo),
        out_shape=(pltpu.VMEM(control.shape, F32), pltpu.VMEM((1, tiles * CAP), F32)),
        in_specs=[hbm, hbm] + [VMEM] * (len(operands) - 2),
        out_specs=(VMEM, VMEM),
        scratch_shapes=scratch,
        compiler_params=pltpu.CompilerParams(collective_id=0, has_side_effects=True, vmem_limit_bytes=58 * 1024 * 1024),
        name="gradient",
    )(*operands)


def solution(mesh):
    return jax.shard_map(
        body,
        mesh=mesh,
        in_specs=(
            P("mem", None, "row", "col"),
            P("mem", None, "row", "col"),
            P(("mem", "row", "col"), None),
            P(("mem", "row", "col"), None),
            P(("mem", "row", "col"), None),
            P(("mem", "row", "col"), None),
            P(("mem", "row", "col"), None),
            P(("mem", "row", "col"), None),
            P(("mem", "row", "col"), None),
        ),
        out_specs=(P("mem", None, "row", "col"), P(("mem", "row", "col"), None)),
        check_vma=False,
    )
```

```python
import functools

import jax
import jax.numpy as jnp
import numpy as np
from jax import lax
from jax.experimental import pallas as pl
from jax.experimental.pallas import tpu as pltpu
from jax.sharding import PartitionSpec as P

CAP = 128
LANES = 128
BLOCK = 256
F32 = jnp.float32
BF16 = jnp.bfloat16
MESH = pl.DeviceIdType.MESH
VMEM = pl.BlockSpec(memory_space=pltpu.VMEM)


def filter_rates(length):
    one = np.float32(1.0)
    decay = np.exp(-one / np.float32(length), dtype=np.float32)
    square = np.float32(decay * decay)
    weight = np.power(np.power(one - square, np.float32(3.0)) / (one + square), np.float32(0.25))
    return float(decay), float(weight)


def halves(array):
    high = array.astype(jnp.bfloat16)
    low = (array - high.astype(np.float32)).astype(jnp.bfloat16)
    return high, low


class Geometry:
    def __init__(self, members, levels, ty, tx, rows):
        self.m, self.levels, self.ty, self.tx, self.rows = members, levels, ty, tx, rows
        self.lines = members * ty
        self.blocks = tx // LANES
        self.wide = tx // BLOCK
        self.chunks = levels * self.blocks
        self.half = rows // 2
        self.per = self.chunks // self.half
        self.x_rates = [filter_rates(tx / 16.0), filter_rates(tx / 64.0)]
        self.y_rates = [filter_rates(rows * ty / 2.0), filter_rates(ty / 2.0)]

    def row_matrix(self, reverse):
        m, ty = self.m, self.ty
        result = []
        for a, b in self.y_rates:
            place = np.arange(ty)
            gap = place[:, None] - place[None, :]
            local = np.where(gap >= 0, b * b * (gap + 1.0) * a ** np.maximum(gap, 0), 0.0)
            edge = np.stack([b * a ** (ty - 1.0 - place), b * b * (ty - place) * a ** (ty - 1.0 - place)])
            if reverse:
                local, edge = local.T, edge[:, ::-1]
            main = np.kron(np.eye(m), local)
            ends = np.concatenate([np.kron(np.eye(m), edge[s : s + 1]) for s in range(2)])
            result.append(np.concatenate([main, ends]))
        return halves(np.stack(result).astype(np.float32))

    def col_tables(self, reverse):
        tx = self.tx
        result = []
        for a, b in self.x_rates:
            place = np.arange(tx)
            ends = [b * a ** (tx - 1.0 - place), b * b * (tx - place) * a ** (tx - 1.0 - place)]
            enter = [b * (place + 1.0) * a ** (place + 1.0), a ** (place + 1.0)]
            table = np.stack(ends + enter)
            result.append(table[:, ::-1] if reverse else table)
        return np.stack(result).astype(np.float32)

    def row_tables(self, reverse):
        result = []
        for a, b in self.y_rates:
            place = np.arange(self.ty)
            table = np.stack([b * (place + 1.0) * a ** (place + 1.0), a ** (place + 1.0)])
            table = table[:, ::-1] if reverse else table
            result.append(np.broadcast_to(table[:, :, None], (2, self.ty, LANES)))
        return np.stack(result).astype(np.float32)

    def row_step(self):
        return [(a**self.ty, b * self.ty * a**self.ty) for a, b in self.y_rates]


def split(value):
    high = value.astype(BF16)
    return high, (value - high.astype(F32)).astype(BF16)


def dot(a, b):
    return jnp.dot(a, b, preferred_element_type=F32)


def dot3(ah, al, bh, bl):
    return dot(ah, bh) + dot(al, bh) + dot(ah, bl)


def each(low, high, action, unroll=1):
    def one(i, carry):
        action(i)
        return carry

    lax.fori_loop(low, high, one, 0, unroll=unroll)


def lanes(start, size=LANES):
    return pl.ds(pl.multiple_of(start, LANES), size)


def remote(src, dst, send, recv, device):
    return pltpu.make_async_remote_copy(
        src_ref=src, dst_ref=dst, send_sem=send, recv_sem=recv, device_id=device, device_id_type=MESH
    )


def scale_of(geo):
    return float(geo.m * 2) ** -0.5


def joined(ref, index, first, last, rows=slice(None)):
    return jnp.concatenate([ref[index, k, rows, :] for k in range(first, last)], axis=1)


def make_strips(geo, reverse, high, low):
    step = LANES
    tx = geo.tx
    down = lax.broadcasted_iota(jnp.int32, (step, LANES), 0).astype(F32)
    across = lax.broadcasted_iota(jnp.int32, (step, LANES), 1).astype(F32)
    lane = lax.broadcasted_iota(jnp.int32, (1, LANES), 1).astype(F32)
    slope = down - across if reverse else across - down
    for level, (a, b) in enumerate(geo.x_rates):
        rate = float(np.log(a))
        power = jnp.exp(down * (rate if reverse else -rate))
        for index in range(tx // step):
            for half in range(BLOCK // LANES):
                first = index * step
                if reverse:
                    shift = first - half * LANES
                    line = (b * b) * jnp.exp((shift - lane) * rate)
                else:
                    shift = tx - BLOCK - first + half * LANES
                    line = (b * b) * jnp.exp((shift + lane) * rate)
                if shift <= -LANES:
                    value = jnp.zeros((step, LANES), F32)
                else:
                    value = (slope + (shift + 1.0)) * (power * line)
                    if shift < LANES:
                        value = jnp.where(slope >= -float(shift), value, 0.0)
                h, w = split(value)
                high[level, half, first : first + step, :] = h
                low[level, half, first : first + step, :] = w


class Peers:
    def __init__(self, geo, row, col):
        bits = geo.rows.bit_length() - 1
        flips = [(1 - 2 * lax.rem(row // 2**i, 2)) * 2**i for i in range(bits)]
        self.row_at = [row]
        for i in range(bits):
            self.row_at += [r + flips[i] for r in self.row_at]
        self.col_at = [col, 1 - col]
        ring = (0, 1, 2, 1)
        hops = lambda k: 2 * ((k >> 1) & 1) + ring[(k >> 2) & 3] + ring[(k >> 4) & 3]
        self.order = sorted(range(1, 2 * geo.rows), key=lambda k: -hops(k))

    def device(self, k):
        return {"row": self.row_at[k >> 1], "col": self.col_at[k & 1]}

    def index(self, k):
        return self.row_at[k >> 1] * 2 + self.col_at[k & 1]


class Filter:
    def __init__(self, geo, reverse, consts, comm, work, place):
        self.geo, self.reverse = geo, reverse
        self.ph, self.plo, self.cols, self.rowt = consts
        (self.esend, self.erecv, self.bsend, self.brecv, self.csend, self.crecv, self.dsend, self.sh, self.sl,
         self.e_s, self.e_r, self.b_s, self.b_r, self.c_s, self.c_r, self.d_s, self.d_r) = comm
        self.dh, self.dl, self.bcat, self.bout, self.field = work
        self.row, self.col = place
        self.other = 1 - self.col
        self.enters = jnp.where(self.col == (0 if reverse else 1), 1.0, 0.0).astype(F32)
        self.scans = lax.rem(self.row, 2) == self.col
        self.spot = self.row // 2
        self.end_scan = 1 - self.col
        self.ends = geo.chunks

    def edge(self, wide, totals):
        geo = self.geo
        for level in range(geo.levels):
            value = dot3(
                self.ph[level, geo.lines :, :], self.plo[level, geo.lines :, :],
                joined(self.dh, level, 2 * wide, 2 * wide + 2), joined(self.dl, level, 2 * wide, 2 * wide + 2),
            )
            h, w = split(value)
            base = wide * 4 * geo.m
            self.bcat[level, base : base + 2 * geo.m, :] = h
            self.bcat[level, base + 2 * geo.m : base + 4 * geo.m, :] = w
            for s in range(2):
                for k in range(BLOCK // LANES):
                    at = wide * BLOCK + k * LANES
                    totals[level][s] += value[:, k * LANES : (k + 1) * LANES] * self.cols[level, s : s + 1, at : at + LANES]

    def edge_start(self):
        geo = self.geo
        return [[jnp.zeros((2 * geo.m, LANES), F32) for s in range(2)] for level in range(geo.levels)]

    def edge_along_x(self, totals):
        geo = self.geo
        m, size = geo.m, 4 * geo.m
        lane = lax.broadcasted_iota(jnp.int32, (2 * m, LANES), 1)
        ends = jnp.zeros((2 * m, LANES), F32)
        for level in range(geo.levels):
            for s in range(2):
                total = jnp.sum(totals[level][s], axis=1, keepdims=True)
                ends = jnp.where(lane == 2 * level + s, total, ends)
        self.bsend[self.ends, 0] = ends[:m]
        self.bsend[self.ends, 1] = ends[m:]
        for level in range(geo.levels):
            sums = [None] * geo.wide
            for gap in range(geo.wide):
                count = geo.wide - gap
                if self.reverse:
                    rows = slice(gap * size, geo.wide * size)
                    strip = slice(gap * BLOCK, (gap + 1) * BLOCK)
                else:
                    rows = slice(0, count * size)
                    strip = slice((count - 1) * BLOCK, count * BLOCK)
                left = self.bcat[level, rows, :]
                value = dot(left, joined(self.sh, level, 0, 2, strip)) + dot(left, joined(self.sl, level, 0, 2, strip))
                for i in range(count):
                    to = i if self.reverse else i + gap
                    term = value[i * size : i * size + 2 * m] + value[i * size + 2 * m : (i + 1) * size]
                    sums[to] = term if sums[to] is None else sums[to] + term
            for wide in range(geo.wide):
                for k in range(BLOCK // LANES):
                    piece = sums[wide][:, k * LANES : (k + 1) * LANES]
                    chunk = level * geo.blocks + wide * (BLOCK // LANES) + k
                    self.bsend[chunk, 0] = piece[:m]
                    self.bsend[chunk, 1] = piece[m:]

    def row_of(self, i):
        return 2 * i + self.col

    def b_copy(self, p, i, source):
        half, rows = self.geo.half, self.geo.rows
        return remote(
            self.bsend.at[p * half + i], self.brecv.at[p, source], self.b_s.at[p * half + i],
            self.b_r.at[p * rows + source], {"row": self.row_of(i)},
        )

    def c_copy(self, p, i, target):
        half, rows = self.geo.half, self.geo.rows
        return remote(
            self.csend.at[p, target], self.crecv.at[p * half + i], self.c_s.at[p * rows + target],
            self.c_r.at[p * half + i], {"row": target},
        )

    def end_copy(self, source):
        slot, rows = self.geo.per, self.geo.rows
        return remote(
            self.bsend.at[self.ends], self.brecv.at[0, source], self.d_s.at[0], self.b_r.at[source], {"row": self.end_scan}
        )

    def give_copy(self, target):
        return remote(
            self.csend.at[0, target], self.crecv.at[self.ends], self.c_s.at[target], self.d_r.at[0],
            {"row": target, "col": self.other},
        )

    def gather_start(self):
        geo = self.geo
        pl.when(self.row != self.end_scan)(lambda: self.end_copy(self.row).start())
        for p in range(geo.per):
            def begin(i, p=p):
                pl.when(self.row_of(i) != self.row)(lambda: self.b_copy(p, i, self.row).start())

            each(0, geo.half, begin, 4 if geo.half % 4 == 0 else 1)

        @pl.when(self.row == self.end_scan)
        def _():
            self.brecv[0, self.row] = self.bsend[self.ends]

        @pl.when(self.scans)
        def _():
            for p in range(geo.per):
                self.brecv[p, self.row] = self.bsend[p * geo.half + self.spot]

    def run_scan(self, p, keep, mix):
        geo = self.geo

        def advance(lap, state):
            s1, s2 = state
            r = geo.rows - 1 - lap if self.reverse else lap
            self.csend[p, r, 0] = s1
            self.csend[p, r, 1] = s2
            return keep * s1 + self.brecv[p, r, 0], keep * s2 + mix * s1 + self.brecv[p, r, 1]

        zero = jnp.zeros((geo.m, LANES), F32)
        lax.fori_loop(0, geo.rows, advance, (zero, zero), unroll=4 if geo.rows % 4 == 0 else 1)

    def scan(self):
        geo = self.geo
        steps = geo.row_step()

        @pl.when(self.row == self.end_scan)
        def _():
            each(0, geo.rows, lambda r: pl.when(r != self.row)(lambda: self.end_copy(r).wait_recv()))
            lane = lax.broadcasted_iota(jnp.int32, (geo.m, LANES), 1)
            keep = jnp.where(lane < 2, steps[0][0], steps[1][0]).astype(F32)
            mix = jnp.where(lane < 2, steps[0][1], steps[1][1]).astype(F32)
            self.run_scan(0, keep, mix)
            each(0, geo.rows, lambda r: self.give_copy(r).start())

        @pl.when(self.scans)
        def _():
            for p in range(geo.per):
                each(0, geo.rows, lambda r, p=p: pl.when(r != self.row)(lambda: self.b_copy(p, self.spot, r).wait_recv()))
                first = p * geo.half + self.spot < geo.blocks
                keep = jnp.where(first, steps[0][0], steps[1][0]).astype(F32)
                mix = jnp.where(first, steps[0][1], steps[1][1]).astype(F32)
                self.run_scan(p, keep, mix)
                each(0, geo.rows, lambda r, p=p: pl.when(r != self.row)(lambda: self.c_copy(p, self.spot, r).start()))
                self.crecv[p * geo.half + self.spot] = self.csend[p, self.row]

    def main_rows(self):
        geo = self.geo
        for level in range(geo.levels):
            sums = [jnp.zeros((geo.lines, LANES), F32) for s in range(2)]
            for wide in range(geo.wide):
                value = dot3(
                    self.ph[level, : geo.lines, :], self.plo[level, : geo.lines, :],
                    joined(self.dh, level, 2 * wide, 2 * wide + 2), joined(self.dl, level, 2 * wide, 2 * wide + 2),
                )
                for k in range(BLOCK // LANES):
                    at = wide * BLOCK + k * LANES
                    piece = value[:, k * LANES : (k + 1) * LANES]
                    h, w = split(piece)
                    self.dh[level, 2 * wide + k] = h
                    self.dl[level, 2 * wide + k] = w
                    sums = [sums[s] + piece * self.cols[level, s : s + 1, at : at + LANES] for s in range(2)]
            for s in range(2):
                total = jnp.sum(sums[s], axis=1, keepdims=True)
                self.esend[level, s] = jnp.broadcast_to(total, (geo.lines, LANES))

    def e_copy(self):
        return remote(self.esend, self.erecv, self.e_s, self.e_r, {"col": self.other})

    def main_cols(self):
        geo = self.geo
        tx = geo.tx
        for level in range(geo.levels):
            for wide in range(geo.wide):
                if self.reverse:
                    cut, strip = (2 * wide, geo.blocks), slice(0, tx - BLOCK * wide)
                else:
                    cut, strip = (0, 2 * wide + 2), slice(tx - BLOCK * (wide + 1), tx)
                self.field[level, :, wide * BLOCK : (wide + 1) * BLOCK] = dot3(
                    joined(self.dh, level, *cut), joined(self.dl, level, *cut),
                    joined(self.sh, level, 0, 2, strip), joined(self.sl, level, 0, 2, strip),
                )

    def inner(self, level, i, at):
        cut = slice(i * self.geo.ty, (i + 1) * self.geo.ty)
        q = self.cols[level, 2:3, at] * self.enters
        w = self.cols[level, 3:4, at] * self.enters
        return self.field[level, cut, at] + self.erecv[level, 0, cut] * q + self.erecv[level, 1, cut] * w

    def take(self):
        geo = self.geo
        for p in range(geo.per):
            def taken(i, p=p):
                @pl.when(self.row_of(i) != self.row)
                def _():
                    self.b_copy(p, i, self.row).wait_send()
                    self.c_copy(p, i, self.row).wait_recv()

            each(0, geo.half, taken)
        self.give_copy(self.row).wait_recv()
        ends = [self.crecv[self.ends, s] * self.enters for s in range(2)]
        return [
            [[jnp.broadcast_to(ends[s][:, 2 * level + e : 2 * level + e + 1], (geo.m, LANES)) for e in range(2)] for s in range(2)]
            for level in range(geo.levels)
        ]

    def entering(self, ends, level, k):
        at = slice(k * LANES, (k + 1) * LANES)
        q, w = self.cols[level, 2:3, at], self.cols[level, 3:4, at]
        return [
            self.crecv[level * self.geo.blocks + k, s] + ends[level][s][0] * q + ends[level][s][1] * w for s in range(2)
        ]

    def sent(self):
        geo = self.geo
        pl.when(self.row != self.end_scan)(lambda: self.end_copy(self.row).wait_send())

        @pl.when(self.row == self.end_scan)
        def _():
            each(0, geo.rows, lambda r: self.give_copy(r).wait_send())

        @pl.when(self.scans)
        def _():
            for p in range(geo.per):
                each(0, geo.rows, lambda r, p=p: pl.when(r != self.row)(lambda: self.c_copy(p, self.spot, r).wait_send()))


def stencil_rows(data, ty):
    y0, fy, fz = data[0:1], data[2:3], data[4:5]
    place = lax.broadcasted_iota(jnp.int32, (ty, CAP), 0).astype(F32)
    weight = jnp.where(place == y0, 1.0 - fy, jnp.where(place == y0 + 1.0, fy, 0.0))
    return jnp.concatenate([weight * (1.0 - fz), weight * fz], axis=0)


def kernel(geo, *refs):
    (control_h, members_h, corner, count, off_y, off_x, off_z, innov, prec, ph0, pl0, cols0, rowt0, ph1, pl1, cols1, rowt1,
     out, out_dep) = refs[:19]
    refs = refs[19:]
    control, members, in_sem = refs[:3]
    work, comms = refs[3:8], (refs[8:25], refs[25:42])
    (payload, arrived, back, returned, obs_s, obs_r, dep_s, dep_r, own, got, total, got2, own_s, own_r, tot_s, tot_r,
     select, parts, even, odd, spread) = refs[42:]
    m, levels, ty, tx, rows = geo.m, geo.levels, geo.ty, geo.tx, geo.rows
    cells = levels * ty
    wides, per_wide = geo.wide, BLOCK // LANES
    row, col, mem = lax.axis_index("row"), lax.axis_index("col"), lax.axis_index("mem")
    tiles = rows * 2
    me = row * 2 + col
    partner = {"mem": 1 - mem}
    dh, dl, bcat, bout, field = work
    peers = Peers(geo, row, col)

    loads = [
        pltpu.make_async_copy(control_h, control, in_sem.at[0]),
        pltpu.make_async_copy(members_h, members, in_sem.at[1]),
    ]
    for load in loads:
        load.start()

    barrier = pltpu.get_barrier_semaphore()
    for k in peers.order:
        pl.semaphore_signal(barrier, inc=1, device_id=peers.device(k), device_id_type=MESH)
    pl.semaphore_signal(barrier, inc=1, device_id=partner, device_id_type=MESH)

    place = (row, col)
    ahead = Filter(geo, False, (ph0, pl0, cols0, rowt0), comms[0], work, place)
    behind = Filter(geo, True, (ph1, pl1, cols1, rowt1), comms[1], work, place)

    make_strips(geo, False, ahead.sh, ahead.sl)
    for load in loads:
        load.wait()
    for level in range(levels):
        for i in range(m):
            cut = slice(i * ty, (i + 1) * ty)
            for k in range(geo.blocks):
                h, w = split(control[i, level, :, k * LANES : (k + 1) * LANES])
                dh[level, k, cut, :] = h
                dl[level, k, cut, :] = w
    totals = ahead.edge_start()
    for wide in range(wides):
        ahead.edge(wide, totals)
    ahead.edge_along_x(totals)

    pl.semaphore_wait(barrier, tiles)
    ahead.gather_start()

    corners = corner[...]
    row_in = lax.shift_right_logical(corners, int(tx).bit_length() - 1)
    payload[:, 0, :] = row_in.astype(F32)
    payload[:, 1, :] = (corners - row_in * tx).astype(F32)
    payload[:, 2, :] = off_y[...]
    payload[:, 3, :] = off_x[...]
    payload[:, 4, :] = off_z[...]
    payload[:, 5, :] = innov[...]
    down = lax.broadcasted_iota(jnp.int32, (tiles, tiles), 0)
    across = lax.broadcasted_iota(jnp.int32, (tiles, tiles), 1)
    used = jnp.sum(jnp.where(down == across, count[...].astype(F32), 0.0), axis=1, keepdims=True)
    slot = lax.broadcasted_iota(jnp.int32, (tiles, CAP), 1).astype(F32)
    payload[:, 6, :] = jnp.where(slot < used, prec[...], 0.0)
    payload[:, 7, :] = jnp.zeros((tiles, CAP), F32)

    def obs_copy(k, to, slot):
        return remote(payload.at[to], arrived.at[slot], obs_s.at[k - 1], obs_r.at[k - 1], peers.device(k))

    def dep_copy(k, to, slot):
        return remote(back.at[to], returned.at[slot], dep_s.at[k - 1], dep_r.at[k - 1], peers.device(k))

    for k in peers.order:
        obs_copy(k, peers.index(k), me).start()
    arrived[me] = payload[me]

    ahead.main_rows()
    ahead.e_copy().start()
    ahead.main_cols()
    ahead.scan()

    make_strips(geo, True, behind.sh, behind.sl)
    ahead.e_copy().wait()
    for wide in range(wides):
        for k in range(per_wide):
            at = slice(wide * BLOCK + k * LANES, wide * BLOCK + (k + 1) * LANES)
            for level in range(levels):
                value = members[0, level, :, at].astype(F32) * ahead.inner(level, 0, at)
                for i in range(1, m):
                    value = value + members[i, level, :, at].astype(F32) * ahead.inner(level, i, at)
                own[wide, level * ty : (level + 1) * ty, k * LANES : (k + 1) * LANES] = value

    for k in peers.order:
        copy = obs_copy(k, peers.index(k), peers.index(k))
        copy.wait_send()
        copy.wait_recv()

    iota = lax.broadcasted_iota(jnp.int32, (LANES, CAP), 0).astype(F32).astype(BF16)
    packed = 16

    def choose(s):
        x0 = arrived[s, 1:2, :]
        for first in range(0, tx, LANES):
            spot = jnp.broadcast_to(x0 - float(first), (packed, CAP)).astype(BF16)
            for g in range(0, LANES, packed):
                hit = iota[g : g + packed] == spot
                select[s, first + g : first + g + packed, :] = jnp.where(hit, 1.0, 0.0).astype(BF16)

    each(0, tiles, choose)

    ends = ahead.take()

    def own_copy(wide):
        return remote(own.at[wide], got.at[wide], own_s.at[wide], own_r.at[wide], partner)

    for wide in reversed(range(wides)):
        for k in range(per_wide):
            block = wide * per_wide + k
            at = slice(block * LANES, (block + 1) * LANES)
            here = slice(k * LANES, (k + 1) * LANES)
            for level in range(levels):
                s1, s2 = ahead.entering(ends, level, block)
                value = own[wide, level * ty : (level + 1) * ty, here]
                for i in range(m):
                    value = value + members[i, level, :, at].astype(F32) * (
                        rowt0[level, 0] * s1[i : i + 1, :] + rowt0[level, 1] * s2[i : i + 1, :]
                    )
                own[wide, level * ty : (level + 1) * ty, here] = value * scale_of(geo)
        own_copy(wide).start()

    lane = lax.broadcasted_iota(jnp.int32, (cells, BLOCK), 1)
    first_of_right = jnp.zeros((cells, 1), F32)
    for wide in reversed(range(wides)):
        own_copy(wide).wait_recv()
        value = own[wide] + got[wide]
        moved = jnp.where(lane == BLOCK - 1, first_of_right, pltpu.roll(value, BLOCK - 1, 1))
        first_of_right = value[:, 0:1]
        h, w = split(value)
        parts[0:cells, wide * BLOCK : (wide + 1) * BLOCK] = h
        parts[cells : 2 * cells, wide * BLOCK : (wide + 1) * BLOCK] = w
        h, w = split(moved)
        parts[2 * cells : 3 * cells, wide * BLOCK : (wide + 1) * BLOCK] = h
        parts[3 * cells :, wide * BLOCK : (wide + 1) * BLOCK] = w

    size = 4 if tiles >= 8 else 2
    groups = tiles // size

    def fetch(group, buffer):
        columns = jnp.concatenate([select[group * size + i] for i in range(size)], axis=1)
        buffer[...] = dot(parts[...], columns)

    def use(group, buffer):
        for i in range(size):
            s = group * size + i
            data = arrived[s]
            cut = slice(i * CAP, (i + 1) * CAP)
            fx = data[3:4]
            left = buffer[0:cells, cut] + buffer[cells : 2 * cells, cut]
            right = buffer[2 * cells : 3 * cells, cut] + buffer[3 * cells :, cut]
            weight = stencil_rows(data, ty)
            image = jnp.sum(weight * (left + fx * (right - left)), axis=0, keepdims=True)
            departure = data[6:7] * (image - data[5:6])
            back[s] = jnp.broadcast_to(departure, (8, CAP))
            weight = weight * (departure * scale_of(geo))
            far = weight * fx
            h, w = split(weight - far)
            spread[s, 0:cells] = h
            spread[s, cells : 2 * cells] = w
            h, w = split(far)
            spread[s, 2 * cells : 3 * cells] = h
            spread[s, 3 * cells :] = w

    fetch(0, even)

    def interpolate(t):
        fetch(2 * t + 1, odd)
        use(2 * t, even)
        fetch(jnp.minimum(2 * t + 2, groups - 1), even)
        use(2 * t + 1, odd)

    each(0, groups // 2, interpolate)

    def tot_copy(wide):
        return remote(total.at[wide], got2.at[wide], tot_s.at[wide], tot_r.at[wide], partner)

    lane = lax.broadcasted_iota(jnp.int32, (cells, LANES), 1)
    last = jnp.zeros((cells, LANES), F32)
    for wide in range(wides):
        piece = lax.dot_general(
            jnp.concatenate([select[s, wide * BLOCK : (wide + 1) * BLOCK, :] for s in range(tiles)], axis=1),
            jnp.concatenate([spread[s] for s in range(tiles)], axis=1),
            (((1,), (1,)), ((), ())),
            preferred_element_type=F32,
        )
        piece = piece.T
        for k in range(per_wide):
            cut = slice(k * LANES, (k + 1) * LANES)
            here = piece[0:cells, cut] + piece[cells : 2 * cells, cut]
            moved = pltpu.roll(piece[2 * cells : 3 * cells, cut] + piece[3 * cells :, cut], 1, 1)
            total[wide, :, cut] = here + jnp.where(lane == 0, last, moved)
            last = moved
        tot_copy(wide).start()

    totals = behind.edge_start()
    for wide in range(wides):
        tot_copy(wide).wait_recv()
        for level in range(levels):
            part = slice(level * ty, (level + 1) * ty)
            for k in range(per_wide):
                block = wide * per_wide + k
                here = slice(k * LANES, (k + 1) * LANES)
                forcing = total[wide, part, here] + got2[wide, part, here]
                for i in range(m):
                    h, w = split(members[i, level, :, block * LANES : (block + 1) * LANES].astype(F32) * forcing)
                    dh[level, block, i * ty : (i + 1) * ty, :] = h
                    dl[level, block, i * ty : (i + 1) * ty, :] = w
        behind.edge(wide, totals)
    behind.edge_along_x(totals)
    behind.gather_start()
    for k in peers.order:
        dep_copy(k, peers.index(k), me).start()
    returned[me] = back[me]
    behind.main_rows()
    behind.e_copy().start()
    behind.main_cols()
    behind.scan()
    behind.e_copy().wait()
    for level in range(levels):
        def finish(k, level=level):
            at = lanes(k * LANES)
            for i in range(m):
                out[i, level, :, at] = control[i, level, :, at] + behind.inner(level, i, at)

        each(0, geo.blocks, finish)

    for k in peers.order:
        copy = dep_copy(k, peers.index(k), peers.index(k))
        copy.wait_send()
        copy.wait_recv()
    for t in range(tiles):
        out_dep[0:1, t * CAP : (t + 1) * CAP] = returned[t, 0:1, :]
    ahead.sent()
    for wide in range(wides):
        own_copy(wide).wait_send()
        tot_copy(wide).wait_send()
    ends = behind.take()
    for k in range(geo.blocks):
        at = slice(k * LANES, (k + 1) * LANES)
        for level in range(levels):
            s1, s2 = behind.entering(ends, level, k)
            for i in range(m):
                out[i, level, :, at] += rowt1[level, 0] * s1[i : i + 1, :] + rowt1[level, 1] * s2[i : i + 1, :]
    behind.sent()


def body(control, members, obs_corner, obs_count, offset_y, offset_x, offset_z, innovation, precision):
    m, levels, ty, tx = control.shape
    rows = lax.axis_size("row")
    tiles = rows * lax.axis_size("col")
    geo = Geometry(m, levels, ty, tx, rows)
    cells = levels * ty
    size = 4 if tiles >= 8 else 2

    def by_tile(array):
        return array.reshape(tiles, CAP)

    operands = [control, members, by_tile(obs_corner), obs_count]
    operands += [by_tile(a) for a in (offset_y, offset_x, offset_z, innovation, precision)]
    for reverse in (False, True):
        ph, plo = geo.row_matrix(reverse)
        operands += [ph, plo, geo.col_tables(reverse), geo.row_tables(reverse)]
    operands = [jnp.asarray(a) for a in operands]
    dma = pltpu.SemaphoreType.DMA
    chunks, per, lines = geo.chunks, geo.per, geo.lines
    comm = [
        pltpu.VMEM((levels, 2, lines, LANES), F32),
        pltpu.VMEM((levels, 2, lines, LANES), F32),
        pltpu.VMEM((chunks + 1, 2, m, LANES), F32),
        pltpu.VMEM((per, rows, 2, m, LANES), F32),
        pltpu.VMEM((per, rows, 2, m, LANES), F32),
        pltpu.VMEM((chunks + 1, 2, m, LANES), F32),
        pltpu.VMEM((8, LANES), F32),
        pltpu.VMEM((levels, BLOCK // LANES, tx, LANES), BF16),
        pltpu.VMEM((levels, BLOCK // LANES, tx, LANES), BF16),
        dma,
        dma,
        dma((chunks,)),
        dma((per * rows,)),
        dma((per * rows,)),
        dma((chunks,)),
        dma((1,)),
        dma((1,)),
    ]
    scratch = [
        pltpu.VMEM(control.shape, F32),
        pltpu.VMEM(members.shape, BF16),
        dma((2,)),
        pltpu.VMEM((levels, geo.blocks, lines, LANES), BF16),
        pltpu.VMEM((levels, geo.blocks, lines, LANES), BF16),
        pltpu.VMEM((levels, geo.wide * 4 * m, BLOCK), BF16),
        pltpu.VMEM((8, LANES), F32),
        pltpu.VMEM((levels, lines, tx), F32),
    ]
    scratch += comm + comm
    wide_shape = (geo.wide, cells, BLOCK)
    scratch += [
        pltpu.VMEM((tiles, 8, CAP), F32),
        pltpu.VMEM((tiles, 8, CAP), F32),
        pltpu.VMEM((tiles, 8, CAP), F32),
        pltpu.VMEM((tiles, 8, CAP), F32),
        dma((tiles - 1,)),
        dma((tiles - 1,)),
        dma((tiles - 1,)),
        dma((tiles - 1,)),
        pltpu.VMEM(wide_shape, F32),
        pltpu.VMEM(wide_shape, F32),
        pltpu.VMEM(wide_shape, F32),
        pltpu.VMEM(wide_shape, F32),
        dma((geo.wide,)),
        dma((geo.wide,)),
        dma((geo.wide,)),
        dma((geo.wide,)),
        pltpu.VMEM((tiles, tx, CAP), BF16),
        pltpu.VMEM((4 * cells, tx), BF16),
        pltpu.VMEM((4 * cells, size * CAP), F32),
        pltpu.VMEM((4 * cells, size * CAP), F32),
        pltpu.VMEM((tiles, 4 * cells, CAP), BF16),
    ]
    hbm = pl.BlockSpec(memory_space=pl.ANY)
    return pl.pallas_call(
        functools.partial(kernel, geo),
        out_shape=(pltpu.VMEM(control.shape, F32), pltpu.VMEM((1, tiles * CAP), F32)),
        in_specs=[hbm, hbm] + [VMEM] * (len(operands) - 2),
        out_specs=(VMEM, VMEM),
        scratch_shapes=scratch,
        compiler_params=pltpu.CompilerParams(collective_id=0, has_side_effects=True, vmem_limit_bytes=58 * 1024 * 1024),
        name="gradient",
    )(*operands)


def solution(mesh):
    return jax.shard_map(
        body,
        mesh=mesh,
        in_specs=(
            P("mem", None, "row", "col"),
            P("mem", None, "row", "col"),
            P(("mem", "row", "col"), None),
            P(("mem", "row", "col"), None),
            P(("mem", "row", "col"), None),
            P(("mem", "row", "col"), None),
            P(("mem", "row", "col"), None),
            P(("mem", "row", "col"), None),
            P(("mem", "row", "col"), None),
        ),
        out_specs=(P("mem", None, "row", "col"), P(("mem", "row", "col"), None)),
        check_vma=False,
    )
```

```python
import functools

import jax
import jax.numpy as jnp
import numpy as np
from jax import lax
from jax.experimental import pallas as pl
from jax.experimental.pallas import tpu as pltpu
from jax.sharding import PartitionSpec as P

CAP = 128
LANES = 128
BLOCK = 256
F32 = jnp.float32
BF16 = jnp.bfloat16
MESH = pl.DeviceIdType.MESH
VMEM = pl.BlockSpec(memory_space=pltpu.VMEM)


def filter_rates(length):
    one = np.float32(1.0)
    decay = np.exp(-one / np.float32(length), dtype=np.float32)
    square = np.float32(decay * decay)
    weight = np.power(np.power(one - square, np.float32(3.0)) / (one + square), np.float32(0.25))
    return float(decay), float(weight)


def halves(array):
    high = array.astype(jnp.bfloat16)
    low = (array - high.astype(np.float32)).astype(jnp.bfloat16)
    return high, low


class Geometry:
    def __init__(self, members, levels, ty, tx, rows):
        self.m, self.levels, self.ty, self.tx, self.rows = members, levels, ty, tx, rows
        self.lines = members * ty
        self.blocks = tx // LANES
        self.wide = tx // BLOCK
        self.chunks = levels * self.blocks
        self.half = rows // 2
        self.per = self.chunks // self.half
        self.x_rates = [filter_rates(tx / 16.0), filter_rates(tx / 64.0)]
        self.y_rates = [filter_rates(rows * ty / 2.0), filter_rates(ty / 2.0)]

    def row_matrix(self, reverse):
        m, ty = self.m, self.ty
        result = []
        for a, b in self.y_rates:
            place = np.arange(ty)
            gap = place[:, None] - place[None, :]
            local = np.where(gap >= 0, b * b * (gap + 1.0) * a ** np.maximum(gap, 0), 0.0)
            edge = np.stack([b * a ** (ty - 1.0 - place), b * b * (ty - place) * a ** (ty - 1.0 - place)])
            if reverse:
                local, edge = local.T, edge[:, ::-1]
            main = np.kron(np.eye(m), local)
            ends = np.concatenate([np.kron(np.eye(m), edge[s : s + 1]) for s in range(2)])
            result.append(np.concatenate([main, ends]))
        return halves(np.stack(result).astype(np.float32))

    def col_tables(self, reverse):
        tx = self.tx
        result = []
        for a, b in self.x_rates:
            place = np.arange(tx)
            ends = [b * a ** (tx - 1.0 - place), b * b * (tx - place) * a ** (tx - 1.0 - place)]
            enter = [b * (place + 1.0) * a ** (place + 1.0), a ** (place + 1.0)]
            table = np.stack(ends + enter)
            result.append(table[:, ::-1] if reverse else table)
        return np.stack(result).astype(np.float32)

    def row_tables(self, reverse):
        result = []
        for a, b in self.y_rates:
            place = np.arange(self.ty)
            table = np.stack([b * (place + 1.0) * a ** (place + 1.0), a ** (place + 1.0)])
            table = table[:, ::-1] if reverse else table
            result.append(np.broadcast_to(table[:, :, None], (2, self.ty, LANES)))
        return np.stack(result).astype(np.float32)

    def row_step(self):
        return [(a**self.ty, b * self.ty * a**self.ty) for a, b in self.y_rates]


def split(value):
    high = value.astype(BF16)
    return high, (value - high.astype(F32)).astype(BF16)


def dot(a, b):
    return jnp.dot(a, b, preferred_element_type=F32)


def dot3(ah, al, bh, bl):
    return dot(ah, bh) + dot(al, bh) + dot(ah, bl)


def each(low, high, action, unroll=1):
    def one(i, carry):
        action(i)
        return carry

    lax.fori_loop(low, high, one, 0, unroll=unroll)


def lanes(start, size=LANES):
    return pl.ds(pl.multiple_of(start, LANES), size)


def remote(src, dst, send, recv, device):
    return pltpu.make_async_remote_copy(
        src_ref=src, dst_ref=dst, send_sem=send, recv_sem=recv, device_id=device, device_id_type=MESH
    )


def scale_of(geo):
    return float(geo.m * 2) ** -0.5


def joined(ref, index, first, last, rows=slice(None)):
    return jnp.concatenate([ref[index, k, rows, :] for k in range(first, last)], axis=1)


def make_strips(geo, reverse, high, low):
    step = LANES
    tx = geo.tx
    down = lax.broadcasted_iota(jnp.int32, (step, LANES), 0).astype(F32)
    across = lax.broadcasted_iota(jnp.int32, (step, LANES), 1).astype(F32)
    lane = lax.broadcasted_iota(jnp.int32, (1, LANES), 1).astype(F32)
    slope = down - across if reverse else across - down
    for level, (a, b) in enumerate(geo.x_rates):
        rate = float(np.log(a))
        power = jnp.exp(down * (rate if reverse else -rate))
        for index in range(tx // step):
            for half in range(BLOCK // LANES):
                first = index * step
                if reverse:
                    shift = first - half * LANES
                    line = (b * b) * jnp.exp((shift - lane) * rate)
                else:
                    shift = tx - BLOCK - first + half * LANES
                    line = (b * b) * jnp.exp((shift + lane) * rate)
                if shift <= -LANES:
                    value = jnp.zeros((step, LANES), F32)
                else:
                    value = (slope + (shift + 1.0)) * (power * line)
                    if shift < LANES:
                        value = jnp.where(slope >= -float(shift), value, 0.0)
                h, w = split(value)
                high[level, half, first : first + step, :] = h
                low[level, half, first : first + step, :] = w


class Peers:
    def __init__(self, geo, row, col):
        bits = geo.rows.bit_length() - 1
        flips = [(1 - 2 * lax.rem(row // 2**i, 2)) * 2**i for i in range(bits)]
        self.row_at = [row]
        for i in range(bits):
            self.row_at += [r + flips[i] for r in self.row_at]
        self.col_at = [col, 1 - col]
        ring = (0, 1, 2, 1)
        hops = lambda k: 2 * ((k >> 1) & 1) + ring[(k >> 2) & 3] + ring[(k >> 4) & 3]
        self.order = sorted(range(1, 2 * geo.rows), key=lambda k: -hops(k))

    def device(self, k):
        return {"row": self.row_at[k >> 1], "col": self.col_at[k & 1]}

    def index(self, k):
        return self.row_at[k >> 1] * 2 + self.col_at[k & 1]


class Filter:
    def __init__(self, geo, reverse, consts, comm, work, place):
        self.geo, self.reverse = geo, reverse
        self.ph, self.plo, self.cols, self.rowt = consts
        (self.esend, self.erecv, self.bsend, self.brecv, self.csend, self.crecv, self.dsend, self.sh, self.sl,
         self.e_s, self.e_r, self.b_s, self.b_r, self.c_s, self.c_r, self.d_s, self.d_r) = comm
        self.dh, self.dl, self.bcat, self.bout, self.field = work
        self.row, self.col = place
        self.other = 1 - self.col
        self.enters = jnp.where(self.col == (0 if reverse else 1), 1.0, 0.0).astype(F32)
        self.scans = lax.rem(self.row, 2) == self.col
        self.spot = self.row // 2
        self.end_scan = 1 - self.col
        self.ends = geo.chunks

    def edge(self, wide, totals):
        geo = self.geo
        for level in range(geo.levels):
            value = dot3(
                self.ph[level, geo.lines :, :], self.plo[level, geo.lines :, :],
                joined(self.dh, level, 2 * wide, 2 * wide + 2), joined(self.dl, level, 2 * wide, 2 * wide + 2),
            )
            h, w = split(value)
            base = wide * 4 * geo.m
            self.bcat[level, base : base + 2 * geo.m, :] = h
            self.bcat[level, base + 2 * geo.m : base + 4 * geo.m, :] = w
            for s in range(2):
                for k in range(BLOCK // LANES):
                    at = wide * BLOCK + k * LANES
                    totals[level][s] += value[:, k * LANES : (k + 1) * LANES] * self.cols[level, s : s + 1, at : at + LANES]

    def edge_start(self):
        geo = self.geo
        return [[jnp.zeros((2 * geo.m, LANES), F32) for s in range(2)] for level in range(geo.levels)]

    def edge_along_x(self, totals):
        geo = self.geo
        m, size = geo.m, 4 * geo.m
        lane = lax.broadcasted_iota(jnp.int32, (2 * m, LANES), 1)
        ends = jnp.zeros((2 * m, LANES), F32)
        for level in range(geo.levels):
            for s in range(2):
                total = jnp.sum(totals[level][s], axis=1, keepdims=True)
                ends = jnp.where(lane == 2 * level + s, total, ends)
        self.bsend[self.ends, 0] = ends[:m]
        self.bsend[self.ends, 1] = ends[m:]
        for level in range(geo.levels):
            sums = [None] * geo.wide
            for gap in range(geo.wide):
                count = geo.wide - gap
                if self.reverse:
                    rows = slice(gap * size, geo.wide * size)
                    strip = slice(gap * BLOCK, (gap + 1) * BLOCK)
                else:
                    rows = slice(0, count * size)
                    strip = slice((count - 1) * BLOCK, count * BLOCK)
                left = self.bcat[level, rows, :]
                value = dot(left, joined(self.sh, level, 0, 2, strip)) + dot(left, joined(self.sl, level, 0, 2, strip))
                for i in range(count):
                    to = i if self.reverse else i + gap
                    term = value[i * size : i * size + 2 * m] + value[i * size + 2 * m : (i + 1) * size]
                    sums[to] = term if sums[to] is None else sums[to] + term
            for wide in range(geo.wide):
                for k in range(BLOCK // LANES):
                    piece = sums[wide][:, k * LANES : (k + 1) * LANES]
                    chunk = level * geo.blocks + wide * (BLOCK // LANES) + k
                    self.bsend[chunk, 0] = piece[:m]
                    self.bsend[chunk, 1] = piece[m:]

    def row_of(self, i):
        return 2 * i + self.col

    def b_copy(self, p, i, source):
        half = self.geo.half
        return remote(
            self.bsend.at[p * half + i], self.brecv.at[p, source], self.b_s, self.b_r, {"row": self.row_of(i)}
        )

    def c_copy(self, p, i, target):
        half = self.geo.half
        return remote(
            self.csend.at[p, target], self.crecv.at[p * half + i], self.c_s, self.c_r, {"row": target}
        )

    def end_copy(self, source):
        return remote(
            self.bsend.at[self.ends], self.brecv.at[0, source], self.d_s, self.b_r, {"row": self.end_scan}
        )

    def give_copy(self, target):
        return remote(
            self.csend.at[0, target], self.crecv.at[self.ends], self.c_s, self.d_r,
            {"row": target, "col": self.other},
        )

    def whole(self, src, dst, send, recv):
        return remote(src, dst, send, recv, {"col": self.other})

    def gather_start(self):
        geo = self.geo
        pl.when(self.row != self.end_scan)(lambda: self.end_copy(self.row).start())
        for p in range(geo.per):
            def begin(i, p=p):
                pl.when(self.row_of(i) != self.row)(lambda: self.b_copy(p, i, self.row).start())

            each(0, geo.half, begin, 4 if geo.half % 4 == 0 else 1)

        @pl.when(self.row == self.end_scan)
        def _():
            self.brecv[0, self.row] = self.bsend[self.ends]

        @pl.when(self.scans)
        def _():
            for p in range(geo.per):
                self.brecv[p, self.row] = self.bsend[p * geo.half + self.spot]

    def run_scan(self, p, keep, mix):
        geo = self.geo

        def advance(lap, state):
            s1, s2 = state
            r = geo.rows - 1 - lap if self.reverse else lap
            self.csend[p, r, 0] = s1
            self.csend[p, r, 1] = s2
            return keep * s1 + self.brecv[p, r, 0], keep * s2 + mix * s1 + self.brecv[p, r, 1]

        zero = jnp.zeros((geo.m, LANES), F32)
        lax.fori_loop(0, geo.rows, advance, (zero, zero), unroll=4 if geo.rows % 4 == 0 else 1)

    def scan(self):
        geo = self.geo
        steps = geo.row_step()

        @pl.when(self.row == self.end_scan)
        def _():
            got = self.brecv.at[0, 0 : geo.rows - 1]
            self.whole(got, got, self.d_s, self.b_r).wait_recv()
            lane = lax.broadcasted_iota(jnp.int32, (geo.m, LANES), 1)
            keep = jnp.where(lane < 2, steps[0][0], steps[1][0]).astype(F32)
            mix = jnp.where(lane < 2, steps[0][1], steps[1][1]).astype(F32)
            self.run_scan(0, keep, mix)
            each(0, geo.rows, lambda r: self.give_copy(r).start())

        @pl.when(self.scans)
        def _():
            got = self.brecv.at[:, 0 : geo.rows - 1]
            self.whole(got, got, self.b_s, self.b_r).wait_recv()
            for p in range(geo.per):
                first = p * geo.half + self.spot < geo.blocks
                keep = jnp.where(first, steps[0][0], steps[1][0]).astype(F32)
                mix = jnp.where(first, steps[0][1], steps[1][1]).astype(F32)
                self.run_scan(p, keep, mix)
                each(0, geo.rows, lambda r, p=p: pl.when(r != self.row)(lambda: self.c_copy(p, self.spot, r).start()))
                self.crecv[p * geo.half + self.spot] = self.csend[p, self.row]

    def main_rows(self):
        geo = self.geo
        for level in range(geo.levels):
            sums = [jnp.zeros((geo.lines, LANES), F32) for s in range(2)]
            for wide in range(geo.wide):
                value = dot3(
                    self.ph[level, : geo.lines, :], self.plo[level, : geo.lines, :],
                    joined(self.dh, level, 2 * wide, 2 * wide + 2), joined(self.dl, level, 2 * wide, 2 * wide + 2),
                )
                for k in range(BLOCK // LANES):
                    at = wide * BLOCK + k * LANES
                    piece = value[:, k * LANES : (k + 1) * LANES]
                    h, w = split(piece)
                    self.dh[level, 2 * wide + k] = h
                    self.dl[level, 2 * wide + k] = w
                    sums = [sums[s] + piece * self.cols[level, s : s + 1, at : at + LANES] for s in range(2)]
            for s in range(2):
                total = jnp.sum(sums[s], axis=1, keepdims=True)
                self.esend[level, s] = jnp.broadcast_to(total, (geo.lines, LANES))

    def e_copy(self):
        return remote(self.esend, self.erecv, self.e_s, self.e_r, {"col": self.other})

    def main_cols(self, chosen):
        geo = self.geo
        tx = geo.tx
        for level in chosen:
            for wide in range(geo.wide):
                if self.reverse:
                    cut, strip = (2 * wide, geo.blocks), slice(0, tx - BLOCK * wide)
                else:
                    cut, strip = (0, 2 * wide + 2), slice(tx - BLOCK * (wide + 1), tx)
                self.field[level, :, wide * BLOCK : (wide + 1) * BLOCK] = dot3(
                    joined(self.dh, level, *cut), joined(self.dl, level, *cut),
                    joined(self.sh, level, 0, 2, strip), joined(self.sl, level, 0, 2, strip),
                )

    def inner(self, level, i, at):
        cut = slice(i * self.geo.ty, (i + 1) * self.geo.ty)
        q = self.cols[level, 2:3, at] * self.enters
        w = self.cols[level, 3:4, at] * self.enters
        return self.field[level, cut, at] + self.erecv[level, 0, cut] * q + self.erecv[level, 1, cut] * w

    def take(self):
        geo = self.geo

        def wait(count):
            some, part = self.crecv.at[0:count], self.bsend.at[0:count]
            self.whole(part, some, self.b_s, self.c_r).wait_recv()
            self.whole(part, some, self.b_s, self.c_r).wait_send()

        pl.when(self.scans)(lambda: wait(geo.chunks - geo.per))
        pl.when(lax.rem(self.row, 2) != self.col)(lambda: wait(geo.chunks))
        self.give_copy(self.row).wait_recv()
        ends = [self.crecv[self.ends, s] * self.enters for s in range(2)]
        return [
            [[jnp.broadcast_to(ends[s][:, 2 * level + e : 2 * level + e + 1], (geo.m, LANES)) for e in range(2)] for s in range(2)]
            for level in range(geo.levels)
        ]

    def entering(self, ends, level, k):
        at = slice(k * LANES, (k + 1) * LANES)
        q, w = self.cols[level, 2:3, at], self.cols[level, 3:4, at]
        return [
            self.crecv[level * self.geo.blocks + k, s] + ends[level][s][0] * q + ends[level][s][1] * w for s in range(2)
        ]

    def sent(self):
        geo = self.geo
        pl.when(self.row != self.end_scan)(lambda: self.end_copy(self.row).wait_send())

        @pl.when(self.row == self.end_scan)
        def _():
            sent = self.csend.at[0]
            self.whole(sent, sent, self.c_s, self.d_r).wait_send()

        @pl.when(self.scans)
        def _():
            sent = self.csend.at[:, 0 : geo.rows - 1]
            self.whole(sent, sent, self.c_s, self.c_r).wait_send()


def stencil_rows(data, ty):
    y0, fy, fz = data[0:1], data[2:3], data[4:5]
    place = lax.broadcasted_iota(jnp.int32, (ty, CAP), 0).astype(F32)
    weight = jnp.where(place == y0, 1.0 - fy, jnp.where(place == y0 + 1.0, fy, 0.0))
    return jnp.concatenate([weight * (1.0 - fz), weight * fz], axis=0)


def kernel(geo, *refs):
    sources, (out, out_dep) = refs[:12], refs[12:14]
    refs = refs[14:]
    held, in_sem = refs[:12], refs[12]
    control, members, mats, tabs, rowts, corner, count, off_y, off_x, off_z, innov, prec = held
    refs = refs[10:]
    work, comms = refs[3:8], (refs[8:25], refs[25:42])
    (payload, arrived, back, returned, obs_s, obs_r, dep_s, dep_r, own, got, total, got2, own_s, own_r, tot_s, tot_r,
     select, parts, even, odd, spread) = refs[42:]
    m, levels, ty, tx, rows = geo.m, geo.levels, geo.ty, geo.tx, geo.rows
    cells = levels * ty
    wides, per_wide = geo.wide, BLOCK // LANES
    row, col, mem = lax.axis_index("row"), lax.axis_index("col"), lax.axis_index("mem")
    tiles = rows * 2
    me = row * 2 + col
    partner = {"mem": 1 - mem}
    dh, dl, bcat, bout, field = work
    peers = Peers(geo, row, col)

    loads = [pltpu.make_async_copy(a, b, in_sem.at[i]) for i, (a, b) in enumerate(zip(sources, held))]
    for load in loads:
        load.start()

    barrier = pltpu.get_barrier_semaphore()
    for k in peers.order:
        pl.semaphore_signal(barrier, inc=1, device_id=peers.device(k), device_id_type=MESH)
    pl.semaphore_signal(barrier, inc=1, device_id=partner, device_id_type=MESH)

    place = (row, col)
    ahead = Filter(geo, False, (mats.at[0], mats.at[1], tabs.at[0], rowts.at[0]), comms[0], work, place)
    behind = Filter(geo, True, (mats.at[2], mats.at[3], tabs.at[1], rowts.at[1]), comms[1], work, place)
    rowt0, rowt1 = rowts.at[0], rowts.at[1]

    make_strips(geo, False, ahead.sh, ahead.sl)
    for load in loads:
        load.wait()
    for level in range(levels):
        for i in range(m):
            cut = slice(i * ty, (i + 1) * ty)
            for k in range(geo.blocks):
                h, w = split(control[i, level, :, k * LANES : (k + 1) * LANES])
                dh[level, k, cut, :] = h
                dl[level, k, cut, :] = w
    totals = ahead.edge_start()
    for wide in range(wides):
        ahead.edge(wide, totals)
    ahead.edge_along_x(totals)

    pl.semaphore_wait(barrier, tiles)
    ahead.gather_start()

    corners = corner[...]
    row_in = lax.shift_right_logical(corners, int(tx).bit_length() - 1)
    payload[:, 0, :] = row_in.astype(F32)
    payload[:, 1, :] = (corners - row_in * tx).astype(F32)
    payload[:, 2, :] = off_y[...]
    payload[:, 3, :] = off_x[...]
    payload[:, 4, :] = off_z[...]
    payload[:, 5, :] = innov[...]
    down = lax.broadcasted_iota(jnp.int32, (tiles, tiles), 0)
    across = lax.broadcasted_iota(jnp.int32, (tiles, tiles), 1)
    used = jnp.sum(jnp.where(down == across, count[...].astype(F32), 0.0), axis=1, keepdims=True)
    slot = lax.broadcasted_iota(jnp.int32, (tiles, CAP), 1).astype(F32)
    payload[:, 6, :] = jnp.where(slot < used, prec[...], 0.0)
    payload[:, 7, :] = jnp.zeros((tiles, CAP), F32)

    def obs_copy(k, to, slot):
        return remote(payload.at[to], arrived.at[slot], obs_s, obs_r, peers.device(k))

    def dep_copy(k, to, slot):
        return remote(back.at[to], returned.at[slot], dep_s, dep_r, peers.device(k))

    for k in peers.order:
        obs_copy(k, peers.index(k), me).start()
    arrived[me] = payload[me]

    ahead.main_rows()
    ahead.e_copy().start()
    ahead.main_cols(range(0, levels - 1))
    ahead.scan()
    ahead.main_cols(range(levels - 1, levels))

    make_strips(geo, True, behind.sh, behind.sl)
    ahead.e_copy().wait()
    for wide in range(wides):
        for k in range(per_wide):
            at = slice(wide * BLOCK + k * LANES, wide * BLOCK + (k + 1) * LANES)
            for level in range(levels):
                value = members[0, level, :, at].astype(F32) * ahead.inner(level, 0, at)
                for i in range(1, m):
                    value = value + members[i, level, :, at].astype(F32) * ahead.inner(level, i, at)
                own[wide, level * ty : (level + 1) * ty, k * LANES : (k + 1) * LANES] = value

    others = pl.ds(0, tiles - 1)
    every = remote(payload.at[others], arrived.at[others], obs_s, obs_r, partner)
    every.wait_send()
    every.wait_recv()

    iota = lax.broadcasted_iota(jnp.int32, (LANES, CAP), 0).astype(F32)
    packed = 16

    def choose(s):
        x0 = arrived[s, 1:2, :]
        block = jnp.floor(x0 * (1.0 / LANES))
        inside = jnp.where(iota == x0 - block * LANES, 1.0, 0.0).astype(BF16)
        block = jnp.broadcast_to(block, (packed, CAP))
        for h in range(tx // LANES):
            there = jnp.where(block == float(h), 1.0, 0.0).astype(BF16)
            for g in range(0, LANES, packed):
                first = h * LANES + g
                select[s, first : first + packed, :] = inside[g : g + packed] * there

    each(0, tiles, choose)

    ends = ahead.take()

    def own_copy(wide):
        return remote(own.at[wide], got.at[wide], own_s.at[wide], own_r.at[wide], partner)

    for wide in reversed(range(wides)):
        for k in range(per_wide):
            block = wide * per_wide + k
            at = slice(block * LANES, (block + 1) * LANES)
            here = slice(k * LANES, (k + 1) * LANES)
            for level in range(levels):
                s1, s2 = ahead.entering(ends, level, block)
                value = own[wide, level * ty : (level + 1) * ty, here]
                for i in range(m):
                    value = value + members[i, level, :, at].astype(F32) * (
                        rowt0[level, 0] * s1[i : i + 1, :] + rowt0[level, 1] * s2[i : i + 1, :]
                    )
                own[wide, level * ty : (level + 1) * ty, here] = value * scale_of(geo)
        own_copy(wide).start()

    lane = lax.broadcasted_iota(jnp.int32, (cells, BLOCK), 1)
    first_of_right = jnp.zeros((cells, 1), F32)
    for wide in reversed(range(wides)):
        own_copy(wide).wait_recv()
        value = own[wide] + got[wide]
        moved = jnp.where(lane == BLOCK - 1, first_of_right, pltpu.roll(value, BLOCK - 1, 1))
        first_of_right = value[:, 0:1]
        h, w = split(value)
        parts[0:cells, wide * BLOCK : (wide + 1) * BLOCK] = h
        parts[cells : 2 * cells, wide * BLOCK : (wide + 1) * BLOCK] = w
        h, w = split(moved)
        parts[2 * cells : 3 * cells, wide * BLOCK : (wide + 1) * BLOCK] = h
        parts[3 * cells :, wide * BLOCK : (wide + 1) * BLOCK] = w

    size = 4 if tiles >= 8 else 2
    groups = tiles // size

    def fetch(group, buffer):
        columns = jnp.concatenate([select[group * size + i] for i in range(size)], axis=1)
        buffer[...] = dot(parts[...], columns)

    def use(group, buffer):
        for i in range(size):
            s = group * size + i
            data = arrived[s]
            cut = slice(i * CAP, (i + 1) * CAP)
            fx = data[3:4]
            left = buffer[0:cells, cut] + buffer[cells : 2 * cells, cut]
            right = buffer[2 * cells : 3 * cells, cut] + buffer[3 * cells :, cut]
            weight = stencil_rows(data, ty)
            image = jnp.sum(weight * (left + fx * (right - left)), axis=0, keepdims=True)
            departure = data[6:7] * (image - data[5:6])
            back[s] = jnp.broadcast_to(departure, (8, CAP))
            weight = weight * (departure * scale_of(geo))
            far = weight * fx
            h, w = split(weight - far)
            spread[s, 0:cells] = h
            spread[s, cells : 2 * cells] = w
            h, w = split(far)
            spread[s, 2 * cells : 3 * cells] = h
            spread[s, 3 * cells :] = w

    fetch(0, even)

    def interpolate(t):
        fetch(2 * t + 1, odd)
        use(2 * t, even)
        fetch(jnp.minimum(2 * t + 2, groups - 1), even)
        use(2 * t + 1, odd)

    each(0, groups // 2, interpolate)

    def tot_copy(wide):
        return remote(total.at[wide], got2.at[wide], tot_s.at[wide], tot_r.at[wide], partner)

    lane = lax.broadcasted_iota(jnp.int32, (cells, LANES), 1)
    last = jnp.zeros((cells, LANES), F32)
    for wide in range(wides):
        piece = lax.dot_general(
            jnp.concatenate([select[s, wide * BLOCK : (wide + 1) * BLOCK, :] for s in range(tiles)], axis=1),
            jnp.concatenate([spread[s] for s in range(tiles)], axis=1),
            (((1,), (1,)), ((), ())),
            preferred_element_type=F32,
        )
        piece = piece.T
        for k in range(per_wide):
            cut = slice(k * LANES, (k + 1) * LANES)
            here = piece[0:cells, cut] + piece[cells : 2 * cells, cut]
            moved = pltpu.roll(piece[2 * cells : 3 * cells, cut] + piece[3 * cells :, cut], 1, 1)
            total[wide, :, cut] = here + jnp.where(lane == 0, last, moved)
            last = moved
        tot_copy(wide).start()

    totals = behind.edge_start()
    for wide in range(wides):
        tot_copy(wide).wait_recv()
        for level in range(levels):
            part = slice(level * ty, (level + 1) * ty)
            for k in range(per_wide):
                block = wide * per_wide + k
                here = slice(k * LANES, (k + 1) * LANES)
                forcing = total[wide, part, here] + got2[wide, part, here]
                for i in range(m):
                    h, w = split(members[i, level, :, block * LANES : (block + 1) * LANES].astype(F32) * forcing)
                    dh[level, block, i * ty : (i + 1) * ty, :] = h
                    dl[level, block, i * ty : (i + 1) * ty, :] = w
        behind.edge(wide, totals)
    behind.edge_along_x(totals)
    behind.gather_start()
    for k in peers.order:
        dep_copy(k, peers.index(k), me).start()
    returned[me] = back[me]
    behind.main_rows()
    behind.e_copy().start()
    behind.main_cols(range(0, levels - 1))
    behind.scan()
    behind.main_cols(range(levels - 1, levels))
    behind.e_copy().wait()
    for level in range(levels):
        def finish(k, level=level):
            at = lanes(k * LANES)
            for i in range(m):
                out[i, level, :, at] = control[i, level, :, at] + behind.inner(level, i, at)

        each(0, geo.blocks, finish)

    every = remote(back.at[others], returned.at[others], dep_s, dep_r, partner)
    every.wait_send()
    every.wait_recv()
    for t in range(tiles):
        out_dep[0:1, t * CAP : (t + 1) * CAP] = returned[t, 0:1, :]
    ahead.sent()
    for wide in range(wides):
        own_copy(wide).wait_send()
        tot_copy(wide).wait_send()
    ends = behind.take()
    for k in range(geo.blocks):
        at = slice(k * LANES, (k + 1) * LANES)
        for level in range(levels):
            s1, s2 = behind.entering(ends, level, k)
            for i in range(m):
                out[i, level, :, at] += rowt1[level, 0] * s1[i : i + 1, :] + rowt1[level, 1] * s2[i : i + 1, :]
    behind.sent()


def body(control, members, obs_corner, obs_count, offset_y, offset_x, offset_z, innovation, precision):
    m, levels, ty, tx = control.shape
    rows = lax.axis_size("row")
    tiles = rows * lax.axis_size("col")
    geo = Geometry(m, levels, ty, tx, rows)
    cells = levels * ty
    size = 4 if tiles >= 8 else 2

    def by_tile(array):
        return array.reshape(tiles, CAP)

    mats = np.stack([a for reverse in (False, True) for a in geo.row_matrix(reverse)])
    tabs = np.stack([geo.col_tables(reverse) for reverse in (False, True)])
    rowts = np.stack([geo.row_tables(reverse) for reverse in (False, True)])
    operands = [control, members, jnp.asarray(mats), jnp.asarray(tabs), jnp.asarray(rowts), by_tile(obs_corner), obs_count]
    operands += [by_tile(a) for a in (offset_y, offset_x, offset_z, innovation, precision)]
    dma = pltpu.SemaphoreType.DMA
    chunks, per, lines = geo.chunks, geo.per, geo.lines
    comm = [
        pltpu.VMEM((levels, 2, lines, LANES), F32),
        pltpu.VMEM((levels, 2, lines, LANES), F32),
        pltpu.VMEM((chunks + 1, 2, m, LANES), F32),
        pltpu.VMEM((per, rows, 2, m, LANES), F32),
        pltpu.VMEM((per, rows, 2, m, LANES), F32),
        pltpu.VMEM((chunks + 1, 2, m, LANES), F32),
        pltpu.VMEM((8, LANES), F32),
        pltpu.VMEM((levels, BLOCK // LANES, tx, LANES), BF16),
        pltpu.VMEM((levels, BLOCK // LANES, tx, LANES), BF16),
        dma,
        dma,
        dma,
        dma,
        dma,
        dma,
        dma,
        dma,
    ]
    scratch = [
        *[pltpu.VMEM(a.shape, a.dtype) for a in operands],
        dma((len(operands),)),
        pltpu.VMEM((levels, geo.blocks, lines, LANES), BF16),
        pltpu.VMEM((levels, geo.blocks, lines, LANES), BF16),
        pltpu.VMEM((levels, geo.wide * 4 * m, BLOCK), BF16),
        pltpu.VMEM((8, LANES), F32),
        pltpu.VMEM((levels, lines, tx), F32),
    ]
    scratch += comm + comm
    wide_shape = (geo.wide, cells, BLOCK)
    scratch += [
        pltpu.VMEM((tiles, 8, CAP), F32),
        pltpu.VMEM((tiles, 8, CAP), F32),
        pltpu.VMEM((tiles, 8, CAP), F32),
        pltpu.VMEM((tiles, 8, CAP), F32),
        dma,
        dma,
        dma,
        dma,
        pltpu.VMEM(wide_shape, F32),
        pltpu.VMEM(wide_shape, F32),
        pltpu.VMEM(wide_shape, F32),
        pltpu.VMEM(wide_shape, F32),
        dma((geo.wide,)),
        dma((geo.wide,)),
        dma((geo.wide,)),
        dma((geo.wide,)),
        pltpu.VMEM((tiles, tx, CAP), BF16),
        pltpu.VMEM((4 * cells, tx), BF16),
        pltpu.VMEM((4 * cells, size * CAP), F32),
        pltpu.VMEM((4 * cells, size * CAP), F32),
        pltpu.VMEM((tiles, 4 * cells, CAP), BF16),
    ]
    hbm = pl.BlockSpec(memory_space=pl.ANY)
    return pl.pallas_call(
        functools.partial(kernel, geo),
        out_shape=(pltpu.VMEM(control.shape, F32), pltpu.VMEM((1, tiles * CAP), F32)),
        in_specs=[hbm] * len(operands),
        out_specs=(VMEM, VMEM),
        scratch_shapes=scratch,
        compiler_params=pltpu.CompilerParams(collective_id=0, has_side_effects=True, vmem_limit_bytes=58 * 1024 * 1024),
        name="gradient",
    )(*operands)


def solution(mesh):
    return jax.shard_map(
        body,
        mesh=mesh,
        in_specs=(
            P("mem", None, "row", "col"),
            P("mem", None, "row", "col"),
            P(("mem", "row", "col"), None),
            P(("mem", "row", "col"), None),
            P(("mem", "row", "col"), None),
            P(("mem", "row", "col"), None),
            P(("mem", "row", "col"), None),
            P(("mem", "row", "col"), None),
            P(("mem", "row", "col"), None),
        ),
        out_specs=(P("mem", None, "row", "col"), P(("mem", "row", "col"), None)),
        check_vma=False,
    )
```

```python
import functools

import jax
import jax.numpy as jnp
import numpy as np
from jax import lax
from jax.experimental import pallas as pl
from jax.experimental.pallas import tpu as pltpu
from jax.sharding import PartitionSpec as P

CAP = 128
LANES = 128
BLOCK = 256
F32 = jnp.float32
BF16 = jnp.bfloat16
MESH = pl.DeviceIdType.MESH
VMEM = pl.BlockSpec(memory_space=pltpu.VMEM)


def filter_rates(length):
    one = np.float32(1.0)
    decay = np.exp(-one / np.float32(length), dtype=np.float32)
    square = np.float32(decay * decay)
    weight = np.power(np.power(one - square, np.float32(3.0)) / (one + square), np.float32(0.25))
    return float(decay), float(weight)


def halves(array):
    high = array.astype(jnp.bfloat16)
    low = (array - high.astype(np.float32)).astype(jnp.bfloat16)
    return high, low


class Geometry:
    def __init__(self, members, levels, ty, tx, rows):
        self.m, self.levels, self.ty, self.tx, self.rows = members, levels, ty, tx, rows
        self.lines = members * ty
        self.blocks = tx // LANES
        self.wide = tx // BLOCK
        self.chunks = levels * self.blocks
        self.half = rows // 2
        self.per = self.chunks // self.half
        self.x_rates = [filter_rates(tx / 16.0), filter_rates(tx / 64.0)]
        self.y_rates = [filter_rates(rows * ty / 2.0), filter_rates(ty / 2.0)]

    def row_matrix(self, reverse):
        m, ty = self.m, self.ty
        result = []
        for a, b in self.y_rates:
            place = np.arange(ty)
            gap = place[:, None] - place[None, :]
            local = np.where(gap >= 0, b * b * (gap + 1.0) * a ** np.maximum(gap, 0), 0.0)
            edge = np.stack([b * a ** (ty - 1.0 - place), b * b * (ty - place) * a ** (ty - 1.0 - place)])
            if reverse:
                local, edge = local.T, edge[:, ::-1]
            main = np.kron(np.eye(m), local)
            ends = np.concatenate([np.kron(np.eye(m), edge[s : s + 1]) for s in range(2)])
            result.append(np.concatenate([main, ends]))
        return halves(np.stack(result).astype(np.float32))

    def col_tables(self, reverse):
        tx = self.tx
        result = []
        for a, b in self.x_rates:
            place = np.arange(tx)
            ends = [b * a ** (tx - 1.0 - place), b * b * (tx - place) * a ** (tx - 1.0 - place)]
            enter = [b * (place + 1.0) * a ** (place + 1.0), a ** (place + 1.0)]
            table = np.stack(ends + enter)
            result.append(table[:, ::-1] if reverse else table)
        return np.stack(result).astype(np.float32)

    def row_tables(self, reverse):
        result = []
        for a, b in self.y_rates:
            place = np.arange(self.ty)
            table = np.stack([b * (place + 1.0) * a ** (place + 1.0), a ** (place + 1.0)])
            table = table[:, ::-1] if reverse else table
            result.append(np.broadcast_to(table[:, :, None], (2, self.ty, LANES)))
        return np.stack(result).astype(np.float32)

    def row_step(self):
        return [(a**self.ty, b * self.ty * a**self.ty) for a, b in self.y_rates]


def split(value):
    high = value.astype(BF16)
    return high, (value - high.astype(F32)).astype(BF16)


def dot(a, b):
    return jnp.dot(a, b, preferred_element_type=F32)


def dot3(ah, al, bh, bl):
    return dot(ah, bh) + dot(al, bh) + dot(ah, bl)


def each(low, high, action, unroll=1):
    def one(i, carry):
        action(i)
        return carry

    lax.fori_loop(low, high, one, 0, unroll=unroll)


def lanes(start, size=LANES):
    return pl.ds(pl.multiple_of(start, LANES), size)


def remote(src, dst, send, recv, device):
    return pltpu.make_async_remote_copy(
        src_ref=src, dst_ref=dst, send_sem=send, recv_sem=recv, device_id=device, device_id_type=MESH
    )


def scale_of(geo):
    return float(geo.m * 2) ** -0.5


def joined(ref, index, first, last, rows=slice(None)):
    return jnp.concatenate([ref[index, k, rows, :] for k in range(first, last)], axis=1)


def make_strips(geo, reverse, high, low):
    step = LANES
    tx = geo.tx
    down = lax.broadcasted_iota(jnp.int32, (step, LANES), 0).astype(F32)
    across = lax.broadcasted_iota(jnp.int32, (step, LANES), 1).astype(F32)
    lane = lax.broadcasted_iota(jnp.int32, (1, LANES), 1).astype(F32)
    slope = down - across if reverse else across - down
    for level, (a, b) in enumerate(geo.x_rates):
        rate = float(np.log(a))
        power = jnp.exp(down * (rate if reverse else -rate))
        for index in range(tx // step):
            for half in range(BLOCK // LANES):
                first = index * step
                if reverse:
                    shift = first - half * LANES
                    line = (b * b) * jnp.exp((shift - lane) * rate)
                else:
                    shift = tx - BLOCK - first + half * LANES
                    line = (b * b) * jnp.exp((shift + lane) * rate)
                if shift <= -LANES:
                    value = jnp.zeros((step, LANES), F32)
                else:
                    value = (slope + (shift + 1.0)) * (power * line)
                    if shift < LANES:
                        value = jnp.where(slope >= -float(shift), value, 0.0)
                h, w = split(value)
                high[level, half, first : first + step, :] = h
                low[level, half, first : first + step, :] = w


class Peers:
    def __init__(self, geo, row, col):
        bits = geo.rows.bit_length() - 1
        flips = [(1 - 2 * lax.rem(row // 2**i, 2)) * 2**i for i in range(bits)]
        self.row_at = [row]
        for i in range(bits):
            self.row_at += [r + flips[i] for r in self.row_at]
        self.col_at = [col, 1 - col]
        ring = (0, 1, 2, 1)
        hops = lambda k: 2 * ((k >> 1) & 1) + ring[(k >> 2) & 3] + ring[(k >> 4) & 3]
        self.order = sorted(range(1, 2 * geo.rows), key=lambda k: -hops(k))
        self.rows_order = sorted(range(1, geo.rows), key=lambda k: -hops(2 * k))
        self.scan_order = sorted(range(1, geo.half), key=lambda k: -hops(4 * k))

    def device(self, k):
        return {"row": self.row_at[k >> 1], "col": self.col_at[k & 1]}

    def index(self, k):
        return self.row_at[k >> 1] * 2 + self.col_at[k & 1]


class Filter:
    def __init__(self, geo, reverse, consts, comm, work, place, peers):
        self.geo, self.reverse, self.peers = geo, reverse, peers
        self.ph, self.plo, self.cols, self.rowt = consts
        (self.esend, self.erecv, self.bsend, self.brecv, self.csend, self.crecv, self.dsend, self.sh, self.sl,
         self.e_s, self.e_r, self.b_s, self.b_r, self.c_s, self.c_r, self.d_s, self.d_r) = comm
        self.dh, self.dl, self.bcat, self.bout, self.field = work
        self.row, self.col = place
        self.other = 1 - self.col
        self.enters = jnp.where(self.col == (0 if reverse else 1), 1.0, 0.0).astype(F32)
        self.scans = lax.rem(self.row, 2) == self.col
        self.spot = self.row // 2
        self.end_scan = 1 - self.col
        self.ends = geo.chunks

    def edge(self, wide, totals):
        geo = self.geo
        for level in range(geo.levels):
            value = dot3(
                self.ph[level, geo.lines :, :], self.plo[level, geo.lines :, :],
                joined(self.dh, level, 2 * wide, 2 * wide + 2), joined(self.dl, level, 2 * wide, 2 * wide + 2),
            )
            h, w = split(value)
            base = wide * 4 * geo.m
            self.bcat[level, base : base + 2 * geo.m, :] = h
            self.bcat[level, base + 2 * geo.m : base + 4 * geo.m, :] = w
            for s in range(2):
                for k in range(BLOCK // LANES):
                    at = wide * BLOCK + k * LANES
                    totals[level][s] += value[:, k * LANES : (k + 1) * LANES] * self.cols[level, s : s + 1, at : at + LANES]

    def edge_start(self):
        geo = self.geo
        return [[jnp.zeros((2 * geo.m, LANES), F32) for s in range(2)] for level in range(geo.levels)]

    def edge_along_x(self, totals):
        geo = self.geo
        m, size = geo.m, 4 * geo.m
        lane = lax.broadcasted_iota(jnp.int32, (2 * m, LANES), 1)
        ends = jnp.zeros((2 * m, LANES), F32)
        for level in range(geo.levels):
            for s in range(2):
                total = jnp.sum(totals[level][s], axis=1, keepdims=True)
                ends = jnp.where(lane == 2 * level + s, total, ends)
        self.bsend[self.ends, 0] = ends[:m]
        self.bsend[self.ends, 1] = ends[m:]
        for level in range(geo.levels):
            sums = [None] * geo.wide
            for gap in range(geo.wide):
                count = geo.wide - gap
                if self.reverse:
                    rows = slice(gap * size, geo.wide * size)
                    strip = slice(gap * BLOCK, (gap + 1) * BLOCK)
                else:
                    rows = slice(0, count * size)
                    strip = slice((count - 1) * BLOCK, count * BLOCK)
                left = self.bcat[level, rows, :]
                value = dot(left, joined(self.sh, level, 0, 2, strip)) + dot(left, joined(self.sl, level, 0, 2, strip))
                for i in range(count):
                    to = i if self.reverse else i + gap
                    term = value[i * size : i * size + 2 * m] + value[i * size + 2 * m : (i + 1) * size]
                    sums[to] = term if sums[to] is None else sums[to] + term
            for wide in range(geo.wide):
                for k in range(BLOCK // LANES):
                    piece = sums[wide][:, k * LANES : (k + 1) * LANES]
                    chunk = level * geo.blocks + wide * (BLOCK // LANES) + k
                    self.bsend[chunk, 0] = piece[:m]
                    self.bsend[chunk, 1] = piece[m:]

    def row_of(self, i):
        return 2 * i + self.col

    def b_copy(self, p, i, source):
        half = self.geo.half
        return remote(
            self.bsend.at[p * half + i], self.brecv.at[p, source], self.b_s, self.b_r, {"row": self.row_of(i)}
        )

    def c_copy(self, p, i, target):
        half = self.geo.half
        return remote(
            self.csend.at[p, target], self.crecv.at[p * half + i], self.c_s, self.c_r, {"row": target}
        )

    def end_copy(self, source):
        return remote(
            self.bsend.at[self.ends], self.brecv.at[0, source], self.d_s, self.b_r, {"row": self.end_scan}
        )

    def give_copy(self, target):
        return remote(
            self.csend.at[0, target], self.crecv.at[self.ends], self.c_s, self.d_r,
            {"row": target, "col": self.other},
        )

    def whole(self, src, dst, send, recv):
        return remote(src, dst, send, recv, {"col": self.other})

    def gather_start(self):
        geo = self.geo
        pl.when(self.row != self.end_scan)(lambda: self.end_copy(self.row).start())
        for p in range(geo.per):
            for k in self.peers.scan_order:
                self.b_copy(p, self.peers.row_at[2 * k] // 2, self.row).start()
            pl.when(lax.rem(self.row, 2) != self.col)(lambda p=p: self.b_copy(p, self.spot, self.row).start())

        @pl.when(self.row == self.end_scan)
        def _():
            self.brecv[0, self.row] = self.bsend[self.ends]

        @pl.when(self.scans)
        def _():
            for p in range(geo.per):
                self.brecv[p, self.row] = self.bsend[p * geo.half + self.spot]

    def run_scan(self, p, keep, mix):
        geo = self.geo

        def advance(lap, state):
            s1, s2 = state
            r = geo.rows - 1 - lap if self.reverse else lap
            self.csend[p, r, 0] = s1
            self.csend[p, r, 1] = s2
            return keep * s1 + self.brecv[p, r, 0], keep * s2 + mix * s1 + self.brecv[p, r, 1]

        zero = jnp.zeros((geo.m, LANES), F32)
        lax.fori_loop(0, geo.rows, advance, (zero, zero), unroll=4 if geo.rows % 4 == 0 else 1)

    def scan(self):
        geo = self.geo
        steps = geo.row_step()

        @pl.when(self.row == self.end_scan)
        def _():
            got = self.brecv.at[0, 0 : geo.rows - 1]
            self.whole(got, got, self.d_s, self.b_r).wait_recv()
            lane = lax.broadcasted_iota(jnp.int32, (geo.m, LANES), 1)
            keep = jnp.where(lane < 2, steps[0][0], steps[1][0]).astype(F32)
            mix = jnp.where(lane < 2, steps[0][1], steps[1][1]).astype(F32)
            self.run_scan(0, keep, mix)
            for k in self.peers.rows_order + [0]:
                self.give_copy(self.peers.row_at[k]).start()

        @pl.when(self.scans)
        def _():
            got = self.brecv.at[:, 0 : geo.rows - 1]
            self.whole(got, got, self.b_s, self.b_r).wait_recv()
            for p in range(geo.per):
                first = p * geo.half + self.spot < geo.blocks
                keep = jnp.where(first, steps[0][0], steps[1][0]).astype(F32)
                mix = jnp.where(first, steps[0][1], steps[1][1]).astype(F32)
                self.run_scan(p, keep, mix)
                for k in self.peers.rows_order:
                    self.c_copy(p, self.spot, self.peers.row_at[k]).start()
                self.crecv[p * geo.half + self.spot] = self.csend[p, self.row]

    def main_rows(self):
        geo = self.geo
        for level in range(geo.levels):
            sums = [jnp.zeros((geo.lines, LANES), F32) for s in range(2)]
            for wide in range(geo.wide):
                value = dot3(
                    self.ph[level, : geo.lines, :], self.plo[level, : geo.lines, :],
                    joined(self.dh, level, 2 * wide, 2 * wide + 2), joined(self.dl, level, 2 * wide, 2 * wide + 2),
                )
                for k in range(BLOCK // LANES):
                    at = wide * BLOCK + k * LANES
                    piece = value[:, k * LANES : (k + 1) * LANES]
                    h, w = split(piece)
                    self.dh[level, 2 * wide + k] = h
                    self.dl[level, 2 * wide + k] = w
                    sums = [sums[s] + piece * self.cols[level, s : s + 1, at : at + LANES] for s in range(2)]
            for s in range(2):
                total = jnp.sum(sums[s], axis=1, keepdims=True)
                self.esend[level, s] = jnp.broadcast_to(total, (geo.lines, LANES))

    def e_copy(self):
        return remote(self.esend, self.erecv, self.e_s, self.e_r, {"col": self.other})

    def main_cols(self, chosen):
        geo = self.geo
        tx = geo.tx
        for level in chosen:
            for wide in range(geo.wide):
                if self.reverse:
                    cut, strip = (2 * wide, geo.blocks), slice(0, tx - BLOCK * wide)
                else:
                    cut, strip = (0, 2 * wide + 2), slice(tx - BLOCK * (wide + 1), tx)
                self.field[level, :, wide * BLOCK : (wide + 1) * BLOCK] = dot3(
                    joined(self.dh, level, *cut), joined(self.dl, level, *cut),
                    joined(self.sh, level, 0, 2, strip), joined(self.sl, level, 0, 2, strip),
                )

    def inner(self, level, i, at):
        cut = slice(i * self.geo.ty, (i + 1) * self.geo.ty)
        q = self.cols[level, 2:3, at] * self.enters
        w = self.cols[level, 3:4, at] * self.enters
        return self.field[level, cut, at] + self.erecv[level, 0, cut] * q + self.erecv[level, 1, cut] * w

    def take(self):
        geo = self.geo

        def wait(count):
            some, part = self.crecv.at[0:count], self.bsend.at[0:count]
            self.whole(part, some, self.b_s, self.c_r).wait_recv()
            self.whole(part, some, self.b_s, self.c_r).wait_send()

        pl.when(self.scans)(lambda: wait(geo.chunks - geo.per))
        pl.when(lax.rem(self.row, 2) != self.col)(lambda: wait(geo.chunks))
        self.give_copy(self.row).wait_recv()
        ends = [self.crecv[self.ends, s] * self.enters for s in range(2)]
        return [
            [[jnp.broadcast_to(ends[s][:, 2 * level + e : 2 * level + e + 1], (geo.m, LANES)) for e in range(2)] for s in range(2)]
            for level in range(geo.levels)
        ]

    def entering(self, ends, level, k):
        at = slice(k * LANES, (k + 1) * LANES)
        q, w = self.cols[level, 2:3, at], self.cols[level, 3:4, at]
        return [
            self.crecv[level * self.geo.blocks + k, s] + ends[level][s][0] * q + ends[level][s][1] * w for s in range(2)
        ]

    def sent(self):
        geo = self.geo
        pl.when(self.row != self.end_scan)(lambda: self.end_copy(self.row).wait_send())

        @pl.when(self.row == self.end_scan)
        def _():
            sent = self.csend.at[0]
            self.whole(sent, sent, self.c_s, self.d_r).wait_send()

        @pl.when(self.scans)
        def _():
            sent = self.csend.at[:, 0 : geo.rows - 1]
            self.whole(sent, sent, self.c_s, self.c_r).wait_send()


def stencil_rows(data, ty):
    y0, fy, fz = data[0:1], data[2:3], data[4:5]
    place = lax.broadcasted_iota(jnp.int32, (ty, CAP), 0).astype(F32)
    weight = jnp.where(place == y0, 1.0 - fy, jnp.where(place == y0 + 1.0, fy, 0.0))
    return jnp.concatenate([weight * (1.0 - fz), weight * fz], axis=0)


def kernel(geo, *refs):
    sources, (out, out_dep) = refs[:12], refs[12:14]
    refs = refs[14:]
    held, in_sem = refs[:12], refs[12]
    control, members, mats, tabs, rowts, corner, count, off_y, off_x, off_z, innov, prec = held
    refs = refs[10:]
    work, comms = refs[3:8], (refs[8:25], refs[25:42])
    (payload, arrived, back, returned, obs_s, obs_r, dep_s, dep_r, own, got, total, got2, own_s, own_r, tot_s, tot_r,
     select, parts, even, odd, spread) = refs[42:]
    m, levels, ty, tx, rows = geo.m, geo.levels, geo.ty, geo.tx, geo.rows
    cells = levels * ty
    wides, per_wide = geo.wide, BLOCK // LANES
    row, col, mem = lax.axis_index("row"), lax.axis_index("col"), lax.axis_index("mem")
    tiles = rows * 2
    me = row * 2 + col
    partner = {"mem": 1 - mem}
    dh, dl, bcat, bout, field = work
    peers = Peers(geo, row, col)

    loads = [pltpu.make_async_copy(a, b, in_sem.at[i]) for i, (a, b) in enumerate(zip(sources, held))]
    for load in loads:
        load.start()

    barrier = pltpu.get_barrier_semaphore()
    for k in peers.order:
        pl.semaphore_signal(barrier, inc=1, device_id=peers.device(k), device_id_type=MESH)
    pl.semaphore_signal(barrier, inc=1, device_id=partner, device_id_type=MESH)

    place = (row, col)
    ahead = Filter(geo, False, (mats.at[0], mats.at[1], tabs.at[0], rowts.at[0]), comms[0], work, place, peers)
    behind = Filter(geo, True, (mats.at[2], mats.at[3], tabs.at[1], rowts.at[1]), comms[1], work, place, peers)
    rowt0, rowt1 = rowts.at[0], rowts.at[1]

    make_strips(geo, False, ahead.sh, ahead.sl)
    for load in loads:
        load.wait()
    for level in range(levels):
        for i in range(m):
            cut = slice(i * ty, (i + 1) * ty)
            for k in range(geo.blocks):
                h, w = split(control[i, level, :, k * LANES : (k + 1) * LANES])
                dh[level, k, cut, :] = h
                dl[level, k, cut, :] = w
    totals = ahead.edge_start()
    for wide in range(wides):
        ahead.edge(wide, totals)
    ahead.edge_along_x(totals)

    pl.semaphore_wait(barrier, tiles)
    ahead.gather_start()

    corners = corner[...]
    row_in = lax.shift_right_logical(corners, int(tx).bit_length() - 1)
    payload[:, 0, :] = row_in.astype(F32)
    payload[:, 1, :] = (corners - row_in * tx).astype(F32)
    payload[:, 2, :] = off_y[...]
    payload[:, 3, :] = off_x[...]
    payload[:, 4, :] = off_z[...]
    payload[:, 5, :] = innov[...]
    down = lax.broadcasted_iota(jnp.int32, (tiles, tiles), 0)
    across = lax.broadcasted_iota(jnp.int32, (tiles, tiles), 1)
    used = jnp.sum(jnp.where(down == across, count[...].astype(F32), 0.0), axis=1, keepdims=True)
    slot = lax.broadcasted_iota(jnp.int32, (tiles, CAP), 1).astype(F32)
    payload[:, 6, :] = jnp.where(slot < used, prec[...], 0.0)
    payload[:, 7, :] = jnp.zeros((tiles, CAP), F32)

    def obs_copy(k, to, slot):
        return remote(payload.at[to], arrived.at[slot], obs_s, obs_r, peers.device(k))

    def dep_copy(k, to, slot):
        return remote(back.at[to], returned.at[slot], dep_s, dep_r, peers.device(k))

    for k in peers.order:
        obs_copy(k, peers.index(k), me).start()
    arrived[me] = payload[me]

    ahead.main_rows()
    ahead.e_copy().start()
    ahead.main_cols(range(0, levels - 1))
    ahead.scan()
    ahead.main_cols(range(levels - 1, levels))

    make_strips(geo, True, behind.sh, behind.sl)
    ahead.e_copy().wait()
    for wide in range(wides):
        for k in range(per_wide):
            at = slice(wide * BLOCK + k * LANES, wide * BLOCK + (k + 1) * LANES)
            for level in range(levels):
                value = members[0, level, :, at].astype(F32) * ahead.inner(level, 0, at)
                for i in range(1, m):
                    value = value + members[i, level, :, at].astype(F32) * ahead.inner(level, i, at)
                own[wide, level * ty : (level + 1) * ty, k * LANES : (k + 1) * LANES] = value

    others = pl.ds(0, tiles - 1)
    every = remote(payload.at[others], arrived.at[others], obs_s, obs_r, partner)
    every.wait_send()
    every.wait_recv()

    iota = lax.broadcasted_iota(jnp.int32, (LANES, CAP), 0).astype(F32)
    packed = 16

    def choose(s):
        x0 = arrived[s, 1:2, :]
        block = jnp.floor(x0 * (1.0 / LANES))
        inside = jnp.where(iota == x0 - block * LANES, 1.0, 0.0).astype(BF16)
        block = jnp.broadcast_to(block, (packed, CAP))
        for h in range(tx // LANES):
            there = jnp.where(block == float(h), 1.0, 0.0).astype(BF16)
            for g in range(0, LANES, packed):
                first = h * LANES + g
                select[s, first : first + packed, :] = inside[g : g + packed] * there

    early = 3 * tiles // 8
    each(0, early, choose, 2 if early % 2 == 0 else 1)

    ends = ahead.take()

    def own_copy(wide):
        return remote(own.at[wide], got.at[wide], own_s.at[wide], own_r.at[wide], partner)

    for wide in reversed(range(wides)):
        for k in range(per_wide):
            block = wide * per_wide + k
            at = slice(block * LANES, (block + 1) * LANES)
            here = slice(k * LANES, (k + 1) * LANES)
            for level in range(levels):
                s1, s2 = ahead.entering(ends, level, block)
                value = own[wide, level * ty : (level + 1) * ty, here]
                for i in range(m):
                    value = value + members[i, level, :, at].astype(F32) * (
                        rowt0[level, 0] * s1[i : i + 1, :] + rowt0[level, 1] * s2[i : i + 1, :]
                    )
                own[wide, level * ty : (level + 1) * ty, here] = value * scale_of(geo)
        own_copy(wide).start()
    each(early, tiles, choose, 2 if early % 2 == 0 else 1)

    lane = lax.broadcasted_iota(jnp.int32, (cells, BLOCK), 1)
    first_of_right = jnp.zeros((cells, 1), F32)
    for wide in reversed(range(wides)):
        own_copy(wide).wait_recv()
        value = own[wide] + got[wide]
        moved = jnp.where(lane == BLOCK - 1, first_of_right, pltpu.roll(value, BLOCK - 1, 1))
        first_of_right = value[:, 0:1]
        h, w = split(value)
        parts[0:cells, wide * BLOCK : (wide + 1) * BLOCK] = h
        parts[cells : 2 * cells, wide * BLOCK : (wide + 1) * BLOCK] = w
        h, w = split(moved)
        parts[2 * cells : 3 * cells, wide * BLOCK : (wide + 1) * BLOCK] = h
        parts[3 * cells :, wide * BLOCK : (wide + 1) * BLOCK] = w

    size = 4 if tiles >= 8 else 2
    groups = tiles // size

    def fetch(group, buffer):
        columns = jnp.concatenate([select[group * size + i] for i in range(size)], axis=1)
        buffer[...] = dot(parts[...], columns)

    def use(group, buffer):
        for i in range(size):
            s = group * size + i
            data = arrived[s]
            cut = slice(i * CAP, (i + 1) * CAP)
            fx = data[3:4]
            left = buffer[0:cells, cut] + buffer[cells : 2 * cells, cut]
            right = buffer[2 * cells : 3 * cells, cut] + buffer[3 * cells :, cut]
            weight = stencil_rows(data, ty)
            image = jnp.sum(weight * (left + fx * (right - left)), axis=0, keepdims=True)
            departure = data[6:7] * (image - data[5:6])
            back[s] = jnp.broadcast_to(departure, (8, CAP))
            weight = weight * (departure * scale_of(geo))
            far = weight * fx
            near = weight - far
            high = [near.astype(BF16).astype(F32), far.astype(BF16).astype(F32)]
            stacked = jnp.concatenate([high[0], near - high[0], high[1], far - high[1]], axis=0)
            turned = stacked.T
            here = pl.ds(pl.multiple_of(s * CAP, CAP), CAP)
            for k in range(4 * cells // LANES):
                spread[k, here, :] = turned[:, k * LANES : (k + 1) * LANES].astype(BF16)

    fetch(0, even)

    def interpolate(t):
        fetch(2 * t + 1, odd)
        use(2 * t, even)
        fetch(jnp.minimum(2 * t + 2, groups - 1), even)
        use(2 * t + 1, odd)

    each(0, groups // 2, interpolate)

    def tot_copy(wide):
        return remote(total.at[wide], got2.at[wide], tot_s.at[wide], tot_r.at[wide], partner)

    lane = lax.broadcasted_iota(jnp.int32, (cells, LANES), 1)
    last = jnp.zeros((cells, LANES), F32)
    for wide in range(wides):
        piece = lax.dot_general(
            jnp.concatenate([select[s, wide * BLOCK : (wide + 1) * BLOCK, :] for s in range(tiles)], axis=1),
            jnp.concatenate([spread[k] for k in range(4 * cells // LANES)], axis=1),
            (((1,), (0,)), ((), ())),
            preferred_element_type=F32,
        )
        piece = piece.T
        for k in range(per_wide):
            cut = slice(k * LANES, (k + 1) * LANES)
            here = piece[0:cells, cut] + piece[cells : 2 * cells, cut]
            moved = pltpu.roll(piece[2 * cells : 3 * cells, cut] + piece[3 * cells :, cut], 1, 1)
            total[wide, :, cut] = here + jnp.where(lane == 0, last, moved)
            last = moved
        tot_copy(wide).start()

    totals = behind.edge_start()
    for wide in range(wides):
        tot_copy(wide).wait_recv()
        for level in range(levels):
            part = slice(level * ty, (level + 1) * ty)
            for k in range(per_wide):
                block = wide * per_wide + k
                here = slice(k * LANES, (k + 1) * LANES)
                forcing = total[wide, part, here] + got2[wide, part, here]
                for i in range(m):
                    h, w = split(members[i, level, :, block * LANES : (block + 1) * LANES].astype(F32) * forcing)
                    dh[level, block, i * ty : (i + 1) * ty, :] = h
                    dl[level, block, i * ty : (i + 1) * ty, :] = w
        behind.edge(wide, totals)
    behind.edge_along_x(totals)
    behind.gather_start()
    for k in peers.order:
        dep_copy(k, peers.index(k), me).start()
    returned[me] = back[me]
    behind.main_rows()
    behind.e_copy().start()
    behind.main_cols(range(0, levels - 1))
    behind.scan()
    behind.main_cols(range(levels - 1, levels))
    behind.e_copy().wait()
    for level in range(levels):
        def finish(k, level=level):
            at = lanes(k * LANES)
            for i in range(m):
                out[i, level, :, at] = control[i, level, :, at] + behind.inner(level, i, at)

        each(0, geo.blocks, finish)

    every = remote(back.at[others], returned.at[others], dep_s, dep_r, partner)
    every.wait_send()
    every.wait_recv()
    for t in range(tiles):
        out_dep[0:1, t * CAP : (t + 1) * CAP] = returned[t, 0:1, :]
    ahead.sent()
    for wide in range(wides):
        own_copy(wide).wait_send()
        tot_copy(wide).wait_send()
    ends = behind.take()
    for k in range(geo.blocks):
        at = slice(k * LANES, (k + 1) * LANES)
        for level in range(levels):
            s1, s2 = behind.entering(ends, level, k)
            for i in range(m):
                out[i, level, :, at] += rowt1[level, 0] * s1[i : i + 1, :] + rowt1[level, 1] * s2[i : i + 1, :]
    behind.sent()


def body(control, members, obs_corner, obs_count, offset_y, offset_x, offset_z, innovation, precision):
    m, levels, ty, tx = control.shape
    rows = lax.axis_size("row")
    tiles = rows * lax.axis_size("col")
    geo = Geometry(m, levels, ty, tx, rows)
    cells = levels * ty
    size = 4 if tiles >= 8 else 2

    def by_tile(array):
        return array.reshape(tiles, CAP)

    mats = np.stack([a for reverse in (False, True) for a in geo.row_matrix(reverse)])
    tabs = np.stack([geo.col_tables(reverse) for reverse in (False, True)])
    rowts = np.stack([geo.row_tables(reverse) for reverse in (False, True)])
    operands = [control, members, jnp.asarray(mats), jnp.asarray(tabs), jnp.asarray(rowts), by_tile(obs_corner), obs_count]
    operands += [by_tile(a) for a in (offset_y, offset_x, offset_z, innovation, precision)]
    dma = pltpu.SemaphoreType.DMA
    chunks, per, lines = geo.chunks, geo.per, geo.lines
    comm = [
        pltpu.VMEM((levels, 2, lines, LANES), F32),
        pltpu.VMEM((levels, 2, lines, LANES), F32),
        pltpu.VMEM((chunks + 1, 2, m, LANES), F32),
        pltpu.VMEM((per, rows, 2, m, LANES), F32),
        pltpu.VMEM((per, rows, 2, m, LANES), F32),
        pltpu.VMEM((chunks + 1, 2, m, LANES), F32),
        pltpu.VMEM((8, LANES), F32),
        pltpu.VMEM((levels, BLOCK // LANES, tx, LANES), BF16),
        pltpu.VMEM((levels, BLOCK // LANES, tx, LANES), BF16),
        dma,
        dma,
        dma,
        dma,
        dma,
        dma,
        dma,
        dma,
    ]
    scratch = [
        *[pltpu.VMEM(a.shape, a.dtype) for a in operands],
        dma((len(operands),)),
        pltpu.VMEM((levels, geo.blocks, lines, LANES), BF16),
        pltpu.VMEM((levels, geo.blocks, lines, LANES), BF16),
        pltpu.VMEM((levels, geo.wide * 4 * m, BLOCK), BF16),
        pltpu.VMEM((8, LANES), F32),
        pltpu.VMEM((levels, lines, tx), F32),
    ]
    scratch += comm + comm
    wide_shape = (geo.wide, cells, BLOCK)
    scratch += [
        pltpu.VMEM((tiles, 8, CAP), F32),
        pltpu.VMEM((tiles, 8, CAP), F32),
        pltpu.VMEM((tiles, 8, CAP), F32),
        pltpu.VMEM((tiles, 8, CAP), F32),
        dma,
        dma,
        dma,
        dma,
        pltpu.VMEM(wide_shape, F32),
        pltpu.VMEM(wide_shape, F32),
        pltpu.VMEM(wide_shape, F32),
        pltpu.VMEM(wide_shape, F32),
        dma((geo.wide,)),
        dma((geo.wide,)),
        dma((geo.wide,)),
        dma((geo.wide,)),
        pltpu.VMEM((tiles, tx, CAP), BF16),
        pltpu.VMEM((4 * cells, tx), BF16),
        pltpu.VMEM((4 * cells, size * CAP), F32),
        pltpu.VMEM((4 * cells, size * CAP), F32),
        pltpu.VMEM((4 * cells // LANES, tiles * CAP, LANES), BF16),
    ]
    hbm = pl.BlockSpec(memory_space=pl.ANY)
    return pl.pallas_call(
        functools.partial(kernel, geo),
        out_shape=(pltpu.VMEM(control.shape, F32), pltpu.VMEM((1, tiles * CAP), F32)),
        in_specs=[hbm] * len(operands),
        out_specs=(VMEM, VMEM),
        scratch_shapes=scratch,
        compiler_params=pltpu.CompilerParams(collective_id=0, has_side_effects=True, vmem_limit_bytes=58 * 1024 * 1024),
        name="gradient",
    )(*operands)


def solution(mesh):
    return jax.shard_map(
        body,
        mesh=mesh,
        in_specs=(
            P("mem", None, "row", "col"),
            P("mem", None, "row", "col"),
            P(("mem", "row", "col"), None),
            P(("mem", "row", "col"), None),
            P(("mem", "row", "col"), None),
            P(("mem", "row", "col"), None),
            P(("mem", "row", "col"), None),
            P(("mem", "row", "col"), None),
            P(("mem", "row", "col"), None),
        ),
        out_specs=(P("mem", None, "row", "col"), P(("mem", "row", "col"), None)),
        check_vma=False,
    )
```

```python
import functools

import jax
import jax.numpy as jnp
import numpy as np
from jax import lax
from jax.experimental import pallas as pl
from jax.experimental.pallas import tpu as pltpu
from jax.sharding import PartitionSpec as P

CAP = 128
LANES = 128
BLOCK = 256
F32 = jnp.float32
BF16 = jnp.bfloat16
MESH = pl.DeviceIdType.MESH
VMEM = pl.BlockSpec(memory_space=pltpu.VMEM)


def filter_rates(length):
    one = np.float32(1.0)
    decay = np.exp(-one / np.float32(length), dtype=np.float32)
    square = np.float32(decay * decay)
    weight = np.power(np.power(one - square, np.float32(3.0)) / (one + square), np.float32(0.25))
    return float(decay), float(weight)


def halves(array):
    high = array.astype(jnp.bfloat16)
    low = (array - high.astype(np.float32)).astype(jnp.bfloat16)
    return high, low


class Geometry:
    def __init__(self, members, levels, ty, tx, rows):
        self.m, self.levels, self.ty, self.tx, self.rows = members, levels, ty, tx, rows
        self.lines = members * ty
        self.blocks = tx // LANES
        self.wide = tx // BLOCK
        self.chunks = levels * self.blocks
        self.half = rows // 2
        self.per = self.chunks // self.half
        self.x_rates = [filter_rates(tx / 16.0), filter_rates(tx / 64.0)]
        self.y_rates = [filter_rates(rows * ty / 2.0), filter_rates(ty / 2.0)]

    def row_matrix(self, reverse):
        m, ty = self.m, self.ty
        result = []
        for a, b in self.y_rates:
            place = np.arange(ty)
            gap = place[:, None] - place[None, :]
            local = np.where(gap >= 0, b * b * (gap + 1.0) * a ** np.maximum(gap, 0), 0.0)
            edge = np.stack([b * a ** (ty - 1.0 - place), b * b * (ty - place) * a ** (ty - 1.0 - place)])
            if reverse:
                local, edge = local.T, edge[:, ::-1]
            main = np.kron(np.eye(m), local)
            ends = np.concatenate([np.kron(np.eye(m), edge[s : s + 1]) for s in range(2)])
            result.append(np.concatenate([main, ends]))
        return halves(np.stack(result).astype(np.float32))

    def col_tables(self, reverse):
        tx = self.tx
        result = []
        for a, b in self.x_rates:
            place = np.arange(tx)
            ends = [b * a ** (tx - 1.0 - place), b * b * (tx - place) * a ** (tx - 1.0 - place)]
            enter = [b * (place + 1.0) * a ** (place + 1.0), a ** (place + 1.0)]
            table = np.stack(ends + enter)
            result.append(table[:, ::-1] if reverse else table)
        return np.stack(result).astype(np.float32)

    def row_tables(self, reverse):
        result = []
        for a, b in self.y_rates:
            place = np.arange(self.ty)
            table = np.stack([b * (place + 1.0) * a ** (place + 1.0), a ** (place + 1.0)])
            table = table[:, ::-1] if reverse else table
            result.append(np.broadcast_to(table[:, :, None], (2, self.ty, LANES)))
        return np.stack(result).astype(np.float32)

    def row_step(self):
        return [(a**self.ty, b * self.ty * a**self.ty) for a, b in self.y_rates]


def split(value):
    high = value.astype(BF16)
    return high, (value - high.astype(F32)).astype(BF16)


def dot(a, b):
    return jnp.dot(a, b, preferred_element_type=F32)


def dot3(ah, al, bh, bl):
    return dot(ah, bh) + dot(al, bh) + dot(ah, bl)


def each(low, high, action, unroll=1):
    def one(i, carry):
        action(i)
        return carry

    lax.fori_loop(low, high, one, 0, unroll=unroll)


def lanes(start, size=LANES):
    return pl.ds(pl.multiple_of(start, LANES), size)


def remote(src, dst, send, recv, device):
    return pltpu.make_async_remote_copy(
        src_ref=src, dst_ref=dst, send_sem=send, recv_sem=recv, device_id=device, device_id_type=MESH
    )


def scale_of(geo):
    return float(geo.m * 2) ** -0.5


def joined(ref, index, first, last, rows=slice(None)):
    return jnp.concatenate([ref[index, k, rows, :] for k in range(first, last)], axis=1)


def make_strips(geo, reverse, high, low):
    step = LANES
    tx = geo.tx
    down = lax.broadcasted_iota(jnp.int32, (step, LANES), 0).astype(F32)
    across = lax.broadcasted_iota(jnp.int32, (step, LANES), 1).astype(F32)
    lane = lax.broadcasted_iota(jnp.int32, (1, LANES), 1).astype(F32)
    slope = down - across if reverse else across - down
    for level, (a, b) in enumerate(geo.x_rates):
        rate = float(np.log(a))
        power = jnp.exp(down * (rate if reverse else -rate))
        for index in range(tx // step):
            for half in range(BLOCK // LANES):
                first = index * step
                if reverse:
                    shift = first - half * LANES
                    line = (b * b) * jnp.exp((shift - lane) * rate)
                else:
                    shift = tx - BLOCK - first + half * LANES
                    line = (b * b) * jnp.exp((shift + lane) * rate)
                if shift <= -LANES:
                    value = jnp.zeros((step, LANES), F32)
                else:
                    value = (slope + (shift + 1.0)) * (power * line)
                    if shift < LANES:
                        value = jnp.where(slope >= -float(shift), value, 0.0)
                h, w = split(value)
                high[level, half, first : first + step, :] = h
                low[level, half, first : first + step, :] = w


class Peers:
    def __init__(self, geo, row, col):
        bits = geo.rows.bit_length() - 1
        flips = [(1 - 2 * lax.rem(row // 2**i, 2)) * 2**i for i in range(bits)]
        self.row_at = [row]
        for i in range(bits):
            self.row_at += [r + flips[i] for r in self.row_at]
        self.col_at = [col, 1 - col]
        ring = (0, 1, 2, 1)
        hops = lambda k: 2 * ((k >> 1) & 1) + ring[(k >> 2) & 3] + ring[(k >> 4) & 3]
        self.order = sorted(range(1, 2 * geo.rows), key=lambda k: -hops(k))
        self.rows_order = sorted(range(1, geo.rows), key=lambda k: -hops(2 * k))
        self.scan_order = sorted(range(1, geo.half), key=lambda k: -hops(4 * k))

    def device(self, k):
        return {"row": self.row_at[k >> 1], "col": self.col_at[k & 1]}

    def index(self, k):
        return self.row_at[k >> 1] * 2 + self.col_at[k & 1]


class Filter:
    def __init__(self, geo, reverse, consts, comm, work, place, peers):
        self.geo, self.reverse, self.peers = geo, reverse, peers
        self.ph, self.plo, self.cols, self.rowt = consts
        (self.esend, self.erecv, self.bsend, self.brecv, self.csend, self.crecv, self.dsend, self.sh, self.sl,
         self.e_s, self.e_r, self.b_s, self.b_r, self.c_s, self.c_r, self.d_s, self.d_r) = comm
        self.dh, self.dl, self.bcat, self.bout, self.field = work
        self.row, self.col = place
        self.other = 1 - self.col
        self.enters = jnp.where(self.col == (0 if reverse else 1), 1.0, 0.0).astype(F32)
        self.scans = lax.rem(self.row, 2) == self.col
        self.spot = self.row // 2
        self.end_scan = 1 - self.col
        self.ends = geo.chunks

    def edge(self, wide, totals):
        geo = self.geo
        for level in range(geo.levels):
            value = dot3(
                self.ph[level, geo.lines :, :], self.plo[level, geo.lines :, :],
                joined(self.dh, level, 2 * wide, 2 * wide + 2), joined(self.dl, level, 2 * wide, 2 * wide + 2),
            )
            h, w = split(value)
            base = wide * 4 * geo.m
            self.bcat[level, base : base + 2 * geo.m, :] = h
            self.bcat[level, base + 2 * geo.m : base + 4 * geo.m, :] = w
            for s in range(2):
                for k in range(BLOCK // LANES):
                    at = wide * BLOCK + k * LANES
                    totals[level][s] += value[:, k * LANES : (k + 1) * LANES] * self.cols[level, s : s + 1, at : at + LANES]

    def edge_start(self):
        geo = self.geo
        return [[jnp.zeros((2 * geo.m, LANES), F32) for s in range(2)] for level in range(geo.levels)]

    def edge_along_x(self, totals):
        geo = self.geo
        m, size = geo.m, 4 * geo.m
        lane = lax.broadcasted_iota(jnp.int32, (2 * m, LANES), 1)
        ends = jnp.zeros((2 * m, LANES), F32)
        for level in range(geo.levels):
            for s in range(2):
                total = jnp.sum(totals[level][s], axis=1, keepdims=True)
                ends = jnp.where(lane == 2 * level + s, total, ends)
        self.bsend[self.ends, 0] = ends[:m]
        self.bsend[self.ends, 1] = ends[m:]
        for level in range(geo.levels):
            sums = [None] * geo.wide
            for gap in range(geo.wide):
                count = geo.wide - gap
                if self.reverse:
                    rows = slice(gap * size, geo.wide * size)
                    strip = slice(gap * BLOCK, (gap + 1) * BLOCK)
                else:
                    rows = slice(0, count * size)
                    strip = slice((count - 1) * BLOCK, count * BLOCK)
                left = self.bcat[level, rows, :]
                value = dot(left, joined(self.sh, level, 0, 2, strip)) + dot(left, joined(self.sl, level, 0, 2, strip))
                for i in range(count):
                    to = i if self.reverse else i + gap
                    term = value[i * size : i * size + 2 * m] + value[i * size + 2 * m : (i + 1) * size]
                    sums[to] = term if sums[to] is None else sums[to] + term
            for wide in range(geo.wide):
                for k in range(BLOCK // LANES):
                    piece = sums[wide][:, k * LANES : (k + 1) * LANES]
                    chunk = level * geo.blocks + wide * (BLOCK // LANES) + k
                    self.bsend[chunk, 0] = piece[:m]
                    self.bsend[chunk, 1] = piece[m:]

    def row_of(self, i):
        return 2 * i + self.col

    def b_copy(self, p, i, source):
        half = self.geo.half
        return remote(
            self.bsend.at[p * half + i], self.brecv.at[p, source], self.b_s, self.b_r, {"row": self.row_of(i)}
        )

    def c_copy(self, p, i, target):
        half = self.geo.half
        return remote(
            self.csend.at[p, target], self.crecv.at[p * half + i], self.c_s, self.c_r, {"row": target}
        )

    def end_copy(self, source):
        return remote(
            self.bsend.at[self.ends], self.brecv.at[0, source], self.d_s, self.b_r, {"row": self.end_scan}
        )

    def give_copy(self, target):
        return remote(
            self.csend.at[0, target], self.crecv.at[self.ends], self.c_s, self.d_r,
            {"row": target, "col": self.other},
        )

    def whole(self, src, dst, send, recv):
        return remote(src, dst, send, recv, {"col": self.other})

    def gather_start(self):
        geo = self.geo
        pl.when(self.row != self.end_scan)(lambda: self.end_copy(self.row).start())
        for p in range(geo.per):
            for k in self.peers.scan_order:
                self.b_copy(p, self.peers.row_at[2 * k] // 2, self.row).start()
            pl.when(lax.rem(self.row, 2) != self.col)(lambda p=p: self.b_copy(p, self.spot, self.row).start())

        @pl.when(self.row == self.end_scan)
        def _():
            self.brecv[0, self.row] = self.bsend[self.ends]

        @pl.when(self.scans)
        def _():
            for p in range(geo.per):
                self.brecv[p, self.row] = self.bsend[p * geo.half + self.spot]

    def run_scan(self, p, keep, mix):
        geo = self.geo

        def advance(lap, state):
            s1, s2 = state
            r = geo.rows - 1 - lap if self.reverse else lap
            self.csend[p, r, 0] = s1
            self.csend[p, r, 1] = s2
            return keep * s1 + self.brecv[p, r, 0], keep * s2 + mix * s1 + self.brecv[p, r, 1]

        zero = jnp.zeros((geo.m, LANES), F32)
        lax.fori_loop(0, geo.rows, advance, (zero, zero), unroll=4 if geo.rows % 4 == 0 else 1)

    def scan(self):
        geo = self.geo
        steps = geo.row_step()

        @pl.when(self.row == self.end_scan)
        def _():
            got = self.brecv.at[0, 0 : geo.rows - 1]
            self.whole(got, got, self.d_s, self.b_r).wait_recv()
            lane = lax.broadcasted_iota(jnp.int32, (geo.m, LANES), 1)
            keep = jnp.where(lane < 2, steps[0][0], steps[1][0]).astype(F32)
            mix = jnp.where(lane < 2, steps[0][1], steps[1][1]).astype(F32)
            self.run_scan(0, keep, mix)
            for k in self.peers.rows_order + [0]:
                self.give_copy(self.peers.row_at[k]).start()

        @pl.when(self.scans)
        def _():
            got = self.brecv.at[:, 0 : geo.rows - 1]
            self.whole(got, got, self.b_s, self.b_r).wait_recv()
            for p in range(geo.per):
                first = p * geo.half + self.spot < geo.blocks
                keep = jnp.where(first, steps[0][0], steps[1][0]).astype(F32)
                mix = jnp.where(first, steps[0][1], steps[1][1]).astype(F32)
                self.run_scan(p, keep, mix)
                for k in self.peers.rows_order:
                    self.c_copy(p, self.spot, self.peers.row_at[k]).start()
                self.crecv[p * geo.half + self.spot] = self.csend[p, self.row]

    def main_rows(self):
        geo = self.geo
        for level in range(geo.levels):
            sums = [jnp.zeros((geo.lines, LANES), F32) for s in range(2)]
            for wide in range(geo.wide):
                value = dot3(
                    self.ph[level, : geo.lines, :], self.plo[level, : geo.lines, :],
                    joined(self.dh, level, 2 * wide, 2 * wide + 2), joined(self.dl, level, 2 * wide, 2 * wide + 2),
                )
                for k in range(BLOCK // LANES):
                    at = wide * BLOCK + k * LANES
                    piece = value[:, k * LANES : (k + 1) * LANES]
                    h, w = split(piece)
                    self.dh[level, 2 * wide + k] = h
                    self.dl[level, 2 * wide + k] = w
                    sums = [sums[s] + piece * self.cols[level, s : s + 1, at : at + LANES] for s in range(2)]
            for s in range(2):
                total = jnp.sum(sums[s], axis=1, keepdims=True)
                self.esend[level, s] = jnp.broadcast_to(total, (geo.lines, LANES))

    def e_start(self):
        step = self.geo.lines // 4
        for level in range(self.geo.levels):
            for s in range(2):
                for first in range(0, self.geo.lines, step):
                    cut = slice(first, first + step)
                    remote(
                        self.esend.at[level, s, cut], self.erecv.at[level, s, cut], self.e_s, self.e_r, {"col": self.other}
                    ).start()

    def e_copy(self):
        return remote(self.esend, self.erecv, self.e_s, self.e_r, {"col": self.other})

    def main_cols(self, chosen):
        geo = self.geo
        tx = geo.tx
        for level in chosen:
            for wide in range(geo.wide):
                if self.reverse:
                    cut, strip = (2 * wide, geo.blocks), slice(0, tx - BLOCK * wide)
                else:
                    cut, strip = (0, 2 * wide + 2), slice(tx - BLOCK * (wide + 1), tx)
                self.field[level, :, wide * BLOCK : (wide + 1) * BLOCK] = dot3(
                    joined(self.dh, level, *cut), joined(self.dl, level, *cut),
                    joined(self.sh, level, 0, 2, strip), joined(self.sl, level, 0, 2, strip),
                )

    def inner(self, level, i, at):
        cut = slice(i * self.geo.ty, (i + 1) * self.geo.ty)
        q = self.cols[level, 2:3, at] * self.enters
        w = self.cols[level, 3:4, at] * self.enters
        return self.field[level, cut, at] + self.erecv[level, 0, cut] * q + self.erecv[level, 1, cut] * w

    def take(self):
        geo = self.geo

        def wait(count):
            some, part = self.crecv.at[0:count], self.bsend.at[0:count]
            self.whole(part, some, self.b_s, self.c_r).wait_recv()
            self.whole(part, some, self.b_s, self.c_r).wait_send()

        pl.when(self.scans)(lambda: wait(geo.chunks - geo.per))
        pl.when(lax.rem(self.row, 2) != self.col)(lambda: wait(geo.chunks))
        self.give_copy(self.row).wait_recv()
        ends = [self.crecv[self.ends, s] * self.enters for s in range(2)]
        return [
            [[jnp.broadcast_to(ends[s][:, 2 * level + e : 2 * level + e + 1], (geo.m, LANES)) for e in range(2)] for s in range(2)]
            for level in range(geo.levels)
        ]

    def entering(self, ends, level, k):
        at = slice(k * LANES, (k + 1) * LANES)
        q, w = self.cols[level, 2:3, at], self.cols[level, 3:4, at]
        return [
            self.crecv[level * self.geo.blocks + k, s] + ends[level][s][0] * q + ends[level][s][1] * w for s in range(2)
        ]

    def sent(self):
        geo = self.geo
        pl.when(self.row != self.end_scan)(lambda: self.end_copy(self.row).wait_send())

        @pl.when(self.row == self.end_scan)
        def _():
            sent = self.csend.at[0]
            self.whole(sent, sent, self.c_s, self.d_r).wait_send()

        @pl.when(self.scans)
        def _():
            sent = self.csend.at[:, 0 : geo.rows - 1]
            self.whole(sent, sent, self.c_s, self.c_r).wait_send()


def stencil_rows(data, ty):
    y0, fy, fz = data[0:1], data[2:3], data[4:5]
    place = lax.broadcasted_iota(jnp.int32, (ty, CAP), 0).astype(F32)
    weight = jnp.where(place == y0, 1.0 - fy, jnp.where(place == y0 + 1.0, fy, 0.0))
    return jnp.concatenate([weight * (1.0 - fz), weight * fz], axis=0)


def kernel(geo, *refs):
    sources, (out, out_dep) = refs[:12], refs[12:14]
    refs = refs[14:]
    held, in_sem = refs[:12], refs[12]
    control, members, mats, tabs, rowts, corner, count, off_y, off_x, off_z, innov, prec = held
    refs = refs[10:]
    work, comms = refs[3:8], (refs[8:25], refs[25:42])
    (payload, arrived, back, returned, obs_s, obs_r, dep_s, dep_r, own, got, total, got2, own_s, own_r, tot_s, tot_r,
     select, parts, mixed, even, odd, spread) = refs[42:]
    m, levels, ty, tx, rows = geo.m, geo.levels, geo.ty, geo.tx, geo.rows
    cells = levels * ty
    wides, per_wide = geo.wide, BLOCK // LANES
    row, col, mem = lax.axis_index("row"), lax.axis_index("col"), lax.axis_index("mem")
    tiles = rows * 2
    me = row * 2 + col
    partner = {"mem": 1 - mem}
    dh, dl, bcat, bout, field = work
    peers = Peers(geo, row, col)

    loads = [pltpu.make_async_copy(a, b, in_sem.at[i]) for i, (a, b) in enumerate(zip(sources, held))]
    for load in loads:
        load.start()

    barrier = pltpu.get_barrier_semaphore()
    for k in peers.order:
        pl.semaphore_signal(barrier, inc=1, device_id=peers.device(k), device_id_type=MESH)
    pl.semaphore_signal(barrier, inc=1, device_id=partner, device_id_type=MESH)

    place = (row, col)
    ahead = Filter(geo, False, (mats.at[0], mats.at[1], tabs.at[0], rowts.at[0]), comms[0], work, place, peers)
    behind = Filter(geo, True, (mats.at[2], mats.at[3], tabs.at[1], rowts.at[1]), comms[1], work, place, peers)
    rowt0, rowt1 = rowts.at[0], rowts.at[1]

    make_strips(geo, False, ahead.sh, ahead.sl)
    for load in loads:
        load.wait()
    for level in range(levels):
        for i in range(m):
            cut = slice(i * ty, (i + 1) * ty)
            for k in range(geo.blocks):
                h, w = split(control[i, level, :, k * LANES : (k + 1) * LANES])
                dh[level, k, cut, :] = h
                dl[level, k, cut, :] = w
    totals = ahead.edge_start()
    for wide in range(wides):
        ahead.edge(wide, totals)
    ahead.edge_along_x(totals)

    pl.semaphore_wait(barrier, tiles)
    ahead.gather_start()

    corners = corner[...]
    row_in = lax.shift_right_logical(corners, int(tx).bit_length() - 1)
    payload[:, 0, :] = row_in.astype(F32)
    payload[:, 1, :] = (corners - row_in * tx).astype(F32)
    payload[:, 2, :] = off_y[...]
    payload[:, 3, :] = off_x[...]
    payload[:, 4, :] = off_z[...]
    payload[:, 5, :] = innov[...]
    down = lax.broadcasted_iota(jnp.int32, (tiles, tiles), 0)
    across = lax.broadcasted_iota(jnp.int32, (tiles, tiles), 1)
    used = jnp.sum(jnp.where(down == across, count[...].astype(F32), 0.0), axis=1, keepdims=True)
    slot = lax.broadcasted_iota(jnp.int32, (tiles, CAP), 1).astype(F32)
    payload[:, 6, :] = jnp.where(slot < used, prec[...], 0.0)
    payload[:, 7, :] = jnp.zeros((tiles, CAP), F32)

    def obs_copy(k, to, slot):
        return remote(payload.at[to], arrived.at[slot], obs_s, obs_r, peers.device(k))

    def dep_copy(k, to, slot):
        return remote(back.at[to], returned.at[slot], dep_s, dep_r, peers.device(k))

    for k in peers.order:
        obs_copy(k, peers.index(k), me).start()
    arrived[me] = payload[me]

    ahead.main_rows()
    ahead.e_start()
    ahead.main_cols(range(0, levels - 1))
    ahead.scan()
    ahead.main_cols(range(levels - 1, levels))

    make_strips(geo, True, behind.sh, behind.sl)
    ahead.e_copy().wait()
    for wide in range(wides):
        for k in range(per_wide):
            at = slice(wide * BLOCK + k * LANES, wide * BLOCK + (k + 1) * LANES)
            for level in range(levels):
                value = members[0, level, :, at].astype(F32) * ahead.inner(level, 0, at)
                for i in range(1, m):
                    value = value + members[i, level, :, at].astype(F32) * ahead.inner(level, i, at)
                own[wide, level * ty : (level + 1) * ty, k * LANES : (k + 1) * LANES] = value

    others = pl.ds(0, tiles - 1)
    every = remote(payload.at[others], arrived.at[others], obs_s, obs_r, partner)
    every.wait_send()
    every.wait_recv()

    iota = lax.broadcasted_iota(jnp.int32, (LANES, CAP), 0).astype(F32)
    packed = 16

    def choose(s):
        x0 = arrived[s, 1:2, :]
        block = jnp.floor(x0 * (1.0 / LANES))
        inside = jnp.where(iota == x0 - block * LANES, 1.0, 0.0).astype(BF16)
        block = jnp.broadcast_to(block, (packed, CAP))
        for h in range(tx // LANES):
            there = jnp.where(block == float(h), 1.0, 0.0).astype(BF16)
            for g in range(0, LANES, packed):
                first = h * LANES + g
                select[s, first : first + packed, :] = inside[g : g + packed] * there

    early = tiles // 4
    each(0, early, choose, 2 if early % 2 == 0 else 1)

    ends = ahead.take()

    def own_copy(wide):
        return remote(own.at[wide], got.at[wide], own_s.at[wide], own_r.at[wide], partner)

    for wide in reversed(range(wides)):
        for k in range(per_wide):
            block = wide * per_wide + k
            at = slice(block * LANES, (block + 1) * LANES)
            here = slice(k * LANES, (k + 1) * LANES)
            for level in range(levels):
                s1, s2 = ahead.entering(ends, level, block)
                value = own[wide, level * ty : (level + 1) * ty, here]
                for i in range(m):
                    value = value + members[i, level, :, at].astype(F32) * (
                        rowt0[level, 0] * s1[i : i + 1, :] + rowt0[level, 1] * s2[i : i + 1, :]
                    )
                own[wide, level * ty : (level + 1) * ty, here] = value * scale_of(geo)
        for first in range(0, cells, 8):
            cut = slice(first, first + 8)
            remote(own.at[wide, cut], got.at[wide, cut], own_s.at[wide], own_r.at[wide], partner).start()
    each(early, tiles, choose, 2 if early % 2 == 0 else 1)

    size = 4 if tiles >= 8 else 2
    groups = tiles // size
    middle = tx // 2

    def chosen(group, rows_of):
        return jnp.concatenate([select[group * size + i, rows_of, :] for i in range(size)], axis=1)

    def share(group):
        mixed[group] = dot(parts[:, middle:], chosen(group, slice(middle, tx)))

    lane = lax.broadcasted_iota(jnp.int32, (cells, BLOCK), 1)
    first_of_right = jnp.zeros((cells, 1), F32)
    for wide in reversed(range(wides)):
        own_copy(wide).wait_recv()
        value = own[wide] + got[wide]
        moved = jnp.where(lane == BLOCK - 1, first_of_right, pltpu.roll(value, BLOCK - 1, 1))
        first_of_right = value[:, 0:1]
        h, w = split(value)
        parts[0:cells, wide * BLOCK : (wide + 1) * BLOCK] = h
        parts[cells : 2 * cells, wide * BLOCK : (wide + 1) * BLOCK] = w
        h, w = split(moved)
        parts[2 * cells : 3 * cells, wide * BLOCK : (wide + 1) * BLOCK] = h
        parts[3 * cells :, wide * BLOCK : (wide + 1) * BLOCK] = w
        if wide * BLOCK == middle:
            each(0, groups, share, 2)

    def fetch(group, buffer):
        buffer[...] = mixed[group] + dot(parts[:, :middle], chosen(group, slice(0, middle)))

    def use(group, buffer):
        for i in range(size):
            s = group * size + i
            data = arrived[s]
            cut = slice(i * CAP, (i + 1) * CAP)
            fx = data[3:4]
            left = buffer[0:cells, cut] + buffer[cells : 2 * cells, cut]
            right = buffer[2 * cells : 3 * cells, cut] + buffer[3 * cells :, cut]
            weight = stencil_rows(data, ty)
            image = jnp.sum(weight * (left + fx * (right - left)), axis=0, keepdims=True)
            departure = data[6:7] * (image - data[5:6])
            back[s] = jnp.broadcast_to(departure, (8, CAP))
            weight = weight * (departure * scale_of(geo))
            far = weight * fx
            h, w = split(weight - far)
            spread[s, 0:cells] = h
            spread[s, cells : 2 * cells] = w
            h, w = split(far)
            spread[s, 2 * cells : 3 * cells] = h
            spread[s, 3 * cells :] = w

    fetch(0, even)

    def interpolate(t):
        fetch(2 * t + 1, odd)
        use(2 * t, even)
        fetch(jnp.minimum(2 * t + 2, groups - 1), even)
        use(2 * t + 1, odd)

    each(0, groups // 2, interpolate)

    def tot_copy(wide):
        return remote(total.at[wide], got2.at[wide], tot_s.at[wide], tot_r.at[wide], partner)

    lane = lax.broadcasted_iota(jnp.int32, (cells, LANES), 1)
    last = jnp.zeros((cells, LANES), F32)
    for wide in range(wides):
        piece = lax.dot_general(
            jnp.concatenate([select[s, wide * BLOCK : (wide + 1) * BLOCK, :] for s in range(tiles)], axis=1),
            jnp.concatenate([spread[s] for s in range(tiles)], axis=1),
            (((1,), (1,)), ((), ())),
            preferred_element_type=F32,
        )
        piece = piece.T
        for k in range(per_wide):
            cut = slice(k * LANES, (k + 1) * LANES)
            here = piece[0:cells, cut] + piece[cells : 2 * cells, cut]
            moved = pltpu.roll(piece[2 * cells : 3 * cells, cut] + piece[3 * cells :, cut], 1, 1)
            total[wide, :, cut] = here + jnp.where(lane == 0, last, moved)
            last = moved
        for first in range(0, cells, 8):
            cut = slice(first, first + 8)
            remote(total.at[wide, cut], got2.at[wide, cut], tot_s.at[wide], tot_r.at[wide], partner).start()

    totals = behind.edge_start()
    for wide in range(wides):
        tot_copy(wide).wait_recv()
        for level in range(levels):
            part = slice(level * ty, (level + 1) * ty)
            for k in range(per_wide):
                block = wide * per_wide + k
                here = slice(k * LANES, (k + 1) * LANES)
                forcing = total[wide, part, here] + got2[wide, part, here]
                for i in range(m):
                    h, w = split(members[i, level, :, block * LANES : (block + 1) * LANES].astype(F32) * forcing)
                    dh[level, block, i * ty : (i + 1) * ty, :] = h
                    dl[level, block, i * ty : (i + 1) * ty, :] = w
        behind.edge(wide, totals)
    behind.edge_along_x(totals)
    behind.gather_start()
    for k in peers.order:
        dep_copy(k, peers.index(k), me).start()
    returned[me] = back[me]
    behind.main_rows()
    behind.e_start()
    behind.main_cols(range(0, levels - 1))
    behind.scan()
    behind.main_cols(range(levels - 1, levels))
    behind.e_copy().wait()
    for level in range(levels):
        def finish(k, level=level):
            at = lanes(k * LANES)
            for i in range(m):
                out[i, level, :, at] = control[i, level, :, at] + behind.inner(level, i, at)

        each(0, geo.blocks, finish)

    every = remote(back.at[others], returned.at[others], dep_s, dep_r, partner)
    every.wait_send()
    every.wait_recv()
    for t in range(tiles):
        out_dep[0:1, t * CAP : (t + 1) * CAP] = returned[t, 0:1, :]
    ahead.sent()
    for wide in range(wides):
        own_copy(wide).wait_send()
        tot_copy(wide).wait_send()
    ends = behind.take()
    for k in range(geo.blocks):
        at = slice(k * LANES, (k + 1) * LANES)
        for level in range(levels):
            s1, s2 = behind.entering(ends, level, k)
            for i in range(m):
                out[i, level, :, at] += rowt1[level, 0] * s1[i : i + 1, :] + rowt1[level, 1] * s2[i : i + 1, :]
    behind.sent()


def body(control, members, obs_corner, obs_count, offset_y, offset_x, offset_z, innovation, precision):
    m, levels, ty, tx = control.shape
    rows = lax.axis_size("row")
    tiles = rows * lax.axis_size("col")
    geo = Geometry(m, levels, ty, tx, rows)
    cells = levels * ty
    size = 4 if tiles >= 8 else 2

    def by_tile(array):
        return array.reshape(tiles, CAP)

    mats = np.stack([a for reverse in (False, True) for a in geo.row_matrix(reverse)])
    tabs = np.stack([geo.col_tables(reverse) for reverse in (False, True)])
    rowts = np.stack([geo.row_tables(reverse) for reverse in (False, True)])
    operands = [control, members, jnp.asarray(mats), jnp.asarray(tabs), jnp.asarray(rowts), by_tile(obs_corner), obs_count]
    operands += [by_tile(a) for a in (offset_y, offset_x, offset_z, innovation, precision)]
    dma = pltpu.SemaphoreType.DMA
    chunks, per, lines = geo.chunks, geo.per, geo.lines
    comm = [
        pltpu.VMEM((levels, 2, lines, LANES), F32),
        pltpu.VMEM((levels, 2, lines, LANES), F32),
        pltpu.VMEM((chunks + 1, 2, m, LANES), F32),
        pltpu.VMEM((per, rows, 2, m, LANES), F32),
        pltpu.VMEM((per, rows, 2, m, LANES), F32),
        pltpu.VMEM((chunks + 1, 2, m, LANES), F32),
        pltpu.VMEM((8, LANES), F32),
        pltpu.VMEM((levels, BLOCK // LANES, tx, LANES), BF16),
        pltpu.VMEM((levels, BLOCK // LANES, tx, LANES), BF16),
        dma,
        dma,
        dma,
        dma,
        dma,
        dma,
        dma,
        dma,
    ]
    scratch = [
        *[pltpu.VMEM(a.shape, a.dtype) for a in operands],
        dma((len(operands),)),
        pltpu.VMEM((levels, geo.blocks, lines, LANES), BF16),
        pltpu.VMEM((levels, geo.blocks, lines, LANES), BF16),
        pltpu.VMEM((levels, geo.wide * 4 * m, BLOCK), BF16),
        pltpu.VMEM((8, LANES), F32),
        pltpu.VMEM((levels, lines, tx), F32),
    ]
    scratch += comm + comm
    wide_shape = (geo.wide, cells, BLOCK)
    scratch += [
        pltpu.VMEM((tiles, 8, CAP), F32),
        pltpu.VMEM((tiles, 8, CAP), F32),
        pltpu.VMEM((tiles, 8, CAP), F32),
        pltpu.VMEM((tiles, 8, CAP), F32),
        dma,
        dma,
        dma,
        dma,
        pltpu.VMEM(wide_shape, F32),
        pltpu.VMEM(wide_shape, F32),
        pltpu.VMEM(wide_shape, F32),
        pltpu.VMEM(wide_shape, F32),
        dma((geo.wide,)),
        dma((geo.wide,)),
        dma((geo.wide,)),
        dma((geo.wide,)),
        pltpu.VMEM((tiles, tx, CAP), BF16),
        pltpu.VMEM((4 * cells, tx), BF16),
        pltpu.VMEM((tiles // size, 4 * cells, size * CAP), F32),
        pltpu.VMEM((4 * cells, size * CAP), F32),
        pltpu.VMEM((4 * cells, size * CAP), F32),
        pltpu.VMEM((tiles, 4 * cells, CAP), BF16),
    ]
    hbm = pl.BlockSpec(memory_space=pl.ANY)
    return pl.pallas_call(
        functools.partial(kernel, geo),
        out_shape=(pltpu.VMEM(control.shape, F32), pltpu.VMEM((1, tiles * CAP), F32)),
        in_specs=[hbm] * len(operands),
        out_specs=(VMEM, VMEM),
        scratch_shapes=scratch,
        compiler_params=pltpu.CompilerParams(collective_id=0, has_side_effects=True, vmem_limit_bytes=58 * 1024 * 1024),
        name="gradient",
    )(*operands)


def solution(mesh):
    return jax.shard_map(
        body,
        mesh=mesh,
        in_specs=(
            P("mem", None, "row", "col"),
            P("mem", None, "row", "col"),
            P(("mem", "row", "col"), None),
            P(("mem", "row", "col"), None),
            P(("mem", "row", "col"), None),
            P(("mem", "row", "col"), None),
            P(("mem", "row", "col"), None),
            P(("mem", "row", "col"), None),
            P(("mem", "row", "col"), None),
        ),
        out_specs=(P("mem", None, "row", "col"), P(("mem", "row", "col"), None)),
        check_vma=False,
    )
```

```python
import functools

import jax
import jax.numpy as jnp
import numpy as np
from jax import lax
from jax.experimental import pallas as pl
from jax.experimental.pallas import tpu as pltpu
from jax.sharding import PartitionSpec as P

CAP = 128
LANES = 128
BLOCK = 256
F32 = jnp.float32
BF16 = jnp.bfloat16
MESH = pl.DeviceIdType.MESH
VMEM = pl.BlockSpec(memory_space=pltpu.VMEM)


def filter_rates(length):
    one = np.float32(1.0)
    decay = np.exp(-one / np.float32(length), dtype=np.float32)
    square = np.float32(decay * decay)
    weight = np.power(np.power(one - square, np.float32(3.0)) / (one + square), np.float32(0.25))
    return float(decay), float(weight)


def halves(array):
    high = array.astype(jnp.bfloat16)
    low = (array - high.astype(np.float32)).astype(jnp.bfloat16)
    return high, low


class Geometry:
    def __init__(self, members, levels, ty, tx, rows):
        self.m, self.levels, self.ty, self.tx, self.rows = members, levels, ty, tx, rows
        self.lines = members * ty
        self.blocks = tx // LANES
        self.wide = tx // BLOCK
        self.chunks = levels * self.blocks
        self.half = rows // 2
        self.per = self.chunks // self.half
        self.x_rates = [filter_rates(tx / 16.0), filter_rates(tx / 64.0)]
        self.y_rates = [filter_rates(rows * ty / 2.0), filter_rates(ty / 2.0)]

    def row_matrix(self, reverse):
        m, ty = self.m, self.ty
        result = []
        for a, b in self.y_rates:
            place = np.arange(ty)
            gap = place[:, None] - place[None, :]
            local = np.where(gap >= 0, b * b * (gap + 1.0) * a ** np.maximum(gap, 0), 0.0)
            edge = np.stack([b * a ** (ty - 1.0 - place), b * b * (ty - place) * a ** (ty - 1.0 - place)])
            if reverse:
                local, edge = local.T, edge[:, ::-1]
            main = np.kron(np.eye(m), local)
            ends = np.concatenate([np.kron(np.eye(m), edge[s : s + 1]) for s in range(2)])
            result.append(np.concatenate([main, ends]))
        return halves(np.stack(result).astype(np.float32))

    def col_tables(self, reverse):
        tx = self.tx
        result = []
        for a, b in self.x_rates:
            place = np.arange(tx)
            ends = [b * a ** (tx - 1.0 - place), b * b * (tx - place) * a ** (tx - 1.0 - place)]
            enter = [b * (place + 1.0) * a ** (place + 1.0), a ** (place + 1.0)]
            table = np.stack(ends + enter)
            result.append(table[:, ::-1] if reverse else table)
        return np.stack(result).astype(np.float32)

    def row_tables(self, reverse):
        result = []
        for a, b in self.y_rates:
            place = np.arange(self.ty)
            table = np.stack([b * (place + 1.0) * a ** (place + 1.0), a ** (place + 1.0)])
            table = table[:, ::-1] if reverse else table
            result.append(np.broadcast_to(table[:, :, None], (2, self.ty, LANES)))
        return np.stack(result).astype(np.float32)

    def row_step(self):
        return [(a**self.ty, b * self.ty * a**self.ty) for a, b in self.y_rates]


def split(value):
    high = value.astype(BF16)
    return high, (value - high.astype(F32)).astype(BF16)


def dot(a, b):
    return jnp.dot(a, b, preferred_element_type=F32)


def dot3(ah, al, bh, bl):
    return dot(ah, bh) + dot(al, bh) + dot(ah, bl)


def each(low, high, action, unroll=1):
    def one(i, carry):
        action(i)
        return carry

    lax.fori_loop(low, high, one, 0, unroll=unroll)


def lanes(start, size=LANES):
    return pl.ds(pl.multiple_of(start, LANES), size)


def remote(src, dst, send, recv, device):
    return pltpu.make_async_remote_copy(
        src_ref=src, dst_ref=dst, send_sem=send, recv_sem=recv, device_id=device, device_id_type=MESH
    )


def scale_of(geo):
    return float(geo.m * 2) ** -0.5


def joined(ref, index, first, last, rows=slice(None)):
    return jnp.concatenate([ref[index, k, rows, :] for k in range(first, last)], axis=1)


def make_strips(geo, reverse, high, low):
    step = LANES
    tx = geo.tx
    down = lax.broadcasted_iota(jnp.int32, (step, LANES), 0).astype(F32)
    across = lax.broadcasted_iota(jnp.int32, (step, LANES), 1).astype(F32)
    lane = lax.broadcasted_iota(jnp.int32, (1, LANES), 1).astype(F32)
    slope = down - across if reverse else across - down
    for level, (a, b) in enumerate(geo.x_rates):
        rate = float(np.log(a))
        power = jnp.exp(down * (rate if reverse else -rate))
        for index in range(tx // step):
            for half in range(BLOCK // LANES):
                first = index * step
                if reverse:
                    shift = first - half * LANES
                    line = (b * b) * jnp.exp((shift - lane) * rate)
                else:
                    shift = tx - BLOCK - first + half * LANES
                    line = (b * b) * jnp.exp((shift + lane) * rate)
                if shift <= -LANES:
                    value = jnp.zeros((step, LANES), F32)
                else:
                    value = (slope + (shift + 1.0)) * (power * line)
                    if shift < LANES:
                        value = jnp.where(slope >= -float(shift), value, 0.0)
                h, w = split(value)
                high[level, half, first : first + step, :] = h
                low[level, half, first : first + step, :] = w


class Peers:
    def __init__(self, geo, row, col):
        bits = geo.rows.bit_length() - 1
        flips = [(1 - 2 * lax.rem(row // 2**i, 2)) * 2**i for i in range(bits)]
        self.row_at = [row]
        for i in range(bits):
            self.row_at += [r + flips[i] for r in self.row_at]
        self.col_at = [col, 1 - col]
        ring = (0, 1, 2, 1)
        hops = lambda k: 2 * ((k >> 1) & 1) + ring[(k >> 2) & 3] + ring[(k >> 4) & 3]
        self.order = sorted(range(1, 2 * geo.rows), key=lambda k: -hops(k))
        self.rows_order = sorted(range(1, geo.rows), key=lambda k: -hops(2 * k))
        self.scan_order = sorted(range(1, geo.half), key=lambda k: -hops(4 * k))

    def device(self, k):
        return {"row": self.row_at[k >> 1], "col": self.col_at[k & 1]}

    def index(self, k):
        return self.row_at[k >> 1] * 2 + self.col_at[k & 1]


class Filter:
    def __init__(self, geo, reverse, consts, comm, work, place, peers):
        self.geo, self.reverse, self.peers = geo, reverse, peers
        self.ph, self.plo, self.cols, self.rowt = consts
        (self.esend, self.erecv, self.bsend, self.brecv, self.csend, self.crecv, self.dsend, self.sh, self.sl,
         self.e_s, self.e_r, self.b_s, self.b_r, self.c_s, self.c_r, self.d_s, self.d_r) = comm
        self.dh, self.dl, self.bcat, self.bout, self.field = work
        self.row, self.col = place
        self.other = 1 - self.col
        self.enters = jnp.where(self.col == (0 if reverse else 1), 1.0, 0.0).astype(F32)
        self.scans = lax.rem(self.row, 2) == self.col
        self.spot = self.row // 2
        self.end_scan = 1 - self.col
        self.ends = geo.chunks

    def edge(self, wide, totals):
        geo = self.geo
        for level in range(geo.levels):
            value = dot3(
                self.ph[level, geo.lines :, :], self.plo[level, geo.lines :, :],
                joined(self.dh, level, 2 * wide, 2 * wide + 2), joined(self.dl, level, 2 * wide, 2 * wide + 2),
            )
            h, w = split(value)
            base = wide * 4 * geo.m
            self.bcat[level, base : base + 2 * geo.m, :] = h
            self.bcat[level, base + 2 * geo.m : base + 4 * geo.m, :] = w
            for s in range(2):
                for k in range(BLOCK // LANES):
                    at = wide * BLOCK + k * LANES
                    totals[level][s] += value[:, k * LANES : (k + 1) * LANES] * self.cols[level, s : s + 1, at : at + LANES]

    def edge_start(self):
        geo = self.geo
        return [[jnp.zeros((2 * geo.m, LANES), F32) for s in range(2)] for level in range(geo.levels)]

    def edge_along_x(self, totals):
        geo = self.geo
        m, size = geo.m, 4 * geo.m
        lane = lax.broadcasted_iota(jnp.int32, (2 * m, LANES), 1)
        ends = jnp.zeros((2 * m, LANES), F32)
        for level in range(geo.levels):
            for s in range(2):
                total = jnp.sum(totals[level][s], axis=1, keepdims=True)
                ends = jnp.where(lane == 2 * level + s, total, ends)
        self.bsend[self.ends, 0] = ends[:m]
        self.bsend[self.ends, 1] = ends[m:]
        for level in range(geo.levels):
            sums = [None] * geo.wide
            for gap in range(geo.wide):
                count = geo.wide - gap
                if self.reverse:
                    rows = slice(gap * size, geo.wide * size)
                    strip = slice(gap * BLOCK, (gap + 1) * BLOCK)
                else:
                    rows = slice(0, count * size)
                    strip = slice((count - 1) * BLOCK, count * BLOCK)
                left = self.bcat[level, rows, :]
                value = dot(left, joined(self.sh, level, 0, 2, strip)) + dot(left, joined(self.sl, level, 0, 2, strip))
                for i in range(count):
                    to = i if self.reverse else i + gap
                    term = value[i * size : i * size + 2 * m] + value[i * size + 2 * m : (i + 1) * size]
                    sums[to] = term if sums[to] is None else sums[to] + term
            for wide in range(geo.wide):
                for k in range(BLOCK // LANES):
                    piece = sums[wide][:, k * LANES : (k + 1) * LANES]
                    chunk = level * geo.blocks + wide * (BLOCK // LANES) + k
                    self.bsend[chunk, 0] = piece[:m]
                    self.bsend[chunk, 1] = piece[m:]

    def row_of(self, i):
        return 2 * i + self.col

    def b_copy(self, p, i, source):
        half = self.geo.half
        return remote(
            self.bsend.at[p * half + i], self.brecv.at[p, source], self.b_s, self.b_r, {"row": self.row_of(i)}
        )

    def c_copy(self, p, i, target):
        half = self.geo.half
        return remote(
            self.csend.at[p, target], self.crecv.at[p * half + i], self.c_s, self.c_r, {"row": target}
        )

    def end_copy(self, source):
        return remote(
            self.bsend.at[self.ends], self.brecv.at[0, source], self.d_s, self.b_r, {"row": self.end_scan}
        )

    def give_copy(self, target):
        return remote(
            self.csend.at[0, target], self.crecv.at[self.ends], self.c_s, self.d_r,
            {"row": target, "col": self.other},
        )

    def whole(self, src, dst, send, recv):
        return remote(src, dst, send, recv, {"col": self.other})

    def gather_start(self):
        geo = self.geo
        pl.when(self.row != self.end_scan)(lambda: self.end_copy(self.row).start())
        for p in range(geo.per):
            for k in self.peers.scan_order:
                self.b_copy(p, self.peers.row_at[2 * k] // 2, self.row).start()
            pl.when(lax.rem(self.row, 2) != self.col)(lambda p=p: self.b_copy(p, self.spot, self.row).start())

        @pl.when(self.row == self.end_scan)
        def _():
            self.brecv[0, self.row] = self.bsend[self.ends]

        @pl.when(self.scans)
        def _():
            for p in range(geo.per):
                self.brecv[p, self.row] = self.bsend[p * geo.half + self.spot]

    def run_scan(self, p, keep, mix):
        geo = self.geo

        def advance(lap, state):
            s1, s2 = state
            r = geo.rows - 1 - lap if self.reverse else lap
            self.csend[p, r, 0] = s1
            self.csend[p, r, 1] = s2
            return keep * s1 + self.brecv[p, r, 0], keep * s2 + mix * s1 + self.brecv[p, r, 1]

        zero = jnp.zeros((geo.m, LANES), F32)
        lax.fori_loop(0, geo.rows, advance, (zero, zero), unroll=4 if geo.rows % 4 == 0 else 1)

    def scan(self):
        geo = self.geo
        steps = geo.row_step()

        @pl.when(self.row == self.end_scan)
        def _():
            got = self.brecv.at[0, 0 : geo.rows - 1]
            self.whole(got, got, self.d_s, self.b_r).wait_recv()
            lane = lax.broadcasted_iota(jnp.int32, (geo.m, LANES), 1)
            keep = jnp.where(lane < 2, steps[0][0], steps[1][0]).astype(F32)
            mix = jnp.where(lane < 2, steps[0][1], steps[1][1]).astype(F32)
            self.run_scan(0, keep, mix)
            for k in self.peers.rows_order + [0]:
                self.give_copy(self.peers.row_at[k]).start()

        @pl.when(self.scans)
        def _():
            got = self.brecv.at[:, 0 : geo.rows - 1]
            self.whole(got, got, self.b_s, self.b_r).wait_recv()
            for p in range(geo.per):
                first = p * geo.half + self.spot < geo.blocks
                keep = jnp.where(first, steps[0][0], steps[1][0]).astype(F32)
                mix = jnp.where(first, steps[0][1], steps[1][1]).astype(F32)
                self.run_scan(p, keep, mix)
                for k in self.peers.rows_order:
                    self.c_copy(p, self.spot, self.peers.row_at[k]).start()
                self.crecv[p * geo.half + self.spot] = self.csend[p, self.row]

    def main_rows(self):
        geo = self.geo
        for level in range(geo.levels):
            sums = [jnp.zeros((geo.lines, LANES), F32) for s in range(2)]
            for wide in range(geo.wide):
                value = dot3(
                    self.ph[level, : geo.lines, :], self.plo[level, : geo.lines, :],
                    joined(self.dh, level, 2 * wide, 2 * wide + 2), joined(self.dl, level, 2 * wide, 2 * wide + 2),
                )
                for k in range(BLOCK // LANES):
                    at = wide * BLOCK + k * LANES
                    piece = value[:, k * LANES : (k + 1) * LANES]
                    h, w = split(piece)
                    self.dh[level, 2 * wide + k] = h
                    self.dl[level, 2 * wide + k] = w
                    sums = [sums[s] + piece * self.cols[level, s : s + 1, at : at + LANES] for s in range(2)]
            for s in range(2):
                total = jnp.sum(sums[s], axis=1, keepdims=True)
                self.esend[level, s] = jnp.broadcast_to(total, (geo.lines, LANES))

    def e_start(self):
        step = self.geo.lines // 4
        for level in range(self.geo.levels):
            for s in range(2):
                for first in range(0, self.geo.lines, step):
                    cut = slice(first, first + step)
                    remote(
                        self.esend.at[level, s, cut], self.erecv.at[level, s, cut], self.e_s, self.e_r, {"col": self.other}
                    ).start()

    def e_copy(self):
        return remote(self.esend, self.erecv, self.e_s, self.e_r, {"col": self.other})

    def main_cols(self, chosen):
        geo = self.geo
        tx = geo.tx
        for level in chosen:
            for wide in range(geo.wide):
                if self.reverse:
                    cut, strip = (2 * wide, geo.blocks), slice(0, tx - BLOCK * wide)
                else:
                    cut, strip = (0, 2 * wide + 2), slice(tx - BLOCK * (wide + 1), tx)
                self.field[level, :, wide * BLOCK : (wide + 1) * BLOCK] = dot3(
                    joined(self.dh, level, *cut), joined(self.dl, level, *cut),
                    joined(self.sh, level, 0, 2, strip), joined(self.sl, level, 0, 2, strip),
                )

    def inner(self, level, i, at):
        cut = slice(i * self.geo.ty, (i + 1) * self.geo.ty)
        q = self.cols[level, 2:3, at] * self.enters
        w = self.cols[level, 3:4, at] * self.enters
        return self.field[level, cut, at] + self.erecv[level, 0, cut] * q + self.erecv[level, 1, cut] * w

    def take(self):
        geo = self.geo

        def wait(count):
            some, part = self.crecv.at[0:count], self.bsend.at[0:count]
            self.whole(part, some, self.b_s, self.c_r).wait_recv()
            self.whole(part, some, self.b_s, self.c_r).wait_send()

        pl.when(self.scans)(lambda: wait(geo.chunks - geo.per))
        pl.when(lax.rem(self.row, 2) != self.col)(lambda: wait(geo.chunks))
        self.give_copy(self.row).wait_recv()
        ends = [self.crecv[self.ends, s] * self.enters for s in range(2)]
        return [
            [[jnp.broadcast_to(ends[s][:, 2 * level + e : 2 * level + e + 1], (geo.m, LANES)) for e in range(2)] for s in range(2)]
            for level in range(geo.levels)
        ]

    def entering(self, ends, level, k):
        at = slice(k * LANES, (k + 1) * LANES)
        q, w = self.cols[level, 2:3, at], self.cols[level, 3:4, at]
        return [
            self.crecv[level * self.geo.blocks + k, s] + ends[level][s][0] * q + ends[level][s][1] * w for s in range(2)
        ]

    def sent(self):
        geo = self.geo
        pl.when(self.row != self.end_scan)(lambda: self.end_copy(self.row).wait_send())

        @pl.when(self.row == self.end_scan)
        def _():
            sent = self.csend.at[0]
            self.whole(sent, sent, self.c_s, self.d_r).wait_send()

        @pl.when(self.scans)
        def _():
            sent = self.csend.at[:, 0 : geo.rows - 1]
            self.whole(sent, sent, self.c_s, self.c_r).wait_send()


def stencil_rows(data, ty):
    y0, fy, fz = data[0:1], data[2:3], data[4:5]
    place = lax.broadcasted_iota(jnp.int32, (ty, CAP), 0).astype(F32)
    weight = jnp.where(place == y0, 1.0 - fy, jnp.where(place == y0 + 1.0, fy, 0.0))
    return jnp.concatenate([weight * (1.0 - fz), weight * fz], axis=0)


def kernel(geo, *refs):
    sources, (out, out_dep) = refs[:12], refs[12:14]
    refs = refs[14:]
    held, in_sem = refs[:12], refs[12]
    control, members, mats, tabs, rowts, corner, count, off_y, off_x, off_z, innov, prec = held
    refs = refs[10:]
    work, comms = refs[3:8], (refs[8:25], refs[25:42])
    (payload, arrived, back, returned, obs_s, obs_r, dep_s, dep_r, own, got, total, got2, own_s, own_r, tot_s, tot_r,
     select, parts, mixed, even, odd, spread) = refs[42:]
    m, levels, ty, tx, rows = geo.m, geo.levels, geo.ty, geo.tx, geo.rows
    cells = levels * ty
    wides, per_wide = geo.wide, BLOCK // LANES
    row, col, mem = lax.axis_index("row"), lax.axis_index("col"), lax.axis_index("mem")
    tiles = rows * 2
    me = row * 2 + col
    partner = {"mem": 1 - mem}
    dh, dl, bcat, bout, field = work
    peers = Peers(geo, row, col)

    loads = [pltpu.make_async_copy(a, b, in_sem.at[i]) for i, (a, b) in enumerate(zip(sources, held))]
    for load in loads:
        load.start()

    barrier = pltpu.get_barrier_semaphore()
    for k in peers.order:
        pl.semaphore_signal(barrier, inc=1, device_id=peers.device(k), device_id_type=MESH)
    pl.semaphore_signal(barrier, inc=1, device_id=partner, device_id_type=MESH)

    place = (row, col)
    ahead = Filter(geo, False, (mats.at[0], mats.at[1], tabs.at[0], rowts.at[0]), comms[0], work, place, peers)
    behind = Filter(geo, True, (mats.at[2], mats.at[3], tabs.at[1], rowts.at[1]), comms[1], work, place, peers)
    rowt0, rowt1 = rowts.at[0], rowts.at[1]

    make_strips(geo, False, ahead.sh, ahead.sl)
    for load in loads:
        load.wait()
    for level in range(levels):
        for i in range(m):
            cut = slice(i * ty, (i + 1) * ty)
            for k in range(geo.blocks):
                h, w = split(control[i, level, :, k * LANES : (k + 1) * LANES])
                dh[level, k, cut, :] = h
                dl[level, k, cut, :] = w
    totals = ahead.edge_start()
    for wide in range(wides):
        ahead.edge(wide, totals)
    ahead.edge_along_x(totals)

    pl.semaphore_wait(barrier, tiles)
    ahead.gather_start()

    corners = corner[...]
    row_in = lax.shift_right_logical(corners, int(tx).bit_length() - 1)
    payload[:, 0, :] = row_in.astype(F32)
    payload[:, 1, :] = (corners - row_in * tx).astype(F32)
    payload[:, 2, :] = off_y[...]
    payload[:, 3, :] = off_x[...]
    payload[:, 4, :] = off_z[...]
    payload[:, 5, :] = innov[...]
    down = lax.broadcasted_iota(jnp.int32, (tiles, tiles), 0)
    across = lax.broadcasted_iota(jnp.int32, (tiles, tiles), 1)
    used = jnp.sum(jnp.where(down == across, count[...].astype(F32), 0.0), axis=1, keepdims=True)
    slot = lax.broadcasted_iota(jnp.int32, (tiles, CAP), 1).astype(F32)
    payload[:, 6, :] = jnp.where(slot < used, prec[...], 0.0)
    payload[:, 7, :] = jnp.zeros((tiles, CAP), F32)

    def obs_copy(k, to, slot):
        return remote(payload.at[to], arrived.at[slot], obs_s, obs_r, peers.device(k))

    def dep_copy(k, to, slot):
        return remote(back.at[to], returned.at[slot], dep_s, dep_r, peers.device(k))

    for k in peers.order:
        obs_copy(k, peers.index(k), me).start()
    arrived[me] = payload[me]

    ahead.main_rows()
    ahead.e_start()
    ahead.main_cols(range(0, levels - 1))
    ahead.scan()
    ahead.main_cols(range(levels - 1, levels))

    make_strips(geo, True, behind.sh, behind.sl)
    ahead.e_copy().wait()
    for wide in range(wides):
        for k in range(per_wide):
            at = slice(wide * BLOCK + k * LANES, wide * BLOCK + (k + 1) * LANES)
            for level in range(levels):
                value = members[0, level, :, at].astype(F32) * ahead.inner(level, 0, at)
                for i in range(1, m):
                    value = value + members[i, level, :, at].astype(F32) * ahead.inner(level, i, at)
                own[wide, level * ty : (level + 1) * ty, k * LANES : (k + 1) * LANES] = value

    others = pl.ds(0, tiles - 1)
    every = remote(payload.at[others], arrived.at[others], obs_s, obs_r, partner)
    every.wait_send()
    every.wait_recv()

    iota = lax.broadcasted_iota(jnp.int32, (LANES, CAP), 0).astype(F32)
    packed = 16

    def choose(s):
        x0 = arrived[s, 1:2, :]
        block = jnp.floor(x0 * (1.0 / LANES))
        inside = jnp.where(iota == x0 - block * LANES, 1.0, 0.0).astype(BF16)
        block = jnp.broadcast_to(block, (packed, CAP))
        for h in range(tx // LANES):
            there = jnp.where(block == float(h), 1.0, 0.0).astype(BF16)
            for g in range(0, LANES, packed):
                first = h * LANES + g
                select[s, first : first + packed, :] = inside[g : g + packed] * there

    early = tiles // 4
    each(0, early, choose, 2 if early % 2 == 0 else 1)

    ends = ahead.take()

    def own_copy(wide):
        return remote(own.at[wide], got.at[wide], own_s.at[wide], own_r.at[wide], partner)

    for wide in reversed(range(wides)):
        for k in range(per_wide):
            block = wide * per_wide + k
            at = slice(block * LANES, (block + 1) * LANES)
            here = slice(k * LANES, (k + 1) * LANES)
            for level in range(levels):
                s1, s2 = ahead.entering(ends, level, block)
                value = own[wide, level * ty : (level + 1) * ty, here]
                for i in range(m):
                    value = value + members[i, level, :, at].astype(F32) * (
                        rowt0[level, 0] * s1[i : i + 1, :] + rowt0[level, 1] * s2[i : i + 1, :]
                    )
                own[wide, level * ty : (level + 1) * ty, here] = value * scale_of(geo)
        for first in range(0, cells, 8):
            cut = slice(first, first + 8)
            remote(own.at[wide, cut], got.at[wide, cut], own_s.at[wide], own_r.at[wide], partner).start()
    each(early, tiles, choose, 2 if early % 2 == 0 else 1)

    size = 4 if tiles >= 8 else 2
    groups = tiles // size
    middle = tx // 2

    def chosen(group, rows_of):
        return jnp.concatenate([select[group * size + i, rows_of, :] for i in range(size)], axis=1)

    def share(group):
        mixed[group] = dot(parts[:, middle:], chosen(group, slice(middle, tx)))

    lane = lax.broadcasted_iota(jnp.int32, (cells, BLOCK), 1)
    first_of_right = jnp.zeros((cells, 1), F32)
    for wide in reversed(range(wides)):
        own_copy(wide).wait_recv()
        value = own[wide] + got[wide]
        moved = jnp.where(lane == BLOCK - 1, first_of_right, pltpu.roll(value, BLOCK - 1, 1))
        first_of_right = value[:, 0:1]
        h, w = split(value)
        parts[0:cells, wide * BLOCK : (wide + 1) * BLOCK] = h
        parts[cells : 2 * cells, wide * BLOCK : (wide + 1) * BLOCK] = w
        h, w = split(moved)
        parts[2 * cells : 3 * cells, wide * BLOCK : (wide + 1) * BLOCK] = h
        parts[3 * cells :, wide * BLOCK : (wide + 1) * BLOCK] = w
        if wide * BLOCK == middle:
            each(0, groups, share, 2)

    def fetch(group, buffer):
        buffer[...] = mixed[group] + dot(parts[:, :middle], chosen(group, slice(0, middle)))

    def use(group, buffer):
        for i in range(size):
            s = group * size + i
            data = arrived[s]
            cut = slice(i * CAP, (i + 1) * CAP)
            fx = data[3:4]
            left = buffer[0:cells, cut] + buffer[cells : 2 * cells, cut]
            right = buffer[2 * cells : 3 * cells, cut] + buffer[3 * cells :, cut]
            weight = stencil_rows(data, ty)
            image = jnp.sum(weight * (left + fx * (right - left)), axis=0, keepdims=True)
            departure = data[6:7] * (image - data[5:6])
            back[s] = departure
            weight = weight * (departure * scale_of(geo))
            far = weight * fx
            h, w = split(weight - far)
            spread[s, 0:cells] = h
            spread[s, cells : 2 * cells] = w
            h, w = split(far)
            spread[s, 2 * cells : 3 * cells] = h
            spread[s, 3 * cells :] = w

    fetch(0, even)

    def interpolate(t):
        fetch(2 * t + 1, odd)
        use(2 * t, even)
        fetch(jnp.minimum(2 * t + 2, groups - 1), even)
        use(2 * t + 1, odd)

    each(0, groups // 2, interpolate)

    def tot_copy(wide):
        return remote(total.at[wide], got2.at[wide], tot_s.at[wide], tot_r.at[wide], partner)

    lane = lax.broadcasted_iota(jnp.int32, (cells, LANES), 1)
    last = jnp.zeros((cells, LANES), F32)
    for wide in range(wides):
        piece = lax.dot_general(
            jnp.concatenate([select[s, wide * BLOCK : (wide + 1) * BLOCK, :] for s in range(tiles)], axis=1),
            jnp.concatenate([spread[s] for s in range(tiles)], axis=1),
            (((1,), (1,)), ((), ())),
            preferred_element_type=F32,
        )
        piece = piece.T
        for k in range(per_wide):
            cut = slice(k * LANES, (k + 1) * LANES)
            here = piece[0:cells, cut] + piece[cells : 2 * cells, cut]
            moved = pltpu.roll(piece[2 * cells : 3 * cells, cut] + piece[3 * cells :, cut], 1, 1)
            total[wide, :, cut] = here + jnp.where(lane == 0, last, moved)
            last = moved
        for first in range(0, cells, 8):
            cut = slice(first, first + 8)
            remote(total.at[wide, cut], got2.at[wide, cut], tot_s.at[wide], tot_r.at[wide], partner).start()

    totals = behind.edge_start()
    for wide in range(wides):
        tot_copy(wide).wait_recv()
        for level in range(levels):
            part = slice(level * ty, (level + 1) * ty)
            for k in range(per_wide):
                block = wide * per_wide + k
                here = slice(k * LANES, (k + 1) * LANES)
                forcing = total[wide, part, here] + got2[wide, part, here]
                for i in range(m):
                    h, w = split(members[i, level, :, block * LANES : (block + 1) * LANES].astype(F32) * forcing)
                    dh[level, block, i * ty : (i + 1) * ty, :] = h
                    dl[level, block, i * ty : (i + 1) * ty, :] = w
        behind.edge(wide, totals)
    behind.edge_along_x(totals)
    behind.gather_start()
    for k in peers.order:
        dep_copy(k, peers.index(k), me).start()
    returned[me] = back[me]
    behind.main_rows()
    behind.e_start()
    behind.main_cols(range(0, levels - 1))
    behind.scan()
    behind.main_cols(range(levels - 1, levels))
    behind.e_copy().wait()
    for level in range(levels):
        def finish(k, level=level):
            at = lanes(k * LANES)
            for i in range(m):
                out[i, level, :, at] = control[i, level, :, at] + behind.inner(level, i, at)

        each(0, geo.blocks, finish)

    every = remote(back.at[others], returned.at[others], dep_s, dep_r, partner)
    every.wait_send()
    every.wait_recv()
    for t in range(tiles):
        out_dep[0:1, t * CAP : (t + 1) * CAP] = returned[t, 0:1, :]
    ahead.sent()
    for wide in range(wides):
        own_copy(wide).wait_send()
        tot_copy(wide).wait_send()
    ends = behind.take()
    for k in range(geo.blocks):
        at = slice(k * LANES, (k + 1) * LANES)
        for level in range(levels):
            s1, s2 = behind.entering(ends, level, k)
            for i in range(m):
                out[i, level, :, at] += rowt1[level, 0] * s1[i : i + 1, :] + rowt1[level, 1] * s2[i : i + 1, :]
    behind.sent()


def body(control, members, obs_corner, obs_count, offset_y, offset_x, offset_z, innovation, precision):
    m, levels, ty, tx = control.shape
    rows = lax.axis_size("row")
    tiles = rows * lax.axis_size("col")
    geo = Geometry(m, levels, ty, tx, rows)
    cells = levels * ty
    size = 4 if tiles >= 8 else 2

    def by_tile(array):
        return array.reshape(tiles, CAP)

    mats = np.stack([a for reverse in (False, True) for a in geo.row_matrix(reverse)])
    tabs = np.stack([geo.col_tables(reverse) for reverse in (False, True)])
    rowts = np.stack([geo.row_tables(reverse) for reverse in (False, True)])
    operands = [control, members, jnp.asarray(mats), jnp.asarray(tabs), jnp.asarray(rowts), by_tile(obs_corner), obs_count]
    operands += [by_tile(a) for a in (offset_y, offset_x, offset_z, innovation, precision)]
    dma = pltpu.SemaphoreType.DMA
    chunks, per, lines = geo.chunks, geo.per, geo.lines
    comm = [
        pltpu.VMEM((levels, 2, lines, LANES), F32),
        pltpu.VMEM((levels, 2, lines, LANES), F32),
        pltpu.VMEM((chunks + 1, 2, m, LANES), F32),
        pltpu.VMEM((per, rows, 2, m, LANES), F32),
        pltpu.VMEM((per, rows, 2, m, LANES), F32),
        pltpu.VMEM((chunks + 1, 2, m, LANES), F32),
        pltpu.VMEM((8, LANES), F32),
        pltpu.VMEM((levels, BLOCK // LANES, tx, LANES), BF16),
        pltpu.VMEM((levels, BLOCK // LANES, tx, LANES), BF16),
        dma,
        dma,
        dma,
        dma,
        dma,
        dma,
        dma,
        dma,
    ]
    scratch = [
        *[pltpu.VMEM(a.shape, a.dtype) for a in operands],
        dma((len(operands),)),
        pltpu.VMEM((levels, geo.blocks, lines, LANES), BF16),
        pltpu.VMEM((levels, geo.blocks, lines, LANES), BF16),
        pltpu.VMEM((levels, geo.wide * 4 * m, BLOCK), BF16),
        pltpu.VMEM((8, LANES), F32),
        pltpu.VMEM((levels, lines, tx), F32),
    ]
    scratch += comm + comm
    wide_shape = (geo.wide, cells, BLOCK)
    scratch += [
        pltpu.VMEM((tiles, 8, CAP), F32),
        pltpu.VMEM((tiles, 8, CAP), F32),
        pltpu.VMEM((tiles, 1, CAP), F32),
        pltpu.VMEM((tiles, 1, CAP), F32),
        dma,
        dma,
        dma,
        dma,
        pltpu.VMEM(wide_shape, F32),
        pltpu.VMEM(wide_shape, F32),
        pltpu.VMEM(wide_shape, F32),
        pltpu.VMEM(wide_shape, F32),
        dma((geo.wide,)),
        dma((geo.wide,)),
        dma((geo.wide,)),
        dma((geo.wide,)),
        pltpu.VMEM((tiles, tx, CAP), BF16),
        pltpu.VMEM((4 * cells, tx), BF16),
        pltpu.VMEM((tiles // size, 4 * cells, size * CAP), F32),
        pltpu.VMEM((4 * cells, size * CAP), F32),
        pltpu.VMEM((4 * cells, size * CAP), F32),
        pltpu.VMEM((tiles, 4 * cells, CAP), BF16),
    ]
    hbm = pl.BlockSpec(memory_space=pl.ANY)
    return pl.pallas_call(
        functools.partial(kernel, geo),
        out_shape=(pltpu.VMEM(control.shape, F32), pltpu.VMEM((1, tiles * CAP), F32)),
        in_specs=[hbm] * len(operands),
        out_specs=(VMEM, VMEM),
        scratch_shapes=scratch,
        compiler_params=pltpu.CompilerParams(collective_id=0, has_side_effects=True, vmem_limit_bytes=58 * 1024 * 1024),
        name="gradient",
    )(*operands)


def solution(mesh):
    return jax.shard_map(
        body,
        mesh=mesh,
        in_specs=(
            P("mem", None, "row", "col"),
            P("mem", None, "row", "col"),
            P(("mem", "row", "col"), None),
            P(("mem", "row", "col"), None),
            P(("mem", "row", "col"), None),
            P(("mem", "row", "col"), None),
            P(("mem", "row", "col"), None),
            P(("mem", "row", "col"), None),
            P(("mem", "row", "col"), None),
        ),
        out_specs=(P("mem", None, "row", "col"), P(("mem", "row", "col"), None)),
        check_vma=False,
    )
```
